128 devices in a mesh: wide: 16 (over x, z_lo, core), narrow: 8 (over z_hi, y).
Axes of the slice: x: 4, y: 4, z: 4 (z_hi: 2, z_lo: 2; z = z_hi * 2 + z_lo), core: 2. Of those that a mesh axis runs over, the one named last changes fastest.
Arguments:
- saturation: float32 [256, 128, 1024], P('wide', None, 'narrow'), may hold values from 0.05 to 0.95
- pressure: float32 [256, 128, 1024], P('wide', None, 'narrow'), may hold values from -6 to 6
- rock_class: int32 [256, 128, 1024], P('wide', None, 'narrow'), may hold values from 0 to 15
- rock_table: float32 [3, 16], replicated, may hold values from 0.2 to 5
- well_columns: int32 [64], replicated, may hold values from 0 to 131071
- well_rates: float32 [64], replicated, may hold values from 2 to 8
- residual: float32 [256, 128, 1024], P(None, 'wide', 'narrow'), may hold values from -7 to 7
Outputs:
- sat_new: float32 [256, 128, 1024], P('wide', None, 'narrow')
- precond: float32 [256, 128, 1024], P(None, 'wide', 'narrow')
The draws below stay inside these ranges and needn't reach their ends.
Inputs may be any that keep to these rules, and one draw needn't show every extreme that they name: `well_columns`: a well with column c injects into every depth layer at row c // 1024, column c % 1024; columns may repeat.
All inputs are finite; a program needn't handle non-finite values.
Results may differ from the reference program's by a relative error of at most 0.0003.
Values sent between devices are 32-bit elements; how exact they have to be, the bound alone decides.
No kernel may reach another device: no remote copies, remote signals or barrier semaphores. Data moves between devices by JAX's collectives and lax.ppermute only.
A program may use at most 64 MiB of HBM per device.

```python
import math
import jax
import jax.numpy as jnp
from jax import lax

YB = 8
XD = 128
ROCKS = 16
WELLS = 64
SWEEPS = 6
NZ = 256
NY = 128
NX = 1024
N_WIDE = 16
N_NARROW = 8


def draw_residual(key, part):
    rough_key, wave_key, phase_key = jax.random.split(jax.random.fold_in(key, 17), 3)
    rough = jnp.clip(jax.random.normal(rough_key, (NZ, NY, NX), jnp.float32), -6.0, 6.0)
    waves = jax.random.randint(wave_key, (3, 3), 0, 3).astype(jnp.float32)
    phases = jax.random.uniform(phase_key, (3,), jnp.float32, 0.0, 2.0 * math.pi)
    depth = (jnp.arange(NZ, dtype=jnp.float32) / NZ)[:, None, None]
    across = (jnp.arange(NY, dtype=jnp.float32) / NY)[None, :, None]
    along = (jnp.arange(NX, dtype=jnp.float32) / NX)[None, None, :]
    smooth = jnp.zeros((NZ, NY, NX), jnp.float32)
    for number in range(3):
        angle_sum = 2.0 * math.pi * (waves[number, 0] * depth + waves[number, 1] * across + waves[number, 2] * along)
        smooth = smooth + 0.1 * jnp.cos(angle_sum + phases[number])
    return rough + smooth


def touch_ends(array, rng, low, top_value):
    place = [jax.random.randint(jax.random.fold_in(rng, axis), (), 0, length) for axis, length in enumerate(array.shape)]
    longest = array.shape.index(max(array.shape))
    beside = place[:longest] + [(place[longest] + 1) % array.shape[longest]] + place[longest + 1:]
    return array.at[tuple(place)].set(low).at[tuple(beside)].set(top_value)


def block_scale(rng, dims, cuts, least, largest):
    level = 1.0
    for dim, blocks in cuts:
        heights = jax.random.uniform(jax.random.fold_in(jax.random.fold_in(rng, 6), dim), (blocks,), jnp.float32, least / len(cuts), largest / len(cuts))
        level = level * jnp.repeat(jnp.exp(heights), dims[dim] // blocks).reshape((-1,) + (1,) * (len(dims) - 1 - dim))
    return level


def centred(key, extent, scale, bound, cuts=(), kind=jnp.bfloat16):
    factor_of = block_scale(key, extent, cuts, -0.22, 0.18) if cuts else 1.0
    array = jax.random.normal(key, extent, jnp.float32) * scale * factor_of
    return jnp.minimum(jnp.maximum(array, -bound), bound).astype(kind)


def setup_inputs(seed: int = 0) -> dict:
    streams_of = jax.random.split(jax.random.key(seed), 8)
    return {
        "saturation": jnp.clip(0.05 + 0.9 * jax.random.uniform(streams_of[0], (NZ, NY, NX), jnp.float32) ** block_scale(streams_of[0], (NZ, NY, NX), ((0, 16), (2, 8)), -0.2, 0.2), 0.05, 0.95),
        "pressure": centred(streams_of[1], (NZ, NY, NX), 1.0, 6.0, ((0, 16), (2, 8)), jnp.float32),
        "rock_class": touch_ends(jax.random.randint(streams_of[2], (NZ, NY, NX), 0, ROCKS), jax.random.fold_in(streams_of[2], 1), 0, ROCKS - 1).astype(jnp.int32),
        "rock_table": jnp.clip(jnp.exp(jax.random.uniform(streams_of[3], (3, ROCKS), jnp.float32, math.log(0.2), math.log(5.0))), 0.2, 5.0),
        "well_columns": touch_ends(jax.random.randint(streams_of[4], (WELLS,), 0, NY * NX), jax.random.fold_in(streams_of[4], 1), 0, (NY * NX) - 1).astype(jnp.int32),
        "well_rates": jnp.clip(jax.random.uniform(streams_of[5], (WELLS,), jnp.float32, 2.0, 8.0), 2.0, 8.0),
        "residual": draw_residual(jax.random.fold_in(streams_of[7], 71), 0),
    }


compress = 0.05
relax = 0.8
gravity = 0.5
courant = 0.5
tiny = 1e-06

def harmonic(lower_side, upper_side):
    return 2.0 * lower_side * upper_side / (lower_side + upper_side)

def pad_along(array_in, direction):
    widths = [(0, 0)] * array_in.ndim
    widths[direction] = (1, 1)
    return jnp.pad(array_in, widths)

def shifted(array_in, direction):
    padded = pad_along(array_in, direction)
    length = padded.shape[direction]
    return (lax.slice_in_dim(padded, 0, length - 1, axis=direction), lax.slice_in_dim(padded, 1, length, axis=direction))

def flows_between(lower_side, upper_side, lift):
    transmit = harmonic(lower_side[1], upper_side[1])
    total_flow = transmit * (lower_side[0] - upper_side[0] + lift)
    water_flow = total_flow * jnp.where(total_flow > 0, lower_side[2], upper_side[2])
    return (total_flow, water_flow)

def local_apply(values, diag_local, depth_inner, row_inner, col_inner):
    depth_pad = pad_along(values, 0)
    row_pad = pad_along(values, 1)
    col_pad = pad_along(values, 2)
    return diag_local * values - (depth_inner[:-1] * depth_pad[:-2] + depth_inner[1:] * depth_pad[2:] + row_inner[:, :-1] * row_pad[:, :-2] + row_inner[:, 1:] * row_pad[:, 2:] + col_inner[:, :, :-1] * col_pad[:, :, :-2] + col_inner[:, :, 1:] * col_pad[:, :, 2:])

def coarse_solve(rows, column_count):
    rhs_total = rows[:, 0]
    diagonal = rows[:, 1]
    low_rows = rows[:, 2]
    high_rows = rows[:, 3]
    low_cols = rows[:, 4]
    high_cols = rows[:, 5]
    matrix = jnp.diag(diagonal) - jnp.diag(low_rows[column_count:], -column_count) - jnp.diag(high_rows[:-column_count], column_count) - jnp.diag(low_cols[1:], -1) - jnp.diag(high_cols[:-1], 1)
    factor = jnp.linalg.cholesky(matrix)
    return jax.scipy.linalg.cho_solve((factor, True), rhs_total)

def transport(saturation, pressure, rock_class, rock_table, well_columns, well_rates):
    perm_cell = rock_table[0][rock_class]
    water_gain = rock_table[1][rock_class]
    oil_gain = rock_table[2][rock_class]
    water_mob = water_gain * saturation * saturation
    oil_mob = oil_gain * (1.0 - saturation) * (1.0 - saturation)
    water_frac = water_mob / (water_mob + oil_mob)
    net_parts = []
    out_parts = []
    for direction in range(3):
        lift = gravity if direction == 0 else 0.0
        press_low, press_high = shifted(pressure, direction)
        perm_low, perm_high = shifted(perm_cell, direction)
        frac_low, frac_high = shifted(water_frac, direction)
        total_flow, water_flow = flows_between((press_low, perm_low, frac_low), (press_high, perm_high, frac_high), lift)
        length = total_flow.shape[direction]
        upper_water = lax.slice_in_dim(water_flow, 1, length, axis=direction)
        lower_water = lax.slice_in_dim(water_flow, 0, length - 1, axis=direction)
        upper_total = lax.slice_in_dim(total_flow, 1, length, axis=direction)
        lower_total = lax.slice_in_dim(total_flow, 0, length - 1, axis=direction)
        net_parts.append(upper_water - lower_water)
        out_parts.append(jnp.maximum(upper_total, 0.0) + jnp.maximum(-lower_total, 0.0))
    net_water = net_parts[0] + net_parts[1] + net_parts[2]
    outflow = out_parts[0] + out_parts[1] + out_parts[2]
    step_size = courant / (jnp.max(outflow) + tiny)
    source = jnp.zeros((NY * NX,), jnp.float32).at[well_columns].add(well_rates).reshape(NY, NX)
    sat_new = saturation - step_size * net_water + step_size * source[None]
    coefficient = perm_cell * (water_gain * sat_new * sat_new + oil_gain * (1.0 - sat_new) * (1.0 - sat_new))
    return (sat_new, coefficient)

def brick_total(array_in):
    return jnp.sum(array_in.reshape(NZ, N_WIDE, YB, N_NARROW, XD), axis=(0, 2, 4)).reshape(-1)

def precondition(coefficient, residual):
    depth_faces = harmonic(coefficient[:-1], coefficient[1:])
    row_faces = harmonic(coefficient[:, :-1], coefficient[:, 1:])
    col_faces = harmonic(coefficient[:, :, :-1], coefficient[:, :, 1:])
    row_face_index = lax.broadcasted_iota(jnp.int32, row_faces.shape, 1)
    col_face_index = lax.broadcasted_iota(jnp.int32, col_faces.shape, 2)
    depth_inner = pad_along(depth_faces, 0)
    row_inner = pad_along(jnp.where((row_face_index + 1) % YB == 0, 0.0, row_faces), 1)
    col_inner = pad_along(jnp.where((col_face_index + 1) % XD == 0, 0.0, col_faces), 2)
    diag_local = compress * coefficient + depth_inner[:-1] + depth_inner[1:] + row_inner[:, :-1] + row_inner[:, 1:] + col_inner[:, :, :-1] + col_inner[:, :, 1:]
    values = relax * residual / diag_local
    for number in range(SWEEPS - 1):
        values = values + relax * (residual - local_apply(values, diag_local, depth_inner, row_inner, col_inner)) / diag_local
    rows_index = lax.broadcasted_iota(jnp.int32, values.shape, 1)
    cols_index = lax.broadcasted_iota(jnp.int32, values.shape, 2)
    value_rows = pad_along(values, 1)
    coeff_rows = pad_along(coefficient, 1)
    value_cols = pad_along(values, 2)
    coeff_cols = pad_along(coefficient, 2)
    first_row = rows_index % YB == 0
    last_row = (rows_index + 1) % YB == 0
    first_col = cols_index % XD == 0
    last_col = (cols_index + 1) % XD == 0
    weighted = coefficient * values
    weights = coefficient
    weighted = weighted + jnp.where(first_row, coeff_rows[:, :-2] * value_rows[:, :-2], 0.0)
    weights = weights + jnp.where(first_row, coeff_rows[:, :-2], 0.0)
    weighted = weighted + jnp.where(last_row, coeff_rows[:, 2:] * value_rows[:, 2:], 0.0)
    weights = weights + jnp.where(last_row, coeff_rows[:, 2:], 0.0)
    weighted = weighted + jnp.where(first_col, coeff_cols[:, :, :-2] * value_cols[:, :, :-2], 0.0)
    weights = weights + jnp.where(first_col, coeff_cols[:, :, :-2], 0.0)
    weighted = weighted + jnp.where(last_col, coeff_cols[:, :, 2:] * value_cols[:, :, 2:], 0.0)
    weights = weights + jnp.where(last_col, coeff_cols[:, :, 2:], 0.0)
    averaged = weighted / weights
    cross_rows = jnp.sum(row_faces[:, YB - 1::YB].reshape(NZ, N_WIDE - 1, N_NARROW, XD), axis=(0, 3))
    zero_row = jnp.zeros((1, N_NARROW), jnp.float32)
    high_rows = jnp.concatenate([cross_rows, zero_row], axis=0).reshape(-1)
    low_rows = jnp.concatenate([zero_row, cross_rows], axis=0).reshape(-1)
    cross_cols = jnp.sum(col_faces[:, :, XD - 1::XD].reshape(NZ, N_WIDE, YB, N_NARROW - 1), axis=(0, 2))
    zero_col = jnp.zeros((N_WIDE, 1), jnp.float32)
    high_cols = jnp.concatenate([cross_cols, zero_col], axis=1).reshape(-1)
    low_cols = jnp.concatenate([zero_col, cross_cols], axis=1).reshape(-1)
    diagonal = compress * brick_total(coefficient) + low_rows + high_rows + low_cols + high_cols
    rows = jnp.stack([brick_total(residual), diagonal, low_rows, high_rows, low_cols, high_cols], axis=1)
    solved = coarse_solve(rows, N_NARROW)
    result = averaged.reshape(NZ, N_WIDE, YB, N_NARROW, XD) + solved.reshape(1, N_WIDE, 1, N_NARROW, 1)
    return result.reshape(NZ, NY, NX)

def reference(saturation, pressure, rock_class, rock_table, well_columns, well_rates, residual):
    sat_new, coefficient = transport(saturation, pressure, rock_class, rock_table, well_columns, well_rates)
    precond = precondition(coefficient, residual)
    return (sat_new, precond)
```

```python
import functools

import jax
import jax.numpy as jnp
from jax import lax
from jax.experimental import pallas as pl
from jax.experimental.pallas import tpu as pltpu
from jax.sharding import PartitionSpec as P

SWEEPS = 6
compress = 0.05
relax = 0.8
gravity = 0.5
courant = 0.5
tiny = 1e-06

F32 = jnp.float32
HIGH = lax.Precision.HIGHEST
PARAMS = pltpu.CompilerParams(vmem_limit_bytes=40 * 1024 * 1024)


def harmonic(low, high):
    return 2.0 * low * high / (low + high)


def sub_iota():
    return lax.broadcasted_iota(jnp.int32, (8, 128), 0)


def lane_iota():
    return lax.broadcasted_iota(jnp.int32, (8, 128), 1)


def lane_pick(tile, index):
    return jnp.take_along_axis(tile, jnp.full((8, 128), index, jnp.int32), axis=1)


def spread(tile, lane):
    return jnp.broadcast_to(tile[:, lane : lane + 1], (8, 128))


def call(kernel, outs, scratch=(), aliases=None, out_specs=None, in_specs=None, name=None):
    def run(*args):
        return pl.pallas_call(
            kernel,
            out_shape=[jax.ShapeDtypeStruct(shape, F32) for shape in outs],
            in_specs=in_specs or [pl.BlockSpec(memory_space=pltpu.VMEM)] * len(args),
            out_specs=out_specs or [pl.BlockSpec(memory_space=pltpu.VMEM)] * len(outs),
            scratch_shapes=list(scratch),
            input_output_aliases=aliases or {},
            compiler_params=PARAMS,
            name=name,
        )(*args)

    return run


def prep_kernel(table, sat, press, rock, perm, wgain, ogain, frac, low, high, left, right):
    lane = lane_iota()
    tables = [
        jnp.broadcast_to(
            jnp.concatenate([table[n : n + 1, :], jnp.zeros((1, 112), F32)], axis=1), (8, 128)
        )
        for n in range(3)
    ]
    depth = sat.shape[0]

    def rows(step, carry):
        at = pl.ds(pl.multiple_of(step * 8, 8), 8)
        first = jnp.zeros((8, 128), F32)
        last = jnp.zeros((8, 128), F32)
        for d in range(depth):
            kind = rock[d, at, :]
            k, wg, og = [jnp.take_along_axis(t, kind, axis=1) for t in tables]
            s = sat[d, at, :]
            p = press[d, at, :]
            water = wg * s * s
            oil = og * (1.0 - s) * (1.0 - s)
            f = water / (water + oil)
            perm[d, at, :] = k
            wgain[d, at, :] = wg
            ogain[d, at, :] = og
            frac[d, at, :] = f
            for n, field in enumerate((p, k, f)):
                mark = lane == n * depth + d
                first = jnp.where(mark, spread(field, 0), first)
                last = jnp.where(mark, spread(field, 127), last)
                if d == 0:
                    low[n, at, :] = field
                if d == depth - 1:
                    high[n, at, :] = field
        left[at, :] = first
        right[at, :] = last
        return carry

    lax.fori_loop(0, sat.shape[1] // 8, rows, 0)


def flows(low, high, lift):
    total = harmonic(low[1], high[1]) * (low[0] - high[0] + lift)
    return total, total * jnp.where(total > 0, low[2], high[2])


def flow_kernel(
    place, perm, frac, press, below, above, left, right, from_left, from_right,
    columns, rates, residual, net, source, message, zq, zw, lq, lw, rq, rw,
):
    lane = lane_iota()
    sub = sub_iota()
    depth, rows_all, cols = perm.shape
    tiles = rows_all // 8

    def edge(step, carry):
        at = pl.ds(pl.multiple_of(step * 8, 8), 8)

        def fields(ref):
            tile = ref[at, :]
            return [tile] + [pltpu.roll(tile, 128 - n * depth, 1) for n in (1, 2)]

        q, w = flows(fields(from_left), fields(left), 0.0)
        lq[at, :] = q
        lw[at, :] = w
        q, w = flows(fields(right), fields(from_right), 0.0)
        rq[at, :] = q
        rw[at, :] = w
        q, w = flows(
            [below[n, at, :] for n in range(3)],
            [press[0, at, :], perm[0, at, :], frac[0, at, :]],
            gravity,
        )
        zq[at, :] = q
        zw[at, :] = w
        return carry

    lax.fori_loop(0, tiles, edge, 0)

    def layer(d, top, upper):
        cell = [[ref[d, i * 8 : i * 8 + 8, :] for ref in (press, perm, frac)] for i in range(1)]
        cur = cell[0]
        cur_roll = [pltpu.roll(x, 7, 0) for x in cur]
        last_q = last_w = jnp.zeros((8, 128), F32)
        for i in range(tiles):
            at = slice(i * 8, i * 8 + 8)
            if i + 1 < tiles:
                nxt = [ref[d, i * 8 + 8 : i * 8 + 16, :] for ref in (press, perm, frac)]
                nxt_roll = [pltpu.roll(x, 7, 0) for x in nxt]
            else:
                nxt, nxt_roll = cur, cur_roll
            q, w = flows(cur, upper(at), gravity)
            low_q, low_w = zq[at, :], zw[at, :]
            zq[at, :] = q
            zw[at, :] = w
            net_sum = w - low_w
            out = jnp.maximum(q, 0.0) + jnp.maximum(-low_q, 0.0)
            up = [jnp.where(sub == 7, b, a) for a, b in zip(cur_roll, nxt_roll)]
            q, w = flows(cur, up, 0.0)
            if i + 1 == tiles:
                q = jnp.where(sub == 7, 0.0, q)
                w = jnp.where(sub == 7, 0.0, w)
            q_roll, w_roll = pltpu.roll(q, 1, 0), pltpu.roll(w, 1, 0)
            low_q = jnp.where(sub == 0, last_q, q_roll)
            low_w = jnp.where(sub == 0, last_w, w_roll)
            last_q, last_w = q_roll, w_roll
            net_sum = net_sum + (w - low_w)
            out = out + (jnp.maximum(q, 0.0) + jnp.maximum(-low_q, 0.0))
            q, w = flows(cur, [pltpu.roll(x, 127, 1) for x in cur], 0.0)
            low_q = jnp.where(lane == 0, lane_pick(lq[at, :], d), pltpu.roll(q, 1, 1))
            low_w = jnp.where(lane == 0, lane_pick(lw[at, :], d), pltpu.roll(w, 1, 1))
            q = jnp.where(lane == 127, lane_pick(rq[at, :], d), q)
            w = jnp.where(lane == 127, lane_pick(rw[at, :], d), w)
            net[d, at, :] = net_sum + (w - low_w)
            out = out + (jnp.maximum(q, 0.0) + jnp.maximum(-low_q, 0.0))
            top = jnp.maximum(top, out)
            cur, cur_roll = nxt, nxt_roll
        return top

    top = lax.fori_loop(
        0,
        depth - 1,
        lambda d, top: layer(
            d, top, lambda at: [ref[d + 1, at, :] for ref in (press, perm, frac)]
        ),
        jnp.zeros((8, 128), F32),
    )
    top = layer(depth - 1, top, lambda at: [above[n, at, :] for n in range(3)])

    def add(step, sums):
        at = step * 8
        return tuple(s + residual[at + n] for n, s in enumerate(sums))

    sums = lax.fori_loop(0, residual.shape[0] // 8, add, (jnp.zeros((8, 128), F32),) * 8)
    total = sum(sums[1:], sums[0])
    wide_lane = lax.broadcasted_iota(jnp.int32, (rows_all, 128), 1)
    message[...] = jnp.where(
        wide_lane == 0, jnp.max(top), jnp.where(wide_lane == 1, jnp.sum(total), 0.0)
    )

    wells = columns.shape[0]
    number = columns[...]
    spot = lax.broadcasted_iota(jnp.int32, (wells, 128), 1)
    global_cols = cols * place[1]
    well_row = number // global_cols
    well_col = number % global_cols - place[0] * cols
    in_row = jnp.where(spot == well_row, 1.0, 0.0)
    in_col = jnp.where(spot == well_col, rates[...], 0.0)
    source[...] = lax.dot_general(
        in_row, in_col, (((0,), (0,)), ((), ())), precision=HIGH, preferred_element_type=F32
    )


def update_kernel(
    gathered, sat, net, source, perm, wgain, ogain, new, chunks, first, last, cell_sum, row_sum
):
    lane = lane_iota()
    depth, rows_all, _ = sat.shape
    tiles = rows_all // 8
    stride = (depth + 1) * 8
    spot = lax.broadcasted_iota(jnp.int32, gathered.shape, 1)
    top = jnp.max(jnp.where(spot == 0, gathered[...], 0.0), keepdims=True)
    step_size = jnp.broadcast_to(courant / (top + tiny), (8, 128))

    def rows(step, carry):
        at = pl.ds(pl.multiple_of(step * 8, 8), 8)
        begin = step * stride
        add = step_size * source[at, :]
        total = jnp.zeros((8, 128), F32)
        low = jnp.zeros((8, 128), F32)
        high = jnp.zeros((8, 128), F32)
        for d in range(depth):
            s = sat[d, at, :] - step_size * net[d, at, :] + add
            new[d, at, :] = s
            c = perm[d, at, :] * (
                wgain[d, at, :] * s * s + ogain[d, at, :] * (1.0 - s) * (1.0 - s)
            )
            chunks[pl.ds(pl.multiple_of(begin + d * 8, 8), 8), :] = c
            total = total + c
            low = jnp.where(lane == d, spread(c, 0), low)
            high = jnp.where(lane == d, spread(c, 127), high)
        first[at, :] = low
        last[at, :] = high
        cell_sum[at, :] = total
        return carry

    lax.fori_loop(0, tiles, rows, 0)
    row_sum[0:8, :] = jnp.zeros((8, 128), F32)
    for p in range(1, tiles):
        total = jnp.zeros((8, 128), F32)
        for half in range(depth // 8):
            low = chunks[pl.ds((p - 1) * stride + half * 64 + 7, 8, stride=8), :]
            high = chunks[pl.ds(p * stride + half * 64, 8, stride=8), :]
            total = total + harmonic(low, high)
        row_sum[p * 8 : p * 8 + 8, :] = total


def sums_kernel(depth, chunks_in, first, beside, cell_sum, row_sum, chunks, tile, sem):
    rows_all = first.shape[0]
    tiles = rows_all // 8
    lane = lax.broadcasted_iota(jnp.int32, (rows_all, 128), 1)
    brick = lax.broadcasted_iota(jnp.int32, (rows_all, 128), 0) // 8
    col_face = jnp.where(lane < depth, harmonic(beside[...], first[...]), 0.0)
    total = jnp.zeros((1, 128), F32)
    for n, part in enumerate((cell_sum[...], row_sum[...], col_face)):
        each = jnp.sum(part, axis=1, keepdims=True)
        placed = jnp.where(lane == n * 16 + brick, each, 0.0)
        total = total + jnp.sum(placed, axis=0, keepdims=True)
    tile[...] = jnp.broadcast_to(total, (8, 128))
    copies = []
    for p in range(tiles):
        begin = p * (depth + 1) * 8 + depth * 8
        copies.append(pltpu.make_async_copy(tile, chunks.at[pl.ds(begin, 8), :], sem.at[p]))
        copies[-1].start()
    for copy in copies:
        copy.wait()


def relax_kernel(depth, got, residual, values, row_low, row_high, col_low, col_high, fd, fr, fc, gain):
    lane = lane_iota()
    sub = sub_iota()
    layers = residual.shape[0] // 8
    parts = layers // depth
    zero = jnp.zeros((8, 128), F32)
    fd[0:8, :] = zero

    def build(w, below):
        begin = w * (depth + 1) * 8
        place = w * depth * 8
        after = jnp.minimum(w + 1, parts - 1) * (depth + 1) * 8
        c = got[pl.ds(pl.multiple_of(begin, 8), 8), :]
        for d in range(depth):
            here = pl.ds(pl.multiple_of(place + d * 8, 8), 8)
            if d + 1 < depth:
                c_next = got[pl.ds(pl.multiple_of(begin + d * 8 + 8, 8), 8), :]
                above = harmonic(c, c_next)
            else:
                c_next = got[pl.ds(pl.multiple_of(after, 8), 8), :]
                above = jnp.where(w + 1 < parts, harmonic(c, c_next), 0.0)
            row = jnp.where(sub == 0, 0.0, harmonic(pltpu.roll(c, 1, 0), c))
            col = jnp.where(lane == 0, 0.0, harmonic(pltpu.roll(c, 1, 1), c))
            diag = (
                compress * c + below + above
                + row + pltpu.roll(row, 7, 0) + col + pltpu.roll(col, 127, 1)
            )
            scale = relax / diag
            fd[pl.ds(pl.multiple_of(place + d * 8 + 8, 8), 8), :] = above
            fr[here, :] = row
            fc[here, :] = col
            gain[here, :] = scale
            values[here, :] = scale * residual[here, :]
            c, below = c_next, above
        return below

    lax.fori_loop(0, parts, build, zero)

    def sweep(number, carry):
        def some(step, prev):
            v = values[pl.ds(pl.multiple_of(step * 64, 8), 8), :]
            for n in range(8):
                here = pl.ds(pl.multiple_of(step * 64 + n * 8, 8), 8)
                after = pl.ds(pl.multiple_of(step * 64 + n * 8 + 8, 8), 8)
                if n < 7:
                    v_next = values[after, :]
                else:
                    v_next = values[pl.ds(pl.multiple_of(jnp.minimum(step * 64 + 64, layers * 8 - 8), 8), 8), :]
                above = fd[after, :] * v_next
                row = fr[here, :]
                col = fc[here, :]
                total = residual[here, :] + fd[here, :] * prev + above
                total = total + (row * pltpu.roll(v, 1, 0) + pltpu.roll(row * v, 7, 0))
                total = total + (col * pltpu.roll(v, 1, 1) + pltpu.roll(col * v, 127, 1))
                values[here, :] = (1.0 - relax) * v + gain[here, :] * total
                prev, v = v, v_next
            return prev

        return lax.fori_loop(0, layers // 8, some, zero)

    lax.fori_loop(0, SWEEPS - 1, sweep, zero)

    for w in range(parts):
        for half in range(depth // 8):
            at = w * (depth + 1) * 8 + half * 64
            place = w * depth + half * 8
            for row, out in ((0, row_low), (7, row_high)):
                c = got[pl.ds(at + row, 8, stride=8), :]
                v = values[pl.ds(place * 8 + row, 8, stride=8), :]
                out[place : place + 8, :] = c * v
                out[layers + place : layers + place + 8, :] = c

    per_half = 128 // depth
    for half in range(layers // 128):
        def pack(w, carry):
            carry = list(carry)
            for d in range(depth):
                c = got[pl.ds(pl.multiple_of((half * per_half + w) * (depth + 1) * 8 + d * 8, 8), 8), :]
                v = values[pl.ds(pl.multiple_of(((half * per_half + w) * depth + d) * 8, 8), 8), :]
                mark = lane == w * depth + d
                cv = c * v
                for n, (tile, at) in enumerate(((cv, 0), (c, 0), (cv, 127), (c, 127))):
                    carry[n] = jnp.where(mark, spread(tile, at), carry[n])
            return tuple(carry)

        packed = lax.fori_loop(0, per_half, pack, (zero,) * 4)
        for n in range(2):
            begin = (n * (layers // 128) + half) * 8
            col_low[begin : begin + 8, :] = packed[n]
            col_high[begin : begin + 8, :] = packed[2 + n]


def coarse_kernel(count, place, sums, gathered, out):
    lane = lane_iota()
    sub = sub_iota()
    inside = lane < count
    width = sums.shape[0]
    cells = jnp.where(inside, sums[...], 0.0)
    low_row = jnp.where(inside, pltpu.roll(sums[...], 128 - 16, 1), 0.0)
    low_col = jnp.where(inside, pltpu.roll(sums[...], 128 - 32, 1), 0.0)
    low_row = jnp.where(lane == 0, 0.0, low_row)
    low_col = jnp.where(sub == 0, 0.0, low_col)
    high_row = pltpu.roll(low_row, 127, 1)
    high_col = pltpu.roll(low_col, 7, 0)
    diagonal = jnp.where(inside, compress * cells + low_row + high_row + low_col + high_col, 1.0)
    rhs = jnp.zeros((8, 128), F32)
    for p in range(count):
        rhs = jnp.where(lane == p, spread(gathered[p * width : p * width + width, :], 1), rhs)

    def line(tile, k):
        return jnp.broadcast_to(tile[k : k + 1, :], (8, 128))

    zero = jnp.zeros((8, 128), F32)
    main, lower, upper, right = [], [], [], []
    for k in range(width):
        row = jnp.where(sub == k, line(diagonal, k), zero)
        if k > 0:
            row = jnp.where(sub == k - 1, -line(low_col, k), row)
        if k + 1 < width:
            row = jnp.where(sub == k + 1, -line(low_col, k + 1), row)
        main.append(row)
        lower.append(jnp.where(sub == k, -line(low_row, k), zero))
        upper.append(jnp.where(sub == k, -line(high_row, k), zero))
        right.append(line(rhs, k))

    def eliminate(main, others):
        main = list(main)
        others = [list(rows) for rows in others]
        for k in range(width):
            inverse = 1.0 / line(main[k], k)
            main[k] = main[k] * inverse
            for rows in others:
                rows[k] = rows[k] * inverse
            for j in range(width):
                if j != k:
                    factor = line(main[j], k)
                    main[j] = main[j] - factor * main[k]
                    for rows in others:
                        rows[j] = rows[j] - factor * rows[k]
        return others

    stride = 1
    while stride < count:
        solved = eliminate(main, [lower, upper, right])
        back = [[pltpu.roll(x, stride, 1) for x in rows] for rows in solved]
        ahead = [[pltpu.roll(x, 128 - stride, 1) for x in rows] for rows in solved]
        new_lower, new_upper, new_main, new_right = [], [], [], []
        for k in range(width):
            lo, up, mid, rt = zero, zero, main[k], right[k]
            for j in range(width):
                a = line(lower[k], j)
                b = line(upper[k], j)
                lo = lo - a * back[0][j]
                mid = mid - a * back[1][j] - b * ahead[0][j]
                up = up - b * ahead[1][j]
                rt = rt - a * back[2][j] - b * ahead[2][j]
            new_lower.append(lo)
            new_upper.append(up)
            new_main.append(mid)
            new_right.append(rt)
        lower, upper, main, right = new_lower, new_upper, new_main, new_right
        stride *= 2
    (right,) = eliminate(main, [right])
    mine = zero
    for k in range(width):
        mine = jnp.where(place[0] == k, right[k], mine)
    out[...] = lane_pick(mine, place[2])


def final_kernel(depth, got, values, row_low, row_high, col_low, col_high, coarse, out):
    lane = lane_iota()
    sub = sub_iota()
    layers = values.shape[0] // 8
    halves = layers // 128
    per_half = 128 // depth
    add = coarse[...]
    for half in range(halves):
        def some(w, carry):
            for d in range(depth):
                part = half * per_half + w
                g = part * depth + d
                here = pl.ds(pl.multiple_of(g * 8, 8), 8)
                c = got[pl.ds(pl.multiple_of(part * (depth + 1) * 8 + d * 8, 8), 8), :]
                v = values[here, :]
                pair = []
                for n, tile in enumerate((c * v, c)):
                    begin = (n * halves + half) * 8
                    tile = tile + jnp.where(sub == 0, row_low[pl.ds(n * layers + g, 1), :], 0.0)
                    tile = tile + jnp.where(sub == 7, row_high[pl.ds(n * layers + g, 1), :], 0.0)
                    at = w * depth + d
                    tile = tile + jnp.where(lane == 0, lane_pick(col_low[begin : begin + 8, :], at), 0.0)
                    tile = tile + jnp.where(lane == 127, lane_pick(col_high[begin : begin + 8, :], at), 0.0)
                    pair.append(tile)
                out[here, :] = pair[0] / pair[1] + add
            return carry

        lax.fori_loop(0, per_half, some, 0)


def forward(array, axis):
    count = lax.axis_size(axis)
    return lax.ppermute(array, axis, [(i, i + 1) for i in range(count - 1)])


def backward(array, axis):
    count = lax.axis_size(axis)
    return lax.ppermute(array, axis, [(i + 1, i) for i in range(count - 1)])


def shards(saturation, pressure, rock_class, rock_table, well_columns, well_rates, residual):
    depth, rows_all, cols = saturation.shape
    layers, brick_rows, _ = residual.shape
    wide, narrow = lax.axis_size("wide"), lax.axis_size("narrow")
    block = (depth, rows_all, cols)
    plane = (rows_all, cols)
    place = jnp.stack(
        [lax.axis_index("narrow"), jnp.int32(narrow), lax.axis_index("wide")]
    ).astype(jnp.int32)
    vmem = pl.BlockSpec(memory_space=pltpu.VMEM)
    smem = pl.BlockSpec(memory_space=pltpu.SMEM)
    anywhere = pl.BlockSpec(memory_space=pl.ANY)

    perm, wgain, ogain, frac, low, high, left, right = call(
        prep_kernel, [block] * 4 + [(3,) + plane] * 2 + [plane] * 2, name="prep"
    )(rock_table, saturation, pressure, rock_class)
    below = forward(high, "wide")
    above = backward(low, "wide")
    from_left = forward(right, "narrow")
    from_right = backward(left, "narrow")
    net, source, message = call(
        flow_kernel,
        [block, plane, (wide * narrow, 128)],
        scratch=[pltpu.VMEM(plane, F32)] * 6,
        in_specs=[smem] + [vmem] * 12,
        name="flow",
    )(
        place, perm, frac, pressure, below, above, left, right, from_left, from_right,
        well_columns.reshape(-1, 1), well_rates.reshape(-1, 1), residual,
    )
    gathered = lax.all_to_all(message, ("wide", "narrow"), 0, 0, tiled=True)
    chunk_rows = wide * (depth + 1) * 8
    sat_new, chunks, first, last, cell_sum, row_sum = call(
        update_kernel, [block, (chunk_rows, 128)] + [plane] * 4, name="update"
    )(gathered, saturation, net, source, perm, wgain, ogain)
    beside = forward(last, "narrow")
    (chunks,) = call(
        functools.partial(sums_kernel, depth),
        [(chunk_rows, 128)],
        scratch=[pltpu.VMEM((8, 128), F32), pltpu.SemaphoreType.DMA((wide,))],
        aliases={0: 0},
        in_specs=[anywhere] + [vmem] * 4,
        out_specs=[anywhere],
        name="sums",
    )(chunks, first, beside, cell_sum, row_sum)
    got = lax.all_to_all(chunks, "wide", 0, 0, tiled=True)
    extra = jnp.sum(got.reshape(wide, depth + 1, 8, 128)[:, depth], axis=0)
    sums = lax.all_to_all(extra, "narrow", 0, 0, tiled=True)
    values, row_low, row_high, col_low, col_high = call(
        functools.partial(relax_kernel, depth),
        [(layers * 8, 128)] + [(2 * layers, 128)] * 2 + [(2 * layers // 128 * 8, 128)] * 2,
        scratch=[pltpu.VMEM((layers * 8 + 8, 128), F32)] + [pltpu.VMEM((layers * 8, 128), F32)] * 3,
        name="relaxation",
    )(got, residual.reshape(layers * 8, 128))
    from_low = forward(row_high, "wide")
    from_high = backward(row_low, "wide")
    from_left = forward(col_high, "narrow")
    from_right = backward(col_low, "narrow")
    (coarse,) = call(
        functools.partial(coarse_kernel, wide),
        [(8, 128)],
        in_specs=[smem, vmem, vmem],
        name="coarse",
    )(place, sums, gathered)
    (precond,) = call(
        functools.partial(final_kernel, depth), [(layers * 8, 128)], name="final"
    )(got, values, from_low, from_high, from_left, from_right, coarse)
    return (sat_new, precond.reshape(layers, brick_rows, cols))


def solution(mesh):
    placed = (
        P("wide", None, "narrow"),
        P("wide", None, "narrow"),
        P("wide", None, "narrow"),
        P(),
        P(),
        P(),
        P(None, "wide", "narrow"),
    )
    return jax.shard_map(
        shards,
        mesh=mesh,
        in_specs=placed,
        out_specs=(P("wide", None, "narrow"), P(None, "wide", "narrow")),
        check_vma=False,
    )
```

```python
import functools

import jax
import jax.numpy as jnp
from jax import lax
from jax.experimental import pallas as pl
from jax.experimental.pallas import tpu as pltpu
from jax.sharding import PartitionSpec as P

SWEEPS = 6
compress = 0.05
relax = 0.8
gravity = 0.5
courant = 0.5
tiny = 1e-06

F32 = jnp.float32
HIGH = lax.Precision.HIGHEST
PARAMS = pltpu.CompilerParams(vmem_limit_bytes=16 * 1024 * 1024)


def harmonic(low, high):
    return 2.0 * low * high / (low + high)


def sub_iota():
    return lax.broadcasted_iota(jnp.int32, (8, 128), 0)


def lane_iota():
    return lax.broadcasted_iota(jnp.int32, (8, 128), 1)


def lane_pick(tile, index):
    return jnp.take_along_axis(tile, jnp.full((8, 128), index, jnp.int32), axis=1)


def spread(tile, lane):
    return jnp.broadcast_to(tile[:, lane : lane + 1], (8, 128))


def call(kernel, outs, scratch=(), aliases=None, out_specs=None, in_specs=None, name=None):
    def run(*args):
        return pl.pallas_call(
            kernel,
            out_shape=[jax.ShapeDtypeStruct(shape, F32) for shape in outs],
            in_specs=in_specs or [pl.BlockSpec(memory_space=pltpu.VMEM)] * len(args),
            out_specs=out_specs or [pl.BlockSpec(memory_space=pltpu.VMEM)] * len(outs),
            scratch_shapes=list(scratch),
            input_output_aliases=aliases or {},
            compiler_params=PARAMS,
            name=name,
        )(*args)

    return run


def prep_kernel(
    place, table, sat_in, press_in, rock_in, sat, press, perm, wgain, ogain, frac,
    face_a, face_b, pack_a, pack_b, rock, sem,
):
    lane = lane_iota()
    depth, rows_all, _ = sat.shape
    groups = 4
    each = rows_all // groups
    copies = []
    for g in range(groups):
        part = pl.ds(g * each, each)
        for n, (src, dst) in enumerate(((rock_in, rock), (sat_in, sat), (press_in, press))):
            copies.append(
                pltpu.make_async_copy(src.at[:, part, :], dst.at[:, part, :], sem.at[g * 3 + n])
            )
            copies[-1].start()
    tables = [
        jnp.broadcast_to(
            jnp.concatenate([table[n : n + 1, :], jnp.zeros((1, 112), F32)], axis=1), (8, 128)
        )
        for n in range(3)
    ]
    entries = [[jnp.broadcast_to(table[n : n + 1, m : m + 1], (8, 128)) for m in range(16)] for n in range(3)]

    def tree(kind, n):
        values = entries[n]
        for bit in range(4):
            taken = (kind & (1 << bit)) != 0
            values = [jnp.where(taken, values[m + 1], values[m]) for m in range(0, len(values), 2)]
        return values[0]

    even_row = place[2] % 2 == 0
    even_col = place[0] % 2 == 0

    def rows(step, carry):
        at = pl.ds(pl.multiple_of(step * 8, 8), 8)
        first = jnp.zeros((8, 128), F32)
        last = jnp.zeros((8, 128), F32)
        for d in range(depth):
            kind = rock[d, at, :]
            k = jnp.take_along_axis(tables[0], kind, axis=1)
            wg = jnp.take_along_axis(tables[1], kind, axis=1)
            og = jnp.take_along_axis(tables[2], kind, axis=1)
            s = sat[d, at, :]
            p = press[d, at, :]
            water = wg * s * s
            oil = og * (1.0 - s) * (1.0 - s)
            f = water / (water + oil)
            perm[d, at, :] = k
            wgain[d, at, :] = wg
            ogain[d, at, :] = og
            frac[d, at, :] = f
            for n, field in enumerate((p, k, f)):
                spot = n * depth + d
                turned = pltpu.roll(field, spot + 1, 1)
                first = jnp.where(lane == spot + 1, turned, first)
                last = jnp.where(lane == spot, turned, last)
        first = pltpu.roll(first, 127, 1)
        pack_a[at, :] = jnp.where(even_col, last, first)
        pack_b[at, :] = jnp.where(even_col, first, last)
        for n, ref in enumerate((press, perm, frac)):
            low, high = ref[0, at, :], ref[depth - 1, at, :]
            face_a[n, at, :] = jnp.where(even_row, high, low)
            face_b[n, at, :] = jnp.where(even_row, low, high)
        return carry

    for g in range(groups):
        for copy in copies[g * 3 : g * 3 + 3]:
            copy.wait()
        lax.fori_loop(g * (each // 8), (g + 1) * (each // 8), rows, 0)


def flows(low, high, lift):
    total = low[1] * high[1] / (low[1] + high[1]) * (low[0] - high[0] + lift)
    return total, total * jnp.where(total > 0, low[2], high[2])


def flow_kernel(
    bricks, place, press, perm, frac, face_a, face_b, pack_a, pack_b, got_a, got_b,
    columns, rates, residual, net, source, message, zq, zw, qp, wp,
):
    lane = lane_iota()
    sub = sub_iota()
    depth, rows_all, cols = perm.shape
    tiles = rows_all // 8
    even_row = place[2] % 2 == 0
    even_col = place[0] % 2 == 0
    half = lane >> 1
    odd = (lane & 1) == 1

    def edge(step, carry):
        at = pl.ds(pl.multiple_of(step * 8, 8), 8)

        def fields(tile):
            return [tile] + [pltpu.roll(tile, 128 - n * depth, 1) for n in (1, 2)]

        mine_a, mine_b = pack_a[at, :], pack_b[at, :]
        other_a, other_b = got_a[at, :], got_b[at, :]
        left = flows(
            fields(jnp.where(even_col, other_b, other_a)),
            fields(jnp.where(even_col, mine_b, mine_a)),
            0.0,
        )
        right = flows(
            fields(jnp.where(even_col, mine_a, mine_b)),
            fields(jnp.where(even_col, other_a, other_b)),
            0.0,
        )
        for out, low, high in zip((qp, wp), left, right):
            out[at, :] = jnp.where(
                odd,
                jnp.take_along_axis(low, half, axis=1),
                jnp.take_along_axis(high, half, axis=1),
            )
        q, w = flows(
            [jnp.where(even_row, face_b[n, at, :], face_a[n, at, :]) for n in range(3)],
            [press[0, at, :], perm[0, at, :], frac[0, at, :]],
            gravity,
        )
        zq[at, :] = q
        zw[at, :] = w
        return carry

    lax.fori_loop(0, tiles, edge, 0)

    def layer(d, top, upper):
        cur = [ref[d, 0:8, :] for ref in (press, perm, frac)]
        cur_roll = [pltpu.roll(x, 7, 0) for x in cur]
        last_q = last_w = jnp.zeros((8, 128), F32)
        for i in range(tiles):
            at = slice(i * 8, i * 8 + 8)
            if i + 1 < tiles:
                nxt = [ref[d, i * 8 + 8 : i * 8 + 16, :] for ref in (press, perm, frac)]
                nxt_roll = [pltpu.roll(x, 7, 0) for x in nxt]
            else:
                nxt, nxt_roll = cur, cur_roll
            q, w = flows(cur, upper(at), gravity)
            low_q, low_w = zq[at, :], zw[at, :]
            zq[at, :] = q
            zw[at, :] = w
            net_sum = w - low_w
            out = jnp.maximum(q, 0.0) - jnp.minimum(low_q, 0.0)
            up = [jnp.where(sub == 7, b, a) for a, b in zip(cur_roll, nxt_roll)]
            q, w = flows(cur, up, 0.0)
            if i + 1 == tiles:
                q = jnp.where(sub == 7, 0.0, q)
                w = jnp.where(sub == 7, 0.0, w)
            q_roll, w_roll = pltpu.roll(q, 1, 0), pltpu.roll(w, 1, 0)
            low_q = jnp.where(sub == 0, last_q, q_roll)
            low_w = jnp.where(sub == 0, last_w, w_roll)
            last_q, last_w = q_roll, w_roll
            net_sum = net_sum + (w - low_w)
            out = out + (jnp.maximum(q, 0.0) - jnp.minimum(low_q, 0.0))
            q, w = flows(cur, [pltpu.roll(x, 127, 1) for x in cur], 0.0)
            edge_q = pltpu.roll(qp[at, :], 127 - 2 * d, 1)
            edge_w = pltpu.roll(wp[at, :], 127 - 2 * d, 1)
            low_q = jnp.where(lane == 0, edge_q, pltpu.roll(q, 1, 1))
            low_w = jnp.where(lane == 0, edge_w, pltpu.roll(w, 1, 1))
            q = jnp.where(lane == 127, edge_q, q)
            w = jnp.where(lane == 127, edge_w, w)
            net[d, at, :] = 2.0 * (net_sum + (w - low_w))
            out = out + (jnp.maximum(q, 0.0) - jnp.minimum(low_q, 0.0))
            top = jnp.maximum(top, out)
            cur, cur_roll = nxt, nxt_roll
        return top

    top = lax.fori_loop(
        0,
        depth - 1,
        lambda d, top: layer(
            d, top, lambda at: [ref[d + 1, at, :] for ref in (press, perm, frac)]
        ),
        jnp.zeros((8, 128), F32),
    )
    top = layer(
        depth - 1,
        top,
        lambda at: [jnp.where(even_row, face_a[n, at, :], face_b[n, at, :]) for n in range(3)],
    )

    def add(step, sums):
        at = step * 8
        return tuple(s + residual[at + n] for n, s in enumerate(sums))

    sums = lax.fori_loop(0, residual.shape[0] // 8, add, (jnp.zeros((8, 128), F32),) * 8)
    total = sum(sums[1:], sums[0])
    message[...] = jnp.where(
        lax.broadcasted_iota(jnp.int32, message.shape, 1) == 0,
        2.0 * jnp.max(top),
        jnp.sum(total),
    )

    wells = columns.shape[1]
    spot = lax.broadcasted_iota(jnp.int32, (rows_all, wells), 0)
    apart = columns[...] - spot * (cols * bricks)
    in_row = jnp.where((apart >= 0) & (apart < cols * bricks), 1.0, 0.0)
    number = columns[...]
    well_col = number & (cols * bricks - 1) if (cols * bricks) & (cols * bricks - 1) == 0 else number % (cols * bricks)
    spot = lax.broadcasted_iota(jnp.int32, (cols, wells), 0)
    in_col = jnp.where(well_col - place[0] * cols == spot, rates[...], 0.0)
    source[...] = lax.dot_general(
        in_row, in_col, (((1,), (1,)), ((), ())), precision=HIGH, preferred_element_type=F32
    )


def update_kernel(
    gathered, sat, net, source, perm, wgain, ogain, new, chunks, first, last, cell_sum, row_sum
):
    lane = lane_iota()
    depth, rows_all, _ = sat.shape
    tiles = rows_all // 8
    stride = (depth + 1) * 8
    spot = lax.broadcasted_iota(jnp.int32, gathered.shape, 1)
    top = jnp.max(jnp.where(spot == 0, gathered[...], 0.0), keepdims=True)
    step_size = jnp.broadcast_to(courant / (top + tiny), (8, 128))

    def rows(step, carry):
        at = pl.ds(pl.multiple_of(step * 8, 8), 8)
        begin = step * stride
        add = step_size * source[at, :]
        total = jnp.zeros((8, 128), F32)
        low = jnp.zeros((8, 128), F32)
        high = jnp.zeros((8, 128), F32)
        for d in range(depth):
            s = sat[d, at, :] - step_size * net[d, at, :] + add
            new[d, at, :] = s
            c = perm[d, at, :] * (
                wgain[d, at, :] * s * s + ogain[d, at, :] * (1.0 - s) * (1.0 - s)
            )
            chunks[pl.ds(pl.multiple_of(begin + d * 8, 8), 8), :] = c
            total = total + c
            turned = pltpu.roll(c, d + 1, 1)
            low = jnp.where(lane == d + 1, turned, low)
            high = jnp.where(lane == d, turned, high)
        first[at, :] = pltpu.roll(low, 127, 1)
        last[at, :] = high
        cell_sum[at, :] = total
        return carry

    lax.fori_loop(0, tiles, rows, 0)
    row_sum[0:8, :] = jnp.zeros((8, 128), F32)
    for p in range(1, tiles):
        total = jnp.zeros((8, 128), F32)
        for half in range(depth // 8):
            low = chunks[pl.ds((p - 1) * stride + half * 64 + 7, 8, stride=8), :]
            high = chunks[pl.ds(p * stride + half * 64, 8, stride=8), :]
            total = total + harmonic(low, high)
        row_sum[p * 8 : p * 8 + 8, :] = total


def sums_kernel(depth, chunks_in, first, beside, cell_sum, row_sum, chunks, tile, sem):
    rows_all = first.shape[0]
    tiles = rows_all // 8
    lane = lax.broadcasted_iota(jnp.int32, (rows_all, 128), 1)
    brick = lax.broadcasted_iota(jnp.int32, (rows_all, 128), 0) // 8
    col_face = jnp.where(lane < depth, harmonic(beside[...], first[...]), 0.0)
    total = jnp.zeros((1, 128), F32)
    for n, part in enumerate((cell_sum[...], row_sum[...], col_face)):
        each = jnp.sum(part, axis=1, keepdims=True)
        placed = jnp.where(lane == n * 16 + brick, each, 0.0)
        total = total + jnp.sum(placed, axis=0, keepdims=True)
    tile[...] = jnp.broadcast_to(total, (8, 128))
    copies = []
    for p in range(tiles):
        begin = p * (depth + 1) * 8 + depth * 8
        copies.append(pltpu.make_async_copy(tile, chunks.at[pl.ds(begin, 8), :], sem.at[p]))
        copies[-1].start()
    for copy in copies:
        copy.wait()


def relax_kernel(depth, place, got, residual, values, row_a, row_b, message, fd, fr, fc, gain, base):
    lane = lane_iota()
    sub = sub_iota()
    layers = residual.shape[0] // 8
    parts = layers // depth
    zero = jnp.zeros((8, 128), F32)
    fd[0:8, :] = zero
    even_row = place[2] % 2 == 0

    def half_face(low, high):
        return low * high / (low + high)

    def build(w, carry):
        below, total = carry
        begin = w * (depth + 1) * 8
        place_w = w * depth * 8
        after = jnp.minimum(w + 1, parts - 1) * (depth + 1) * 8
        c = got[pl.ds(pl.multiple_of(begin, 8), 8), :]
        for d in range(depth):
            here = pl.ds(pl.multiple_of(place_w + d * 8, 8), 8)
            if d + 1 < depth:
                c_next = got[pl.ds(pl.multiple_of(begin + d * 8 + 8, 8), 8), :]
                above = half_face(c, c_next)
            else:
                c_next = got[pl.ds(pl.multiple_of(after, 8), 8), :]
                above = jnp.where(w + 1 < parts, half_face(c, c_next), 0.0)
            row = jnp.where(sub == 0, 0.0, half_face(pltpu.roll(c, 1, 0), c))
            col = jnp.where(lane == 0, 0.0, half_face(pltpu.roll(c, 1, 1), c))
            diag = (
                (0.5 * compress) * c + below + above
                + row + pltpu.roll(row, 7, 0) + col + pltpu.roll(col, 127, 1)
            )
            scale = relax / diag
            fd[pl.ds(pl.multiple_of(place_w + d * 8 + 8, 8), 8), :] = above
            fr[here, :] = row
            fc[here, :] = col
            gain[here, :] = scale
            first = (0.5 * scale) * residual[here, :]
            base[here, :] = first
            values[here, :] = first
            c, below = c_next, above
        total = total + got[pl.ds(pl.multiple_of(begin + depth * 8, 8), 8), :]
        return below, total

    _, total = lax.fori_loop(0, parts, build, (zero, zero))

    block = 16

    def sweep(number, carry):
        def some(step, prev):
            begin = step * (block * 8)
            v = values[pl.ds(pl.multiple_of(begin, 8), 8), :]
            for n in range(block):
                here = pl.ds(pl.multiple_of(begin + n * 8, 8), 8)
                after = pl.ds(pl.multiple_of(begin + n * 8 + 8, 8), 8)
                if n + 1 < block:
                    v_next = values[after, :]
                else:
                    last = jnp.minimum(begin + block * 8, layers * 8 - 8)
                    v_next = values[pl.ds(pl.multiple_of(last, 8), 8), :]
                row = fr[here, :]
                col = fc[here, :]
                total = fd[here, :] * prev + fd[after, :] * v_next
                total = total + (row * pltpu.roll(v, 1, 0) + pltpu.roll(row * v, 7, 0))
                total = total + (col * pltpu.roll(v, 1, 1) + pltpu.roll(col * v, 127, 1))
                values[here, :] = ((1.0 - relax) * v + base[here, :]) + gain[here, :] * total
                prev, v = v, v_next
            return prev

        return lax.fori_loop(0, layers // block, some, zero)

    lax.fori_loop(0, SWEEPS - 1, sweep, zero)

    for w in range(parts):
        for half in range(depth // 8):
            at = w * (depth + 1) * 8 + half * 64
            spot = w * depth + half * 8
            pairs = []
            for row in (0, 7):
                c = got[pl.ds(at + row, 8, stride=8), :]
                v = values[pl.ds(spot * 8 + row, 8, stride=8), :]
                pairs.append((c * v, c))
            for n in range(2):
                low, high = pairs[0][n], pairs[1][n]
                rows = slice(n * layers + spot, n * layers + spot + 8)
                row_a[rows, :] = jnp.where(even_row, high, low)
                row_b[rows, :] = jnp.where(even_row, low, high)

    quarters = layers // 64
    per_tile = 64 // depth
    peers = message.shape[0] // (quarters * 16 + 8)
    for quarter in range(quarters):
        def pack(w, carry):
            carry = list(carry)
            part = quarter * per_tile + w
            for d in range(depth):
                c = got[pl.ds(pl.multiple_of(part * (depth + 1) * 8 + d * 8, 8), 8), :]
                v = values[pl.ds(pl.multiple_of((part * depth + d) * 8, 8), 8), :]
                spot = 2 * (w * depth + d) + 2
                mark = (lane == spot - 1) | (lane == (spot & 127))
                for n, tile in enumerate((c * v, c)):
                    carry[n] = jnp.where(mark, pltpu.roll(tile, spot & 127, 1), carry[n])
            return tuple(carry)

        packed = lax.fori_loop(0, per_tile, pack, (zero, zero))
        for peer in range(peers):
            for n in range(2):
                begin = peer * (quarters * 16 + 8) + (n * quarters + quarter) * 8
                message[begin : begin + 8, :] = packed[n]
    for peer in range(peers):
        begin = peer * (quarters * 16 + 8) + quarters * 16
        message[begin : begin + 8, :] = total


def coarse_kernel(count, place, news, gathered, out):
    lane = lane_iota()
    sub = sub_iota()
    inside = lane < count
    width = gathered.shape[0] // count
    stride = news.shape[0] // width
    sums = jnp.zeros((8, 128), F32)
    for k in range(width):
        sums = jnp.where(sub == k, news[(k + 1) * stride - 8 : (k + 1) * stride, :], sums)
    cells = jnp.where(inside, sums, 0.0)
    low_row = jnp.where(inside, pltpu.roll(sums, 128 - 16, 1), 0.0)
    low_col = jnp.where(inside, pltpu.roll(sums, 128 - 32, 1), 0.0)
    low_row = jnp.where(lane == 0, 0.0, low_row)
    low_col = jnp.where(sub == 0, 0.0, low_col)
    high_row = pltpu.roll(low_row, 127, 1)
    high_col = pltpu.roll(low_col, 7, 0)
    diagonal = jnp.where(inside, compress * cells + low_row + high_row + low_col + high_col, 1.0)
    rhs = jnp.zeros((8, 128), F32)
    for p in range(count):
        rhs = jnp.where(lane == p, spread(gathered[p * width : p * width + width, :], 1), rhs)

    def line(tile, k):
        return jnp.broadcast_to(tile[k : k + 1, :], (8, 128))

    zero = jnp.zeros((8, 128), F32)
    main, lower, upper, right = [], [], [], []
    for k in range(width):
        row = jnp.where(sub == k, line(diagonal, k), zero)
        if k > 0:
            row = jnp.where(sub == k - 1, -line(low_col, k), row)
        if k + 1 < width:
            row = jnp.where(sub == k + 1, -line(low_col, k + 1), row)
        main.append(row)
        lower.append(jnp.where(sub == k, -line(low_row, k), zero))
        upper.append(jnp.where(sub == k, -line(high_row, k), zero))
        right.append(line(rhs, k))

    def eliminate(main, others):
        main = list(main)
        others = [list(rows) for rows in others]
        for k in range(width):
            inverse = 1.0 / line(main[k], k)
            main[k] = main[k] * inverse
            for rows in others:
                rows[k] = rows[k] * inverse
            for j in range(width):
                if j != k:
                    factor = line(main[j], k)
                    main[j] = main[j] - factor * main[k]
                    for rows in others:
                        rows[j] = rows[j] - factor * rows[k]
        return others

    stride = 1
    while stride < count:
        solved = eliminate(main, [lower, upper, right])
        back = [[pltpu.roll(x, stride, 1) for x in rows] for rows in solved]
        ahead = [[pltpu.roll(x, 128 - stride, 1) for x in rows] for rows in solved]
        new_lower, new_upper, new_main, new_right = [], [], [], []
        for k in range(width):
            lo, up, mid, rt = zero, zero, main[k], right[k]
            for j in range(width):
                a = line(lower[k], j)
                b = line(upper[k], j)
                lo = lo - a * back[0][j]
                mid = mid - a * back[1][j] - b * ahead[0][j]
                up = up - b * ahead[1][j]
                rt = rt - a * back[2][j] - b * ahead[2][j]
            new_lower.append(lo)
            new_upper.append(up)
            new_main.append(mid)
            new_right.append(rt)
        lower, upper, main, right = new_lower, new_upper, new_main, new_right
        stride *= 2
    (right,) = eliminate(main, [right])
    mine = zero
    for k in range(width):
        mine = jnp.where(place[0] == k, right[k], mine)
    out[...] = lane_pick(mine, place[2])


def final_kernel(depth, place, got, values, row_a, row_b, news, coarse, out, packs):
    lane = lane_iota()
    sub = sub_iota()
    layers = values.shape[0] // 8
    quarters = layers // 64
    per_tile = 64 // depth
    add = coarse[...]
    even_row = place[2] % 2 == 0
    stride = quarters * 16 + 8
    left = pl.multiple_of(jnp.maximum(place[0] - 1, 0) * stride, 8)
    right = pl.multiple_of(jnp.minimum(place[0] + 1, place[1] - 1) * stride, 8)
    odd = (lane & 1) == 1
    has_left = odd & (place[0] > 0)
    has_right = jnp.logical_not(odd) & (place[0] + 1 < place[1])
    for n in range(quarters * 2):
        low = news[pl.ds(left + n * 8, 8), :]
        high = pltpu.roll(news[pl.ds(right + n * 8, 8), :], 126, 1)
        packs[n * 8 : n * 8 + 8, :] = jnp.where(has_left, low, jnp.where(has_right, high, 0.0))
    ends = (lane == 0) | (lane == 127)

    def some(w, carry):
        for d in range(depth):
            g = w * depth + d
            here = pl.ds(pl.multiple_of(g * 8, 8), 8)
            c = got[pl.ds(pl.multiple_of(w * (depth + 1) * 8 + d * 8, 8), 8), :]
            v = values[here, :]
            quarter = w // per_tile
            shift = 127 - 2 * ((w % per_tile) * depth + d)
            pair = []
            for n, tile in enumerate((c * v, c)):
                at = pl.ds(n * layers + g, 1)
                low = jnp.where(even_row, row_b[at, :], row_a[at, :])
                high = jnp.where(even_row, row_a[at, :], row_b[at, :])
                side = packs[pl.ds(pl.multiple_of((n * quarters + quarter) * 8, 8), 8), :]
                tile = tile + jnp.where(sub == 0, low, jnp.where(sub == 7, high, 0.0))
                tile = tile + jnp.where(ends, pltpu.roll(side, shift, 1), 0.0)
                pair.append(tile)
            out[here, :] = pair[0] / pair[1] + add
        return carry

    lax.fori_loop(0, layers // depth, some, 0)


def partners(array, axis, odd):
    count = lax.axis_size(axis)
    pairs = [(i, i + 1) for i in range(odd, count - 1, 2)]
    return lax.ppermute(array, axis, pairs + [(j, i) for i, j in pairs])


def forward(array, axis):
    count = lax.axis_size(axis)
    return lax.ppermute(array, axis, [(i, i + 1) for i in range(count - 1)])


def shards(saturation, pressure, rock_class, rock_table, well_columns, well_rates, residual):
    depth, rows_all, cols = saturation.shape
    layers, brick_rows, _ = residual.shape
    wide, narrow = lax.axis_size("wide"), lax.axis_size("narrow")
    block = (depth, rows_all, cols)
    plane = (rows_all, cols)
    place = jnp.stack(
        [lax.axis_index("narrow"), jnp.int32(narrow), lax.axis_index("wide")]
    ).astype(jnp.int32)
    vmem = pl.BlockSpec(memory_space=pltpu.VMEM)
    smem = pl.BlockSpec(memory_space=pltpu.SMEM)
    anywhere = pl.BlockSpec(memory_space=pl.ANY)

    sat, press, perm, wgain, ogain, frac, face_a, face_b, pack_a, pack_b = call(
        prep_kernel,
        [block] * 6 + [(3,) + plane] * 2 + [plane] * 2,
        scratch=[pltpu.VMEM(block, jnp.int32), pltpu.SemaphoreType.DMA((12,))],
        in_specs=[smem, vmem] + [anywhere] * 3,
        name="prep",
    )(place, rock_table, saturation, pressure, rock_class)
    got_face_a = partners(face_a, "wide", 0)
    got_face_b = partners(face_b, "wide", 1)
    got_pack_a = partners(pack_a, "narrow", 0)
    got_pack_b = partners(pack_b, "narrow", 1)
    net, source, message = call(
        functools.partial(flow_kernel, narrow),
        [block, plane, (wide * narrow, 128)],
        scratch=[pltpu.VMEM(plane, F32)] * 4,
        in_specs=[smem] + [vmem] * 12,
        name="flow",
    )(
        place, press, perm, frac, got_face_a, got_face_b, pack_a, pack_b, got_pack_a, got_pack_b,
        well_columns.reshape(1, -1), well_rates.reshape(1, -1), residual,
    )
    gathered = lax.all_to_all(message, ("wide", "narrow"), 0, 0, tiled=True)
    chunk_rows = wide * (depth + 1) * 8
    sat_new, chunks, first, last, cell_sum, row_sum = call(
        update_kernel, [block, (chunk_rows, 128)] + [plane] * 4, name="update"
    )(gathered, sat, net, source, perm, wgain, ogain)
    beside = forward(last, "narrow")
    (chunks,) = call(
        functools.partial(sums_kernel, depth),
        [(chunk_rows, 128)],
        scratch=[pltpu.VMEM((8, 128), F32), pltpu.SemaphoreType.DMA((wide,))],
        aliases={0: 0},
        in_specs=[anywhere] + [vmem] * 4,
        out_specs=[anywhere],
        name="sums",
    )(chunks, first, beside, cell_sum, row_sum)
    got = lax.all_to_all(chunks, "wide", 0, 0, tiled=True)
    message_rows = narrow * (layers // 4 + 8)
    values, row_a, row_b, message = call(
        functools.partial(relax_kernel, depth),
        [(layers * 8, 128)] + [(2 * layers, 128)] * 2 + [(message_rows, 128)],
        scratch=[pltpu.VMEM((layers * 8 + 8, 128), F32)] + [pltpu.VMEM((layers * 8, 128), F32)] * 4,
        in_specs=[smem, vmem, vmem],
        name="relaxation",
    )(place, got, residual.reshape(layers * 8, 128))
    got_row_a = partners(row_a, "wide", 0)
    got_row_b = partners(row_b, "wide", 1)
    news = lax.all_to_all(message, "narrow", 0, 0, tiled=True)
    (coarse,) = call(
        functools.partial(coarse_kernel, wide),
        [(8, 128)],
        in_specs=[smem, vmem, vmem],
        name="coarse",
    )(place, news, gathered)
    (precond,) = call(
        functools.partial(final_kernel, depth),
        [(layers * 8, 128)],
        scratch=[pltpu.VMEM((layers // 4, 128), F32)],
        in_specs=[smem] + [vmem] * 6,
        name="final",
    )(place, got, values, got_row_a, got_row_b, news, coarse)
    return (sat_new, precond.reshape(layers, brick_rows, cols))


def solution(mesh):
    placed = (
        P("wide", None, "narrow"),
        P("wide", None, "narrow"),
        P("wide", None, "narrow"),
        P(),
        P(),
        P(),
        P(None, "wide", "narrow"),
    )
    return jax.shard_map(
        shards,
        mesh=mesh,
        in_specs=placed,
        out_specs=(P("wide", None, "narrow"), P(None, "wide", "narrow")),
        check_vma=False,
    )
```

```python
import functools

import jax
import jax.numpy as jnp
from jax import lax
from jax.experimental import pallas as pl
from jax.experimental.pallas import tpu as pltpu
from jax.sharding import PartitionSpec as P

SWEEPS = 6
compress = 0.05
relax = 0.8
gravity = 0.5
courant = 0.5
tiny = 1e-06

F32 = jnp.float32
HIGH = lax.Precision.HIGHEST
PARAMS = pltpu.CompilerParams(vmem_limit_bytes=16 * 1024 * 1024)


def harmonic(low, high):
    return 2.0 * low * high / (low + high)


def sub_iota():
    return lax.broadcasted_iota(jnp.int32, (8, 128), 0)


def lane_iota():
    return lax.broadcasted_iota(jnp.int32, (8, 128), 1)


def lane_pick(tile, index):
    return jnp.take_along_axis(tile, jnp.full((8, 128), index, jnp.int32), axis=1)


def lane_take(tile, index):
    return jnp.take_along_axis(tile, index, axis=1, mode="promise_in_bounds")


def lane_table(table, n):
    row = jnp.concatenate([table[n : n + 1, :], jnp.zeros((1, 112), F32)], axis=1)
    return jnp.broadcast_to(row, (8, 128))


def spread(tile, lane):
    return jnp.broadcast_to(tile[:, lane : lane + 1], (8, 128))


def call(kernel, outs, scratch=(), aliases=None, out_specs=None, in_specs=None, name=None):
    def run(*args):
        return pl.pallas_call(
            kernel,
            out_shape=[jax.ShapeDtypeStruct(shape, F32) for shape in outs],
            in_specs=in_specs or [pl.BlockSpec(memory_space=pltpu.VMEM)] * len(args),
            out_specs=out_specs or [pl.BlockSpec(memory_space=pltpu.VMEM)] * len(outs),
            scratch_shapes=list(scratch),
            input_output_aliases=aliases or {},
            compiler_params=PARAMS,
            name=name,
        )(*args)

    return run


def prep_kernel(
    place, table_in, sat_in, press_in, rock_in, sat, press, perm, wgain, ogain, frac,
    face_a, face_b, pack_a, pack_b, rock, table, sem,
):
    lane = lane_iota()
    depth, rows_all, _ = sat.shape
    groups = 4
    each = rows_all // groups
    small = pltpu.make_async_copy(table_in, table, sem.at[groups * 3])
    small.start()
    copies = []
    for g in range(groups):
        part = pl.ds(g * each, each)
        for n, (src, dst) in enumerate(((rock_in, rock), (sat_in, sat), (press_in, press))):
            copies.append(
                pltpu.make_async_copy(src.at[:, part, :], dst.at[:, part, :], sem.at[g * 3 + n])
            )
            copies[-1].start()
    small.wait()
    perm_table = lane_table(table, 0)
    entries = [
        [jnp.broadcast_to(table[n : n + 1, m : m + 1], (8, 128)) for m in range(16)]
        for n in range(3)
    ]

    def tree(kind, n):
        values = entries[n]
        for bit in range(4):
            taken = kind[bit]
            values = [jnp.where(taken, values[m + 1], values[m]) for m in range(0, len(values), 2)]
        return values[0]

    even_row = place[2] % 2 == 0
    even_col = place[0] % 2 == 0

    def rows(step, carry):
        at = pl.ds(pl.multiple_of(step * 8, 8), 8)
        first = jnp.zeros((8, 128), F32)
        last = jnp.zeros((8, 128), F32)
        for d in range(depth):
            kind = rock[d, at, :]
            k = lane_take(perm_table, kind)
            bits = [(kind & (1 << bit)) != 0 for bit in range(4)]
            wg = tree(bits, 1)
            og = tree(bits, 2)
            s = sat[d, at, :]
            p = press[d, at, :]
            water = wg * s * s
            oil = og * (1.0 - s) * (1.0 - s)
            f = water / (water + oil)
            perm[d, at, :] = k
            wgain[d, at, :] = wg
            ogain[d, at, :] = og
            frac[d, at, :] = f
            for n, field in enumerate((p, k, f, s, kind.astype(F32))):
                spot = n * depth + d
                turned = pltpu.roll(field, spot + 1, 1)
                if n < 3:
                    first = jnp.where(lane == spot + 1, turned, first)
                last = jnp.where(lane == spot, turned, last)
        first = pltpu.roll(first, 127, 1)
        pack_a[at, :] = jnp.where(even_col, last, first)
        pack_b[at, :] = jnp.where(even_col, first, last)
        for n, ref in enumerate((press, perm, frac)):
            low, high = ref[0, at, :], ref[depth - 1, at, :]
            face_a[n, at, :] = jnp.where(even_row, high, low)
            face_b[n, at, :] = jnp.where(even_row, low, high)
        return carry

    for g in range(groups):
        for copy in copies[g * 3 : g * 3 + 3]:
            copy.wait()
        lax.fori_loop(g * (each // 8), (g + 1) * (each // 8), rows, 0)


def flows(low, high, lift):
    total = low[1] * high[1] / (low[1] + high[1]) * (low[0] - high[0] + lift)
    return total, total * jnp.where(total > 0, low[2], high[2])


def flow_kernel(
    bricks, place, press, perm, frac, face_a, face_b, pack_a, pack_b, got_a, got_b,
    columns, rates, residual, net, source, ahead, message, zq, zw, qp, wp,
):
    lane = lane_iota()
    sub = sub_iota()
    depth, rows_all, cols = perm.shape
    tiles = rows_all // 8
    even_row = place[2] % 2 == 0
    even_col = place[0] % 2 == 0
    half = lane >> 1
    odd = (lane & 1) == 1

    wells = columns.shape[1]
    spot = lax.broadcasted_iota(jnp.int32, (rows_all, wells), 0)
    apart = columns[...] - spot * (cols * bricks)
    in_row = jnp.where((apart >= 0) & (apart < cols * bricks), 1.0, 0.0)
    number = columns[...]
    well_col = number & (cols * bricks - 1) if (cols * bricks) & (cols * bricks - 1) == 0 else number % (cols * bricks)
    spot = lax.broadcasted_iota(jnp.int32, (cols, wells), 0)
    in_col = jnp.where(well_col - place[0] * cols == spot, rates[...], 0.0)
    source[...] = lax.dot_general(
        in_row, in_col, (((1,), (1,)), ((), ())), precision=HIGH, preferred_element_type=F32
    )

    def edge(step, carry):
        at = pl.ds(pl.multiple_of(step * 8, 8), 8)
        ahead[at, :] = jnp.where(
            (lane >= depth) & (lane < 2 * depth), spread(source[at, :], 127), 0.0
        )

        def fields(tile):
            return [tile] + [pltpu.roll(tile, 128 - n * depth, 1) for n in (1, 2)]

        mine_a, mine_b = pack_a[at, :], pack_b[at, :]
        other_a, other_b = got_a[at, :], got_b[at, :]
        left = flows(
            fields(jnp.where(even_col, other_b, other_a)),
            fields(jnp.where(even_col, mine_b, mine_a)),
            0.0,
        )
        right = flows(
            fields(jnp.where(even_col, mine_a, mine_b)),
            fields(jnp.where(even_col, other_a, other_b)),
            0.0,
        )
        for out, low, high in zip((qp, wp), left, right):
            out[at, :] = jnp.where(
                odd,
                jnp.take_along_axis(low, half, axis=1),
                jnp.take_along_axis(high, half, axis=1),
            )
        q, w = flows(
            [jnp.where(even_row, face_b[n, at, :], face_a[n, at, :]) for n in range(3)],
            [press[0, at, :], perm[0, at, :], frac[0, at, :]],
            gravity,
        )
        zq[at, :] = q
        zw[at, :] = w
        return carry

    lax.fori_loop(0, tiles, edge, 0)

    def layer(d, top, upper):
        cur = [ref[d, 0:8, :] for ref in (press, perm, frac)]
        cur_roll = [pltpu.roll(x, 7, 0) for x in cur]
        last_q = last_w = jnp.zeros((8, 128), F32)
        for i in range(tiles):
            at = slice(i * 8, i * 8 + 8)
            if i + 1 < tiles:
                nxt = [ref[d, i * 8 + 8 : i * 8 + 16, :] for ref in (press, perm, frac)]
                nxt_roll = [pltpu.roll(x, 7, 0) for x in nxt]
            else:
                nxt, nxt_roll = cur, cur_roll
            q, w = flows(cur, upper(at), gravity)
            low_q, low_w = zq[at, :], zw[at, :]
            zq[at, :] = q
            zw[at, :] = w
            net_sum = w - low_w
            out = jnp.maximum(q, 0.0) - jnp.minimum(low_q, 0.0)
            up = [jnp.where(sub == 7, b, a) for a, b in zip(cur_roll, nxt_roll)]
            q, w = flows(cur, up, 0.0)
            if i + 1 == tiles:
                q = jnp.where(sub == 7, 0.0, q)
                w = jnp.where(sub == 7, 0.0, w)
            q_roll, w_roll = pltpu.roll(q, 1, 0), pltpu.roll(w, 1, 0)
            low_q = jnp.where(sub == 0, last_q, q_roll)
            low_w = jnp.where(sub == 0, last_w, w_roll)
            last_q, last_w = q_roll, w_roll
            net_sum = net_sum + (w - low_w)
            out = out + (jnp.maximum(q, 0.0) - jnp.minimum(low_q, 0.0))
            q, w = flows(cur, [pltpu.roll(x, 127, 1) for x in cur], 0.0)
            edge_q = pltpu.roll(qp[at, :], 127 - 2 * d, 1)
            edge_w = pltpu.roll(wp[at, :], 127 - 2 * d, 1)
            low_q = jnp.where(lane == 0, edge_q, pltpu.roll(q, 1, 1))
            low_w = jnp.where(lane == 0, edge_w, pltpu.roll(w, 1, 1))
            q = jnp.where(lane == 127, edge_q, q)
            w = jnp.where(lane == 127, edge_w, w)
            net_sum = 2.0 * (net_sum + (w - low_w))
            net[d, at, :] = net_sum
            ahead[at, :] = jnp.where(lane == d, pltpu.roll(net_sum, d + 1, 1), ahead[at, :])
            out = out + (jnp.maximum(q, 0.0) - jnp.minimum(low_q, 0.0))
            top = jnp.maximum(top, out)
            cur, cur_roll = nxt, nxt_roll
        return top

    top = lax.fori_loop(
        0,
        depth - 1,
        lambda d, top: layer(
            d, top, lambda at: [ref[d + 1, at, :] for ref in (press, perm, frac)]
        ),
        jnp.zeros((8, 128), F32),
    )
    top = layer(
        depth - 1,
        top,
        lambda at: [jnp.where(even_row, face_a[n, at, :], face_b[n, at, :]) for n in range(3)],
    )

    def add(step, sums):
        at = step * 8
        return tuple(s + residual[at + n] for n, s in enumerate(sums))

    sums = lax.fori_loop(0, residual.shape[0] // 8, add, (jnp.zeros((8, 128), F32),) * 8)
    total = sum(sums[1:], sums[0])
    message[...] = jnp.where(
        lax.broadcasted_iota(jnp.int32, message.shape, 1) == 0,
        2.0 * jnp.max(top),
        jnp.sum(total),
    )


def update_kernel(
    place, gathered, table, sat, net, source, perm, wgain, ogain, got_a, got_b, beside,
    new, chunks, cell_sum, row_sum, col_sum,
):
    lane = lane_iota()
    depth, rows_all, _ = sat.shape
    tiles = rows_all // 8
    stride = (depth + 1) * 8
    spot = lax.broadcasted_iota(jnp.int32, gathered.shape, 1)
    top = jnp.max(jnp.where(spot == 0, gathered[...], 0.0), keepdims=True)
    step_size = jnp.broadcast_to(courant / (top + tiny), (8, 128))
    even_col = place[0] % 2 == 0
    water_table, oil_table = lane_table(table, 1), lane_table(table, 2)

    def coefficient(k, wg, og, s):
        return k * (wg * s * s + og * (1.0 - s) * (1.0 - s))

    def rows(step, carry):
        at = pl.ds(pl.multiple_of(step * 8, 8), 8)
        begin = step * stride
        add = step_size * source[at, :]
        total = jnp.zeros((8, 128), F32)
        first = jnp.zeros((8, 128), F32)
        for d in range(depth):
            s = sat[d, at, :] - step_size * net[d, at, :] + add
            new[d, at, :] = s
            c = coefficient(perm[d, at, :], wgain[d, at, :], ogain[d, at, :], s)
            chunks[pl.ds(pl.multiple_of(begin + d * 8, 8), 8), :] = c
            total = total + c
            first = jnp.where(lane == d, pltpu.roll(c, d, 1) if d else c, first)
        cell_sum[at, :] = total
        tile = jnp.where(even_col, got_b[at, :], got_a[at, :])
        flow = beside[at, :]
        kind = jnp.where(lane < depth, pltpu.roll(tile, 128 - 4 * depth, 1), 0.0).astype(jnp.int32)
        s = pltpu.roll(tile, 128 - 3 * depth, 1) - step_size * flow
        s = s + step_size * pltpu.roll(flow, 128 - depth, 1)
        c = coefficient(
            pltpu.roll(tile, 128 - depth, 1),
            lane_take(water_table, kind),
            lane_take(oil_table, kind),
            s,
        )
        col_sum[at, :] = jnp.where(lane < depth, harmonic(c, first), 0.0)
        return carry

    lax.fori_loop(0, tiles, rows, 0)
    row_sum[0:8, :] = jnp.zeros((8, 128), F32)
    for p in range(1, tiles):
        total = jnp.zeros((8, 128), F32)
        for half in range(depth // 8):
            low = chunks[pl.ds((p - 1) * stride + half * 64 + 7, 8, stride=8), :]
            high = chunks[pl.ds(p * stride + half * 64, 8, stride=8), :]
            total = total + harmonic(low, high)
        row_sum[p * 8 : p * 8 + 8, :] = total
    brick = lax.broadcasted_iota(jnp.int32, (rows_all, 128), 0) // 8
    spot = lax.broadcasted_iota(jnp.int32, (rows_all, 128), 1)
    total = jnp.zeros((1, 128), F32)
    for n, part in enumerate((cell_sum, row_sum, col_sum)):
        each = jnp.sum(part[...], axis=1, keepdims=True)
        placed = jnp.where(spot == n * 16 + brick, each, 0.0)
        total = total + jnp.sum(placed, axis=0, keepdims=True)
    for p in range(tiles):
        chunks[p * stride + depth * 8 : (p + 1) * stride, :] = jnp.broadcast_to(total, (8, 128))


def relax_kernel(depth, place, got, residual, values, row_a, row_b, message, fd, fr, fc, gain, base):
    lane = lane_iota()
    sub = sub_iota()
    layers = residual.shape[0] // 8
    parts = layers // depth
    zero = jnp.zeros((8, 128), F32)
    fd[0:8, :] = zero
    values[layers * 8 :, :] = jnp.zeros((64, 128), F32)
    fc[layers * 8 :, :] = jnp.zeros((64, 128), F32)
    even_row = place[2] % 2 == 0

    def half_face(low, high):
        return low * high / (low + high)

    def build(w, carry):
        below, total = carry
        begin = w * (depth + 1) * 8
        place_w = w * depth * 8
        after = jnp.minimum(w + 1, parts - 1) * (depth + 1) * 8
        c = got[pl.ds(pl.multiple_of(begin, 8), 8), :]
        for d in range(depth):
            here = pl.ds(pl.multiple_of(place_w + d * 8, 8), 8)
            if d + 1 < depth:
                c_next = got[pl.ds(pl.multiple_of(begin + d * 8 + 8, 8), 8), :]
                above = half_face(c, c_next)
            else:
                c_next = got[pl.ds(pl.multiple_of(after, 8), 8), :]
                above = jnp.where(w + 1 < parts, half_face(c, c_next), 0.0)
            row = jnp.where(sub == 0, 0.0, half_face(pltpu.roll(c, 1, 0), c))
            col = jnp.where(lane == 0, 0.0, half_face(pltpu.roll(c, 1, 1), c))
            diag = (
                (0.5 * compress) * c + below + above
                + row + pltpu.roll(row, 7, 0) + col + pltpu.roll(col, 127, 1)
            )
            scale = relax / diag
            fd[pl.ds(pl.multiple_of(place_w + d * 8 + 8, 8), 8), :] = above
            fr[here, :] = row
            fc[here, :] = col
            gain[here, :] = scale
            first = (0.5 * scale) * residual[here, :]
            base[here, :] = first
            values[here, :] = first
            c, below = c_next, above
        total = total + got[pl.ds(pl.multiple_of(begin + depth * 8, 8), 8), :]
        return below, total

    _, total = lax.fori_loop(0, parts, build, (zero, zero))

    block = 8

    def turned(begin):
        rolled = []
        for n in range(block):
            here = pl.ds(pl.multiple_of(begin + n * 8, 8), 8)
            v = values[here, :]
            rolled.append((v, pltpu.roll(v, 1, 1), pltpu.roll(fc[here, :] * v, 127, 1)))
        return tuple(rolled)

    def sweep(number, carry):
        def some(step, carry):
            prev, now = carry
            begin = step * (block * 8)
            after = turned(begin + block * 8)
            for n in range(block):
                here = pl.ds(pl.multiple_of(begin + n * 8, 8), 8)
                above = pl.ds(pl.multiple_of(begin + n * 8 + 8, 8), 8)
                v, from_left, from_right = now[n]
                v_next = now[n + 1][0] if n + 1 < block else after[0][0]
                row = fr[here, :]
                total = fd[here, :] * prev + fd[above, :] * v_next
                total = total + (row * pltpu.roll(v, 1, 0) + pltpu.roll(row * v, 7, 0))
                total = total + (fc[here, :] * from_left + from_right)
                values[here, :] = ((1.0 - relax) * v + base[here, :]) + gain[here, :] * total
                prev = v
            return prev, after

        lax.fori_loop(0, layers // block, some, (zero, turned(0)))
        return carry

    lax.fori_loop(0, SWEEPS - 1, sweep, 0)

    for w in range(parts):
        for half in range(depth // 8):
            at = w * (depth + 1) * 8 + half * 64
            spot = w * depth + half * 8
            pairs = []
            for row in (0, 7):
                c = got[pl.ds(at + row, 8, stride=8), :]
                v = values[pl.ds(spot * 8 + row, 8, stride=8), :]
                pairs.append((c * v, c))
            for n in range(2):
                low, high = pairs[0][n], pairs[1][n]
                rows = slice(n * layers + spot, n * layers + spot + 8)
                row_a[rows, :] = jnp.where(even_row, high, low)
                row_b[rows, :] = jnp.where(even_row, low, high)

    quarters = layers // 64
    per_tile = 64 // depth
    peers = message.shape[0] // (quarters * 16 + 8)
    for quarter in range(quarters):
        def pack(w, carry):
            carry = list(carry)
            part = quarter * per_tile + w
            for d in range(depth):
                c = got[pl.ds(pl.multiple_of(part * (depth + 1) * 8 + d * 8, 8), 8), :]
                v = values[pl.ds(pl.multiple_of((part * depth + d) * 8, 8), 8), :]
                spot = 2 * (w * depth + d) + 2
                mark = (lane == spot - 1) | (lane == (spot & 127))
                for n, tile in enumerate((c * v, c)):
                    carry[n] = jnp.where(mark, pltpu.roll(tile, spot & 127, 1), carry[n])
            return tuple(carry)

        packed = lax.fori_loop(0, per_tile, pack, (zero, zero))
        for peer in range(peers):
            for n in range(2):
                begin = peer * (quarters * 16 + 8) + (n * quarters + quarter) * 8
                message[begin : begin + 8, :] = packed[n]
    for peer in range(peers):
        begin = peer * (quarters * 16 + 8) + quarters * 16
        message[begin : begin + 8, :] = total


def coarse_kernel(count, place, news, gathered, out):
    lane = lane_iota()
    sub = sub_iota()
    inside = lane < count
    width = gathered.shape[0] // count
    stride = news.shape[0] // width
    sums = jnp.zeros((8, 128), F32)
    for k in range(width):
        sums = jnp.where(sub == k, news[(k + 1) * stride - 8 : (k + 1) * stride, :], sums)
    cells = jnp.where(inside, sums, 0.0)
    low_row = jnp.where(inside, pltpu.roll(sums, 128 - 16, 1), 0.0)
    low_col = jnp.where(inside, pltpu.roll(sums, 128 - 32, 1), 0.0)
    low_row = jnp.where(lane == 0, 0.0, low_row)
    low_col = jnp.where(sub == 0, 0.0, low_col)
    high_row = pltpu.roll(low_row, 127, 1)
    high_col = pltpu.roll(low_col, 7, 0)
    diagonal = jnp.where(inside, compress * cells + low_row + high_row + low_col + high_col, 1.0)
    rhs = jnp.zeros((8, 128), F32)
    for p in range(count):
        rhs = jnp.where(lane == p, spread(gathered[p * width : p * width + width, :], 1), rhs)

    def line(tile, k):
        return jnp.broadcast_to(tile[k : k + 1, :], (8, 128))

    zero = jnp.zeros((8, 128), F32)
    main, lower, upper, right = [], [], [], []
    for k in range(width):
        row = jnp.where(sub == k, line(diagonal, k), zero)
        if k > 0:
            row = jnp.where(sub == k - 1, -line(low_col, k), row)
        if k + 1 < width:
            row = jnp.where(sub == k + 1, -line(low_col, k + 1), row)
        main.append(row)
        lower.append(jnp.where(sub == k, -line(low_row, k), zero))
        upper.append(jnp.where(sub == k, -line(high_row, k), zero))
        right.append(line(rhs, k))

    def eliminate(main, others):
        main = list(main)
        others = [list(rows) for rows in others]
        for k in range(width):
            inverse = 1.0 / line(main[k], k)
            main[k] = main[k] * inverse
            for rows in others:
                rows[k] = rows[k] * inverse
            for j in range(width):
                if j != k:
                    factor = line(main[j], k)
                    main[j] = main[j] - factor * main[k]
                    for rows in others:
                        rows[j] = rows[j] - factor * rows[k]
        return others

    stride = 1
    while stride < count:
        solved = eliminate(main, [lower, upper, right])
        back = [[pltpu.roll(x, stride, 1) for x in rows] for rows in solved]
        ahead = [[pltpu.roll(x, 128 - stride, 1) for x in rows] for rows in solved]
        new_lower, new_upper, new_main, new_right = [], [], [], []
        for k in range(width):
            lo, up, mid, rt = zero, zero, main[k], right[k]
            for j in range(width):
                a = line(lower[k], j)
                b = line(upper[k], j)
                lo = lo - a * back[0][j]
                mid = mid - a * back[1][j] - b * ahead[0][j]
                up = up - b * ahead[1][j]
                rt = rt - a * back[2][j] - b * ahead[2][j]
            new_lower.append(lo)
            new_upper.append(up)
            new_main.append(mid)
            new_right.append(rt)
        lower, upper, main, right = new_lower, new_upper, new_main, new_right
        stride *= 2
    (right,) = eliminate(main, [right])
    mine = zero
    for k in range(width):
        mine = jnp.where(place[0] == k, right[k], mine)
    out[...] = lane_pick(mine, place[2])


def final_kernel(depth, place, got, values, row_a, row_b, news, coarse, out, packs):
    lane = lane_iota()
    sub = sub_iota()
    layers = out.shape[0] // 8
    quarters = layers // 64
    per_tile = 64 // depth
    add = coarse[...]
    even_row = place[2] % 2 == 0
    stride = quarters * 16 + 8
    left = pl.multiple_of(jnp.maximum(place[0] - 1, 0) * stride, 8)
    right = pl.multiple_of(jnp.minimum(place[0] + 1, place[1] - 1) * stride, 8)
    odd = (lane & 1) == 1
    has_left = odd & (place[0] > 0)
    has_right = jnp.logical_not(odd) & (place[0] + 1 < place[1])
    for n in range(quarters * 2):
        low = news[pl.ds(left + n * 8, 8), :]
        high = pltpu.roll(news[pl.ds(right + n * 8, 8), :], 126, 1)
        packs[n * 8 : n * 8 + 8, :] = jnp.where(has_left, low, jnp.where(has_right, high, 0.0))
    ends = (lane == 0) | (lane == 127)

    def some(w, carry):
        for d in range(depth):
            g = w * depth + d
            here = pl.ds(pl.multiple_of(g * 8, 8), 8)
            c = got[pl.ds(pl.multiple_of(w * (depth + 1) * 8 + d * 8, 8), 8), :]
            v = values[here, :]
            quarter = w // per_tile
            shift = 127 - 2 * ((w % per_tile) * depth + d)
            pair = []
            for n, tile in enumerate((c * v, c)):
                at = pl.ds(n * layers + g, 1)
                low = jnp.where(even_row, row_b[at, :], row_a[at, :])
                high = jnp.where(even_row, row_a[at, :], row_b[at, :])
                side = packs[pl.ds(pl.multiple_of((n * quarters + quarter) * 8, 8), 8), :]
                tile = tile + jnp.where(sub == 0, low, jnp.where(sub == 7, high, 0.0))
                tile = tile + jnp.where(ends, pltpu.roll(side, shift, 1), 0.0)
                pair.append(tile)
            out[here, :] = pair[0] / pair[1] + add
        return carry

    lax.fori_loop(0, layers // depth, some, 0)


def partners(array, axis, odd):
    count = lax.axis_size(axis)
    pairs = [(i, i + 1) for i in range(odd, count - 1, 2)]
    return lax.ppermute(array, axis, pairs + [(j, i) for i, j in pairs])


def forward(array, axis):
    count = lax.axis_size(axis)
    return lax.ppermute(array, axis, [(i, i + 1) for i in range(count - 1)])


def shards(saturation, pressure, rock_class, rock_table, well_columns, well_rates, residual):
    depth, rows_all, cols = saturation.shape
    layers, brick_rows, _ = residual.shape
    wide, narrow = lax.axis_size("wide"), lax.axis_size("narrow")
    block = (depth, rows_all, cols)
    plane = (rows_all, cols)
    place = jnp.stack(
        [lax.axis_index("narrow"), jnp.int32(narrow), lax.axis_index("wide")]
    ).astype(jnp.int32)
    vmem = pl.BlockSpec(memory_space=pltpu.VMEM)
    smem = pl.BlockSpec(memory_space=pltpu.SMEM)
    far = pl.BlockSpec(memory_space=pltpu.HBM)

    sat, press, perm, wgain, ogain, frac, face_a, face_b, pack_a, pack_b = call(
        prep_kernel,
        [block] * 6 + [(3,) + plane] * 2 + [plane] * 2,
        scratch=[
            pltpu.VMEM(block, jnp.int32),
            pltpu.VMEM(rock_table.shape, F32),
            pltpu.SemaphoreType.DMA((13,)),
        ],
        in_specs=[smem] + [far] * 4,
        name="prep",
    )(
        place,
        *(
            pltpu.with_memory_space_constraint(array, pltpu.HBM)
            for array in (rock_table, saturation, pressure, rock_class)
        ),
    )
    got_face_a = partners(face_a, "wide", 0)
    got_face_b = partners(face_b, "wide", 1)
    got_pack_a = partners(pack_a, "narrow", 0)
    got_pack_b = partners(pack_b, "narrow", 1)
    net, source, ahead, message = call(
        functools.partial(flow_kernel, narrow),
        [block, plane, plane, (wide * narrow, 128)],
        scratch=[pltpu.VMEM(plane, F32)] * 4,
        in_specs=[smem] + [vmem] * 12,
        name="flow",
    )(
        place, press, perm, frac, got_face_a, got_face_b, pack_a, pack_b, got_pack_a, got_pack_b,
        well_columns.reshape(1, -1), well_rates.reshape(1, -1), residual,
    )
    beside = forward(ahead, "narrow")
    gathered = lax.all_to_all(message, ("wide", "narrow"), 0, 0, tiled=True)
    chunk_rows = wide * (depth + 1) * 8
    sat_new, chunks = call(
        update_kernel,
        [block, (chunk_rows, 128)],
        scratch=[pltpu.VMEM(plane, F32)] * 3,
        in_specs=[smem] + [vmem] * 11,
        name="update",
    )(
        place, gathered, rock_table, sat, net, source, perm, wgain, ogain, got_pack_a, got_pack_b,
        beside,
    )
    got = lax.all_to_all(chunks, "wide", 0, 0, tiled=True)
    message_rows = narrow * (layers // 4 + 8)
    values, row_a, row_b, message = call(
        functools.partial(relax_kernel, depth),
        [(layers * 8 + 64, 128)] + [(2 * layers, 128)] * 2 + [(message_rows, 128)],
        scratch=[pltpu.VMEM((layers * 8 + 64, 128), F32)] * 5,
        in_specs=[smem, vmem, vmem],
        name="relaxation",
    )(place, got, residual.reshape(layers * 8, 128))
    got_row_a = partners(row_a, "wide", 0)
    got_row_b = partners(row_b, "wide", 1)
    news = lax.all_to_all(message, "narrow", 0, 0, tiled=True)
    (coarse,) = call(
        functools.partial(coarse_kernel, wide),
        [(8, 128)],
        in_specs=[smem, vmem, vmem],
        name="coarse",
    )(place, news, gathered)
    (precond,) = call(
        functools.partial(final_kernel, depth),
        [(layers * 8, 128)],
        scratch=[pltpu.VMEM((layers // 4, 128), F32)],
        in_specs=[smem] + [vmem] * 6,
        name="final",
    )(place, got, values, got_row_a, got_row_b, news, coarse)
    return (sat_new, precond.reshape(layers, brick_rows, cols))


def solution(mesh):
    placed = (
        P("wide", None, "narrow"),
        P("wide", None, "narrow"),
        P("wide", None, "narrow"),
        P(),
        P(),
        P(),
        P(None, "wide", "narrow"),
    )
    return jax.shard_map(
        shards,
        mesh=mesh,
        in_specs=placed,
        out_specs=(P("wide", None, "narrow"), P(None, "wide", "narrow")),
        check_vma=False,
    )
```

```python
import functools

import jax
import jax.numpy as jnp
from jax import lax
from jax.experimental import pallas as pl
from jax.experimental.pallas import tpu as pltpu
from jax.sharding import PartitionSpec as P

SWEEPS = 6
compress = 0.05
relax = 0.8
gravity = 0.5
courant = 0.5
tiny = 1e-06

F32 = jnp.float32
HIGH = lax.Precision.HIGHEST
PARAMS = pltpu.CompilerParams(vmem_limit_bytes=16 * 1024 * 1024)


def harmonic(low, high):
    return 2.0 * low * high / (low + high)


def sub_iota():
    return lax.broadcasted_iota(jnp.int32, (8, 128), 0)


def lane_iota():
    return lax.broadcasted_iota(jnp.int32, (8, 128), 1)


def lane_pick(tile, index):
    return jnp.take_along_axis(tile, jnp.full((8, 128), index, jnp.int32), axis=1)


def lane_take(tile, index):
    return jnp.take_along_axis(tile, index, axis=1, mode="promise_in_bounds")


def mobility(wg, og, s):
    water = wg * s * s
    return water, water + og * (1.0 - s) * (1.0 - s)


def lane_table(table, n):
    row = jnp.concatenate([table[n : n + 1, :], jnp.zeros((1, 112), F32)], axis=1)
    return jnp.broadcast_to(row, (8, 128))


def spread(tile, lane):
    return jnp.broadcast_to(tile[:, lane : lane + 1], (8, 128))


def call(kernel, outs, scratch=(), aliases=None, out_specs=None, in_specs=None, name=None):
    def run(*args):
        return pl.pallas_call(
            kernel,
            out_shape=[jax.ShapeDtypeStruct(shape, F32) for shape in outs],
            in_specs=in_specs or [pl.BlockSpec(memory_space=pltpu.VMEM)] * len(args),
            out_specs=out_specs or [pl.BlockSpec(memory_space=pltpu.VMEM)] * len(outs),
            scratch_shapes=list(scratch),
            input_output_aliases=aliases or {},
            compiler_params=PARAMS,
            name=name,
        )(*args)

    return run


def prep_kernel(
    place, table_in, sat_in, press_in, rock_in, sat, press, perm, wgain, ogain, frac,
    face_a, face_b, pack_a, pack_b, rock, table, sem,
):
    lane = lane_iota()
    depth, rows_all, _ = sat.shape
    groups = 4
    each = rows_all // groups
    small = pltpu.make_async_copy(table_in, table, sem.at[groups * 3])
    small.start()
    copies = []
    for g in range(groups):
        part = pl.ds(g * each, each)
        for n, (src, dst) in enumerate(((rock_in, rock), (sat_in, sat), (press_in, press))):
            copies.append(
                pltpu.make_async_copy(src.at[:, part, :], dst.at[:, part, :], sem.at[g * 3 + n])
            )
            copies[-1].start()
    small.wait()
    tables = [lane_table(table, n) for n in range(3)]
    entries = [jnp.broadcast_to(table[2:3, m : m + 1], (8, 128)) for m in range(16)]

    def tree(kind):
        values = entries
        for bit in range(4):
            taken = (kind & (1 << bit)) != 0
            values = [jnp.where(taken, values[m + 1], values[m]) for m in range(0, len(values), 2)]
        return values[0]

    def complete(pack):
        kind = jnp.where(lane < depth, pack, 0.0).astype(jnp.int32)
        k, wg, og = [lane_take(t, kind) for t in tables]
        water, both = mobility(wg, og, pltpu.roll(pack, 128 - depth, 1))
        tile = jnp.where(lane < 3 * depth, pack, pltpu.roll(k, 3 * depth, 1))
        return jnp.where(lane < 4 * depth, tile, pltpu.roll(water / both, 4 * depth, 1))

    even_row = place[2] % 2 == 0
    even_col = place[0] % 2 == 0

    def rows(step, carry):
        at = pl.ds(pl.multiple_of(step * 8, 8), 8)
        first = jnp.zeros((8, 128), F32)
        last = jnp.zeros((8, 128), F32)
        for d in range(depth):
            kind = rock[d, at, :]
            k = lane_take(tables[0], kind)
            wg = lane_take(tables[1], kind)
            og = tree(kind)
            s = sat[d, at, :]
            p = press[d, at, :]
            water, both = mobility(wg, og, s)
            f = water / both
            perm[d, at, :] = k
            wgain[d, at, :] = wg
            ogain[d, at, :] = og
            frac[d, at, :] = f
            for n, field in enumerate((kind.astype(F32), s, p)):
                spot = n * depth + d
                turned = pltpu.roll(field, spot + 1, 1)
                first = jnp.where(lane == spot + 1, turned, first)
                last = jnp.where(lane == spot, turned, last)
        pack_a[at, :] = last
        pack_b[at, :] = first
        for n, ref in enumerate((press, perm, frac)):
            low, high = ref[0, at, :], ref[depth - 1, at, :]
            face_a[n, at, :] = jnp.where(even_row, high, low)
            face_b[n, at, :] = jnp.where(even_row, low, high)
        return carry

    def two_rows(step, carry):
        return rows(2 * step + 1, rows(2 * step, carry))

    for g in range(groups):
        for copy in copies[g * 3 : g * 3 + 3]:
            copy.wait()
        lax.fori_loop(g * (each // 16), (g + 1) * (each // 16), two_rows, 0)

    def finish(step, carry):
        for n in range(4):
            at = pl.ds(pl.multiple_of(step * 32 + n * 8, 8), 8)
            last = complete(pack_a[at, :])
            first = complete(pltpu.roll(pack_b[at, :], 127, 1))
            pack_a[at, :] = jnp.where(even_col, last, first)
            pack_b[at, :] = jnp.where(even_col, first, last)
        return carry

    lax.fori_loop(0, rows_all // 32, finish, 0)


def flows(low, high, lift):
    total = low[1] * high[1] / (low[1] + high[1]) * (low[0] - high[0] + lift)
    return total, total * jnp.where(total > 0, low[2], high[2])


def flow_kernel(
    bricks, place, press, perm, frac, face_a, face_b, pack_a, pack_b, got_a, got_b,
    columns, rates, residual, net, source, ahead, message, qp, wp, rq, rw,
):
    lane = lane_iota()
    sub = sub_iota()
    depth, rows_all, cols = perm.shape
    tiles = rows_all // 8
    even_row = place[2] % 2 == 0
    even_col = place[0] % 2 == 0
    half = lane >> 1
    odd = (lane & 1) == 1

    wells = columns.shape[1]
    spot = lax.broadcasted_iota(jnp.int32, (rows_all, wells), 0)
    apart = columns[...] - spot * (cols * bricks)
    in_row = jnp.where((apart >= 0) & (apart < cols * bricks), 1.0, 0.0)
    number = columns[...]
    well_col = number & (cols * bricks - 1) if (cols * bricks) & (cols * bricks - 1) == 0 else number % (cols * bricks)
    spot = lax.broadcasted_iota(jnp.int32, (cols, wells), 0)
    in_col = jnp.where(well_col - place[0] * cols == spot, rates[...], 0.0)
    source[...] = lax.dot_general(
        in_row, in_col, (((1,), (1,)), ((), ())), precision=HIGH, preferred_element_type=F32
    )

    def edge(step, carry):
        at = pl.ds(pl.multiple_of(step * 8, 8), 8)

        def fields(tile):
            return [pltpu.roll(tile, 128 - n * depth, 1) for n in (2, 3, 4)]

        mine_a, mine_b = pack_a[at, :], pack_b[at, :]
        other_a, other_b = got_a[at, :], got_b[at, :]
        left = flows(
            fields(jnp.where(even_col, other_b, other_a)),
            fields(jnp.where(even_col, mine_b, mine_a)),
            0.0,
        )
        right = flows(
            fields(jnp.where(even_col, mine_a, mine_b)),
            fields(jnp.where(even_col, other_a, other_b)),
            0.0,
        )
        for out, low, high in zip((qp, wp), left, right):
            out[at, :] = jnp.where(
                odd,
                jnp.take_along_axis(low, half, axis=1),
                jnp.take_along_axis(high, half, axis=1),
            )
        return carry

    lax.fori_loop(0, tiles, edge, 0)
    rq[...] = jnp.zeros(rq.shape, F32)
    rw[...] = jnp.zeros(rw.shape, F32)

    def rows(step, top):
        begin = pl.multiple_of(step * 8, 8)
        at = pl.ds(begin, 8)
        beyond = pl.ds(pl.multiple_of(jnp.minimum(begin + 8, rows_all - 8), 8), 8)
        outer = (sub == 7) & (step == tiles - 1)
        edge_q, edge_w = qp[at, :], wp[at, :]
        below = [jnp.where(even_row, face_b[n, at, :], face_a[n, at, :]) for n in range(3)]
        above = [jnp.where(even_row, face_a[n, at, :], face_b[n, at, :]) for n in range(3)]
        cur = [ref[0, at, :] for ref in (press, perm, frac)]
        depth_q, depth_w = flows(below, cur, gravity)
        told = jnp.where(
            (lane >= depth) & (lane < 2 * depth), spread(source[at, :], 127), 0.0
        )
        for d in range(depth):
            nxt = [ref[d + 1, at, :] for ref in (press, perm, frac)] if d + 1 < depth else above
            q, w = flows(cur, nxt, gravity)
            net_sum = w - depth_w
            out = jnp.maximum(q, 0.0) - jnp.minimum(depth_q, 0.0)
            depth_q, depth_w = q, w
            up = [
                pltpu.roll(jnp.where(sub == 0, ref[d, beyond, :], x), 7, 0)
                for ref, x in zip((press, perm, frac), cur)
            ]
            q, w = flows(cur, up, 0.0)
            q = jnp.where(outer, 0.0, q)
            w = jnp.where(outer, 0.0, w)
            q_roll, w_roll = pltpu.roll(q, 1, 0), pltpu.roll(w, 1, 0)
            low_q = jnp.where(sub == 0, rq[d], q_roll)
            low_w = jnp.where(sub == 0, rw[d], w_roll)
            rq[d] = q_roll
            rw[d] = w_roll
            net_sum = net_sum + (w - low_w)
            out = out + (jnp.maximum(q, 0.0) - jnp.minimum(low_q, 0.0))
            q, w = flows(cur, [pltpu.roll(x, 127, 1) for x in cur], 0.0)
            side_q = pltpu.roll(edge_q, 127 - 2 * d, 1)
            side_w = pltpu.roll(edge_w, 127 - 2 * d, 1)
            low_q = jnp.where(lane == 0, side_q, pltpu.roll(q, 1, 1))
            low_w = jnp.where(lane == 0, side_w, pltpu.roll(w, 1, 1))
            q = jnp.where(lane == 127, side_q, q)
            w = jnp.where(lane == 127, side_w, w)
            net_sum = 2.0 * (net_sum + (w - low_w))
            net[d, at, :] = net_sum
            told = jnp.where(lane == d, pltpu.roll(net_sum, d + 1, 1), told)
            out = out + (jnp.maximum(q, 0.0) - jnp.minimum(low_q, 0.0))
            top = jnp.maximum(top, out)
            cur = nxt
        ahead[at, :] = told
        return top

    top = lax.fori_loop(0, tiles, rows, jnp.zeros((8, 128), F32))

    def add(step, sums):
        at = step * 8
        return tuple(s + residual[at + n] for n, s in enumerate(sums))

    sums = lax.fori_loop(0, residual.shape[0] // 8, add, (jnp.zeros((8, 128), F32),) * 8)
    total = sum(sums[1:], sums[0])
    message[...] = jnp.where(
        lax.broadcasted_iota(jnp.int32, message.shape, 1) == 0,
        2.0 * jnp.max(top),
        jnp.sum(total),
    )


def update_kernel(
    place, gathered, table, sat, net, source, perm, wgain, ogain, got_a, got_b, beside,
    new, chunks, cell_sum, row_sum, col_sum,
):
    lane = lane_iota()
    depth, rows_all, _ = sat.shape
    tiles = rows_all // 8
    stride = (depth + 1) * 8
    spot = lax.broadcasted_iota(jnp.int32, gathered.shape, 1)
    top = jnp.max(jnp.where(spot == 0, gathered[...], 0.0), keepdims=True)
    step_size = jnp.broadcast_to(courant / (top + tiny), (8, 128))
    even_col = place[0] % 2 == 0
    water_table, oil_table = lane_table(table, 1), lane_table(table, 2)

    def coefficient(k, wg, og, s):
        return k * (wg * s * s + og * (1.0 - s) * (1.0 - s))

    def rows(step, carry):
        at = pl.ds(pl.multiple_of(step * 8, 8), 8)
        begin = step * stride
        add = step_size * source[at, :]
        total = jnp.zeros((8, 128), F32)
        first = jnp.zeros((8, 128), F32)
        for d in range(depth):
            s = sat[d, at, :] - step_size * net[d, at, :] + add
            new[d, at, :] = s
            c = coefficient(perm[d, at, :], wgain[d, at, :], ogain[d, at, :], s)
            chunks[pl.ds(pl.multiple_of(begin + d * 8, 8), 8), :] = c
            total = total + c
            first = jnp.where(lane == d, pltpu.roll(c, d, 1) if d else c, first)
        cell_sum[at, :] = total
        tile = jnp.where(even_col, got_b[at, :], got_a[at, :])
        flow = beside[at, :]
        kind = jnp.where(lane < depth, tile, 0.0).astype(jnp.int32)
        s = pltpu.roll(tile, 128 - depth, 1) - step_size * flow
        s = s + step_size * pltpu.roll(flow, 128 - depth, 1)
        c = coefficient(
            pltpu.roll(tile, 128 - 3 * depth, 1),
            lane_take(water_table, kind),
            lane_take(oil_table, kind),
            s,
        )
        col_sum[at, :] = jnp.where(lane < depth, harmonic(c, first), 0.0)
        return carry

    def two_rows(step, carry):
        return rows(2 * step + 1, rows(2 * step, carry))

    lax.fori_loop(0, tiles // 2, two_rows, 0)
    row_sum[0:8, :] = jnp.zeros((8, 128), F32)
    for p in range(1, tiles):
        total = jnp.zeros((8, 128), F32)
        for half in range(depth // 8):
            low = chunks[pl.ds((p - 1) * stride + half * 64 + 7, 8, stride=8), :]
            high = chunks[pl.ds(p * stride + half * 64, 8, stride=8), :]
            total = total + harmonic(low, high)
        row_sum[p * 8 : p * 8 + 8, :] = total
    brick = lax.broadcasted_iota(jnp.int32, (rows_all, 128), 0) // 8
    spot = lax.broadcasted_iota(jnp.int32, (rows_all, 128), 1)
    total = jnp.zeros((1, 128), F32)
    for n, part in enumerate((cell_sum, row_sum, col_sum)):
        each = jnp.sum(part[...], axis=1, keepdims=True)
        placed = jnp.where(spot == n * 16 + brick, each, 0.0)
        total = total + jnp.sum(placed, axis=0, keepdims=True)
    for p in range(tiles):
        chunks[p * stride + depth * 8 : (p + 1) * stride, :] = jnp.broadcast_to(total, (8, 128))


def relax_kernel(depth, place, got, residual, values, row_a, row_b, message, fd, fr, fc, gain, base):
    lane = lane_iota()
    sub = sub_iota()
    layers = residual.shape[0] // 8
    parts = layers // depth
    zero = jnp.zeros((8, 128), F32)
    fd[0:8, :] = zero
    values[layers * 8 :, :] = jnp.zeros((64, 128), F32)
    fc[layers * 8 :, :] = jnp.zeros((64, 128), F32)
    even_row = place[2] % 2 == 0

    def half_face(low, high):
        return low * high / (low + high)

    def part(w, carry):
        below, total = carry
        begin = w * (depth + 1) * 8
        place_w = w * depth * 8
        after = jnp.minimum(w + 1, parts - 1) * (depth + 1) * 8
        c = got[pl.ds(pl.multiple_of(begin, 8), 8), :]
        for d in range(depth):
            here = pl.ds(pl.multiple_of(place_w + d * 8, 8), 8)
            if d + 1 < depth:
                c_next = got[pl.ds(pl.multiple_of(begin + d * 8 + 8, 8), 8), :]
                above = half_face(c, c_next)
            else:
                c_next = got[pl.ds(pl.multiple_of(after, 8), 8), :]
                above = jnp.where(w + 1 < parts, half_face(c, c_next), 0.0)
            row = jnp.where(sub == 0, 0.0, half_face(pltpu.roll(c, 1, 0), c))
            col = jnp.where(lane == 0, 0.0, half_face(pltpu.roll(c, 1, 1), c))
            diag = (
                (0.5 * compress) * c + below + above
                + row + pltpu.roll(row, 7, 0) + col + pltpu.roll(col, 127, 1)
            )
            scale = relax / diag
            fd[pl.ds(pl.multiple_of(place_w + d * 8 + 8, 8), 8), :] = above
            fr[here, :] = row
            fc[here, :] = col
            gain[here, :] = scale
            first = (0.5 * scale) * residual[here, :]
            base[here, :] = first
            values[here, :] = first
            c, below = c_next, above
        total = total + got[pl.ds(pl.multiple_of(begin + depth * 8, 8), 8), :]
        return below, total

    def build(step, carry):
        return part(2 * step + 1, part(2 * step, carry))

    _, total = lax.fori_loop(0, parts // 2, build, (zero, zero))

    block = 32

    def sweep(number, carry):
        def some(step, prev):
            begin = step * (block * 8)
            v = values[pl.ds(pl.multiple_of(begin, 8), 8), :]
            for n in range(block):
                here = pl.ds(pl.multiple_of(begin + n * 8, 8), 8)
                above = pl.ds(pl.multiple_of(begin + n * 8 + 8, 8), 8)
                v_next = values[above, :]
                row = fr[here, :]
                col = fc[here, :]
                total = fd[here, :] * prev + fd[above, :] * v_next
                total = total + (row * pltpu.roll(v, 1, 0) + pltpu.roll(row * v, 7, 0))
                total = total + (col * pltpu.roll(v, 1, 1) + pltpu.roll(col * v, 127, 1))
                values[here, :] = ((1.0 - relax) * v + base[here, :]) + gain[here, :] * total
                prev, v = v, v_next
            return prev

        lax.fori_loop(0, layers // block, some, zero)
        return carry

    lax.fori_loop(0, SWEEPS - 1, sweep, 0)

    for w in range(parts):
        for half in range(depth // 8):
            at = w * (depth + 1) * 8 + half * 64
            spot = w * depth + half * 8
            pairs = []
            for row in (0, 7):
                c = got[pl.ds(at + row, 8, stride=8), :]
                v = values[pl.ds(spot * 8 + row, 8, stride=8), :]
                pairs.append((c * v, c))
            for n in range(2):
                low, high = pairs[0][n], pairs[1][n]
                rows = slice(n * layers + spot, n * layers + spot + 8)
                row_a[rows, :] = jnp.where(even_row, high, low)
                row_b[rows, :] = jnp.where(even_row, low, high)

    quarters = layers // 64
    per_tile = 64 // depth
    peers = message.shape[0] // (quarters * 16 + 8)

    def pack(quarter, carry):
        packed = [zero, zero]
        for l in range(64):
            part = quarter * per_tile + l // depth
            c = got[pl.ds(pl.multiple_of(part * (depth + 1) * 8 + l % depth * 8, 8), 8), :]
            v = values[pl.ds(pl.multiple_of(quarter * 512 + l * 8, 8), 8), :]
            spot = (2 * l + 2) % 128
            mark = (lane == 2 * l + 1) | (lane == spot)
            for n, tile in enumerate((c * v, c)):
                turned = pltpu.roll(tile, spot, 1) if spot else tile
                packed[n] = jnp.where(mark, turned, packed[n])
        for peer in range(peers):
            for n in range(2):
                begin = peer * (quarters * 16 + 8) + (n * quarters + quarter) * 8
                message[pl.ds(pl.multiple_of(begin, 8), 8), :] = packed[n]
        return carry

    lax.fori_loop(0, quarters, pack, 0)
    for peer in range(peers):
        begin = peer * (quarters * 16 + 8) + quarters * 16
        message[begin : begin + 8, :] = total


def coarse_kernel(count, place, news, gathered, out):
    lane = lane_iota()
    sub = sub_iota()
    inside = lane < count
    width = gathered.shape[0] // count
    stride = news.shape[0] // width
    sums = jnp.zeros((8, 128), F32)
    for k in range(width):
        sums = jnp.where(sub == k, news[(k + 1) * stride - 8 : (k + 1) * stride, :], sums)
    cells = jnp.where(inside, sums, 0.0)
    low_row = jnp.where(inside, pltpu.roll(sums, 128 - 16, 1), 0.0)
    low_col = jnp.where(inside, pltpu.roll(sums, 128 - 32, 1), 0.0)
    low_row = jnp.where(lane == 0, 0.0, low_row)
    low_col = jnp.where(sub == 0, 0.0, low_col)
    high_row = pltpu.roll(low_row, 127, 1)
    high_col = pltpu.roll(low_col, 7, 0)
    diagonal = jnp.where(inside, compress * cells + low_row + high_row + low_col + high_col, 1.0)
    rhs = jnp.zeros((8, 128), F32)
    for p in range(count):
        rhs = jnp.where(lane == p, spread(gathered[p * width : p * width + width, :], 1), rhs)

    def line(tile, k):
        return jnp.broadcast_to(tile[k : k + 1, :], (8, 128))

    zero = jnp.zeros((8, 128), F32)
    main, lower, upper, right = [], [], [], []
    for k in range(width):
        row = jnp.where(sub == k, line(diagonal, k), zero)
        if k > 0:
            row = jnp.where(sub == k - 1, -line(low_col, k), row)
        if k + 1 < width:
            row = jnp.where(sub == k + 1, -line(low_col, k + 1), row)
        main.append(row)
        lower.append(jnp.where(sub == k, -line(low_row, k), zero))
        upper.append(jnp.where(sub == k, -line(high_row, k), zero))
        right.append(line(rhs, k))

    def eliminate(main, others):
        main = list(main)
        others = [list(rows) for rows in others]
        for k in range(width):
            inverse = 1.0 / line(main[k], k)
            main[k] = main[k] * inverse
            for rows in others:
                rows[k] = rows[k] * inverse
            for j in range(width):
                if j != k:
                    factor = line(main[j], k)
                    main[j] = main[j] - factor * main[k]
                    for rows in others:
                        rows[j] = rows[j] - factor * rows[k]
        return others

    stride = 1
    while stride < count:
        solved = eliminate(main, [lower, upper, right])
        back = [[pltpu.roll(x, stride, 1) for x in rows] for rows in solved]
        ahead = [[pltpu.roll(x, 128 - stride, 1) for x in rows] for rows in solved]
        new_lower, new_upper, new_main, new_right = [], [], [], []
        for k in range(width):
            lo, up, mid, rt = zero, zero, main[k], right[k]
            for j in range(width):
                a = line(lower[k], j)
                b = line(upper[k], j)
                lo = lo - a * back[0][j]
                mid = mid - a * back[1][j] - b * ahead[0][j]
                up = up - b * ahead[1][j]
                rt = rt - a * back[2][j] - b * ahead[2][j]
            new_lower.append(lo)
            new_upper.append(up)
            new_main.append(mid)
            new_right.append(rt)
        lower, upper, main, right = new_lower, new_upper, new_main, new_right
        stride *= 2
    (right,) = eliminate(main, [right])
    mine = zero
    for k in range(width):
        mine = jnp.where(place[0] == k, right[k], mine)
    out[...] = lane_pick(mine, place[2])


def final_kernel(depth, place, got, values, row_a, row_b, news, coarse, out, packs):
    lane = lane_iota()
    sub = sub_iota()
    layers = out.shape[0] // 8
    quarters = layers // 64
    per_tile = 64 // depth
    add = coarse[...]
    even_row = place[2] % 2 == 0
    stride = quarters * 16 + 8
    left = pl.multiple_of(jnp.maximum(place[0] - 1, 0) * stride, 8)
    right = pl.multiple_of(jnp.minimum(place[0] + 1, place[1] - 1) * stride, 8)
    odd = (lane & 1) == 1
    has_left = odd & (place[0] > 0)
    has_right = jnp.logical_not(odd) & (place[0] + 1 < place[1])
    for n in range(quarters * 2):
        low = news[pl.ds(left + n * 8, 8), :]
        high = pltpu.roll(news[pl.ds(right + n * 8, 8), :], 126, 1)
        packs[n * 8 : n * 8 + 8, :] = jnp.where(has_left, low, jnp.where(has_right, high, 0.0))
    ends = (lane == 0) | (lane == 127)

    def some(quarter, carry):
        sides = [
            packs[pl.ds(pl.multiple_of((n * quarters + quarter) * 8, 8), 8), :] for n in range(2)
        ]
        for l in range(64):
            g = quarter * 64 + l
            part = quarter * per_tile + l // depth
            here = pl.ds(pl.multiple_of(g * 8, 8), 8)
            c = got[pl.ds(pl.multiple_of(part * (depth + 1) * 8 + l % depth * 8, 8), 8), :]
            v = values[here, :]
            pair = []
            for n, tile in enumerate((c * v, c)):
                at = pl.ds(n * layers + g, 1)
                low = jnp.where(even_row, row_b[at, :], row_a[at, :])
                high = jnp.where(even_row, row_a[at, :], row_b[at, :])
                tile = tile + jnp.where(sub == 0, low, jnp.where(sub == 7, high, 0.0))
                tile = tile + jnp.where(ends, pltpu.roll(sides[n], 127 - 2 * l, 1), 0.0)
                pair.append(tile)
            out[here, :] = pair[0] / pair[1] + add
        return carry

    lax.fori_loop(0, quarters, some, 0)


def partners(array, axis, odd):
    count = lax.axis_size(axis)
    pairs = [(i, i + 1) for i in range(odd, count - 1, 2)]
    return lax.ppermute(array, axis, pairs + [(j, i) for i, j in pairs])


def forward(array, axis):
    count = lax.axis_size(axis)
    return lax.ppermute(array, axis, [(i, i + 1) for i in range(count - 1)])


def shards(saturation, pressure, rock_class, rock_table, well_columns, well_rates, residual):
    depth, rows_all, cols = saturation.shape
    layers, brick_rows, _ = residual.shape
    wide, narrow = lax.axis_size("wide"), lax.axis_size("narrow")
    block = (depth, rows_all, cols)
    plane = (rows_all, cols)
    place = jnp.stack(
        [lax.axis_index("narrow"), jnp.int32(narrow), lax.axis_index("wide")]
    ).astype(jnp.int32)
    vmem = pl.BlockSpec(memory_space=pltpu.VMEM)
    smem = pl.BlockSpec(memory_space=pltpu.SMEM)
    far = pl.BlockSpec(memory_space=pltpu.HBM)

    sat, press, perm, wgain, ogain, frac, face_a, face_b, pack_a, pack_b = call(
        prep_kernel,
        [block] * 6 + [(3,) + plane] * 2 + [plane] * 2,
        scratch=[
            pltpu.VMEM(block, jnp.int32),
            pltpu.VMEM(rock_table.shape, F32),
            pltpu.SemaphoreType.DMA((13,)),
        ],
        in_specs=[smem] + [far] * 4,
        name="prep",
    )(
        place,
        *(
            pltpu.with_memory_space_constraint(array, pltpu.HBM)
            for array in (rock_table, saturation, pressure, rock_class)
        ),
    )
    got_face_a = partners(face_a, "wide", 0)
    got_face_b = partners(face_b, "wide", 1)
    got_pack_a = partners(pack_a, "narrow", 0)
    got_pack_b = partners(pack_b, "narrow", 1)
    net, source, ahead, message = call(
        functools.partial(flow_kernel, narrow),
        [block, plane, plane, (wide * narrow, 128)],
        scratch=[pltpu.VMEM(plane, F32)] * 2 + [pltpu.VMEM((depth, 8, cols), F32)] * 2,
        in_specs=[smem] + [vmem] * 12,
        name="flow",
    )(
        place, press, perm, frac, got_face_a, got_face_b, pack_a, pack_b, got_pack_a, got_pack_b,
        well_columns.reshape(1, -1), well_rates.reshape(1, -1), residual,
    )
    beside = forward(ahead, "narrow")
    gathered = lax.all_to_all(message, ("wide", "narrow"), 0, 0, tiled=True)
    chunk_rows = wide * (depth + 1) * 8
    sat_new, chunks = call(
        update_kernel,
        [block, (chunk_rows, 128)],
        scratch=[pltpu.VMEM(plane, F32)] * 3,
        in_specs=[smem] + [vmem] * 11,
        name="update",
    )(
        place, gathered, rock_table, sat, net, source, perm, wgain, ogain, got_pack_a, got_pack_b,
        beside,
    )
    got = lax.all_to_all(chunks, "wide", 0, 0, tiled=True)
    message_rows = narrow * (layers // 4 + 8)
    values, row_a, row_b, message = call(
        functools.partial(relax_kernel, depth),
        [(layers * 8 + 64, 128)] + [(2 * layers, 128)] * 2 + [(message_rows, 128)],
        scratch=[pltpu.VMEM((layers * 8 + 64, 128), F32)] * 5,
        in_specs=[smem, vmem, vmem],
        name="relaxation",
    )(place, got, residual.reshape(layers * 8, 128))
    got_row_a = partners(row_a, "wide", 0)
    got_row_b = partners(row_b, "wide", 1)
    news = lax.all_to_all(message, "narrow", 0, 0, tiled=True)
    (coarse,) = call(
        functools.partial(coarse_kernel, wide),
        [(8, 128)],
        in_specs=[smem, vmem, vmem],
        name="coarse",
    )(place, news, gathered)
    (precond,) = call(
        functools.partial(final_kernel, depth),
        [(layers * 8, 128)],
        scratch=[pltpu.VMEM((layers // 4, 128), F32)],
        in_specs=[smem] + [vmem] * 6,
        name="final",
    )(place, got, values, got_row_a, got_row_b, news, coarse)
    return (sat_new, precond.reshape(layers, brick_rows, cols))


def solution(mesh):
    placed = (
        P("wide", None, "narrow"),
        P("wide", None, "narrow"),
        P("wide", None, "narrow"),
        P(),
        P(),
        P(),
        P(None, "wide", "narrow"),
    )
    return jax.shard_map(
        shards,
        mesh=mesh,
        in_specs=placed,
        out_specs=(P("wide", None, "narrow"), P(None, "wide", "narrow")),
        check_vma=False,
    )
```

```python
import functools

import jax
import jax.numpy as jnp
from jax import lax
from jax.experimental import pallas as pl
from jax.experimental.pallas import tpu as pltpu
from jax.sharding import PartitionSpec as P

SWEEPS = 6
compress = 0.05
relax = 0.8
gravity = 0.5
courant = 0.5
tiny = 1e-06

F32 = jnp.float32
HIGH = lax.Precision.HIGHEST
PARAMS = pltpu.CompilerParams(vmem_limit_bytes=16 * 1024 * 1024)


def harmonic(low, high):
    return 2.0 * low * high / (low + high)


def sub_iota():
    return lax.broadcasted_iota(jnp.int32, (8, 128), 0)


def lane_iota():
    return lax.broadcasted_iota(jnp.int32, (8, 128), 1)


def lane_pick(tile, index):
    return jnp.take_along_axis(tile, jnp.full((8, 128), index, jnp.int32), axis=1)


def lane_take(tile, index):
    return jnp.take_along_axis(tile, index, axis=1, mode="promise_in_bounds")


def mobility(wg, og, s):
    water = wg * s * s
    return water, water + og * (1.0 - s) * (1.0 - s)


def lane_table(table, n):
    row = jnp.concatenate([table[n : n + 1, :], jnp.zeros((1, 112), F32)], axis=1)
    return jnp.broadcast_to(row, (8, 128))


def spread(tile, lane):
    return jnp.broadcast_to(tile[:, lane : lane + 1], (8, 128))


def call(kernel, outs, scratch=(), aliases=None, out_specs=None, in_specs=None, name=None):
    def run(*args):
        return pl.pallas_call(
            kernel,
            out_shape=[jax.ShapeDtypeStruct(shape, F32) for shape in outs],
            in_specs=in_specs or [pl.BlockSpec(memory_space=pltpu.VMEM)] * len(args),
            out_specs=out_specs or [pl.BlockSpec(memory_space=pltpu.VMEM)] * len(outs),
            scratch_shapes=list(scratch),
            input_output_aliases=aliases or {},
            compiler_params=PARAMS,
            name=name,
        )(*args)

    return run


def faces_kernel(
    place, sat_in, press_in, rock_in, sat, press, kinds, face_a, face_b, pack_a, pack_b, rock, sem
):
    lane = lane_iota()
    depth, rows_all, _ = sat.shape
    groups = 4
    each = rows_all // groups
    copies = []
    for g in range(groups):
        part = pl.ds(g * each, each)
        for n, (src, dst) in enumerate(((rock_in, rock), (sat_in, sat), (press_in, press))):
            copies.append(
                pltpu.make_async_copy(src.at[:, part, :], dst.at[:, part, :], sem.at[g * 3 + n])
            )
            copies[-1].start()
    even_row = place[2] % 2 == 0
    even_col = place[0] % 2 == 0

    def rows(step, carry):
        at = pl.ds(pl.multiple_of(step * 8, 8), 8)
        first = jnp.zeros((8, 128), F32)
        last = jnp.zeros((8, 128), F32)
        for d in range(depth):
            kind = rock[d, at, :].astype(F32) + 1.0
            kinds[d, at, :] = kind
            fields = (kind, sat[d, at, :], press[d, at, :])
            for n, field in enumerate(fields):
                spot = n * depth + d
                turned = pltpu.roll(field, spot + 1, 1)
                first = jnp.where(lane == spot + 1, turned, first)
                last = jnp.where(lane == spot, turned, last)
                if d == 0:
                    face_a[n, at, :] = field
                if d + 1 == depth:
                    low = face_a[n, at, :]
                    face_a[n, at, :] = jnp.where(even_row, field, low)
                    face_b[n, at, :] = jnp.where(even_row, low, field)
        first = pltpu.roll(first, 127, 1)
        pack_a[at, :] = jnp.where(even_col, last, first)
        pack_b[at, :] = jnp.where(even_col, first, last)
        return carry

    def two_rows(step, carry):
        return rows(2 * step + 1, rows(2 * step, carry))

    for g in range(groups):
        for copy in copies[g * 3 : g * 3 + 3]:
            copy.wait()
        lax.fori_loop(g * (each // 16), (g + 1) * (each // 16), two_rows, 0)


def rock_of(tables, kind, s):
    index = jnp.maximum(kind.astype(jnp.int32) - 1, 0)
    k, wg, og = [lane_take(table, index) for table in tables]
    water, both = mobility(wg, og, s)
    return jnp.where(kind > 0.5, k, 0.0), water / both


def columns_of(tables, depth, pack):
    lane = lane_iota()
    kind = jnp.where(lane < depth, pack, 0.0)
    k, f = rock_of(tables, kind, pltpu.roll(pack, 128 - depth, 1))
    return [pltpu.roll(pack, 128 - 2 * depth, 1), k, f]


def lookup_kernel(table, kinds, sat, perm, wgain, ogain, frac):
    depth, rows_all, _ = sat.shape
    tables = [lane_table(table, n) for n in range(2)]
    entries = [jnp.broadcast_to(table[2:3, m : m + 1], (8, 128)) for m in range(16)]

    def rows(step, carry):
        at = pl.ds(pl.multiple_of(step * 8, 8), 8)
        for d in range(depth):
            kind = kinds[d, at, :].astype(jnp.int32) - 1
            k = lane_take(tables[0], kind)
            wg = lane_take(tables[1], kind)
            values = entries
            for bit in range(4):
                taken = (kind & (1 << bit)) != 0
                values = [
                    jnp.where(taken, values[m + 1], values[m]) for m in range(0, len(values), 2)
                ]
            og = values[0]
            water, both = mobility(wg, og, sat[d, at, :])
            perm[d, at, :] = k
            wgain[d, at, :] = wg
            ogain[d, at, :] = og
            frac[d, at, :] = water / both
        return carry

    lax.fori_loop(0, rows_all // 8, rows, 0)


def flows(low, high, lift):
    total = low[1] * high[1] / (low[1] + high[1]) * (low[0] - high[0] + lift)
    return total, total * jnp.where(total > 0, low[2], high[2])


def flow_kernel(
    bricks, place, table, press, perm, frac, face_a, face_b, pack_a, pack_b, got_a, got_b,
    columns, rates, residual, net, source, ahead, message, qp, wp, rq, rw,
):
    lane = lane_iota()
    sub = sub_iota()
    depth, rows_all, cols = perm.shape
    tiles = rows_all // 8
    even_row = place[2] % 2 == 0
    even_col = place[0] % 2 == 0
    half = lane >> 1
    odd = (lane & 1) == 1
    tables = [lane_table(table, n) for n in range(3)]

    wells = columns.shape[1]
    spot = lax.broadcasted_iota(jnp.int32, (rows_all, wells), 0)
    apart = columns[...] - spot * (cols * bricks)
    in_row = jnp.where((apart >= 0) & (apart < cols * bricks), 1.0, 0.0)
    number = columns[...]
    well_col = number & (cols * bricks - 1) if (cols * bricks) & (cols * bricks - 1) == 0 else number % (cols * bricks)
    spot = lax.broadcasted_iota(jnp.int32, (cols, wells), 0)
    in_col = jnp.where(well_col - place[0] * cols == spot, rates[...], 0.0)
    source[...] = lax.dot_general(
        in_row, in_col, (((1,), (1,)), ((), ())), precision=HIGH, preferred_element_type=F32
    )

    def edge(step, carry):
        at = pl.ds(pl.multiple_of(step * 8, 8), 8)

        mine_a, mine_b, other_a, other_b = [
            columns_of(tables, depth, ref[at, :]) for ref in (pack_a, pack_b, got_a, got_b)
        ]

        def choose(one, two):
            return [jnp.where(even_col, a, b) for a, b in zip(one, two)]

        left = flows(choose(other_b, other_a), choose(mine_b, mine_a), 0.0)
        right = flows(choose(mine_a, mine_b), choose(other_a, other_b), 0.0)
        for out, low, high in zip((qp, wp), left, right):
            out[at, :] = jnp.where(
                odd,
                jnp.take_along_axis(low, half, axis=1),
                jnp.take_along_axis(high, half, axis=1),
            )
        return carry

    def two_edges(step, carry):
        return edge(2 * step + 1, edge(2 * step, carry))

    lax.fori_loop(0, tiles // 2, two_edges, 0)
    rq[...] = jnp.zeros(rq.shape, F32)
    rw[...] = jnp.zeros(rw.shape, F32)

    def rows(step, top):
        begin = pl.multiple_of(step * 8, 8)
        at = pl.ds(begin, 8)
        beyond = pl.ds(pl.multiple_of(jnp.minimum(begin + 8, rows_all - 8), 8), 8)
        outer = (sub == 7) & (step == tiles - 1)
        edge_q, edge_w = qp[at, :], wp[at, :]
        kind, s, p = [jnp.where(even_row, face_b[n, at, :], face_a[n, at, :]) for n in range(3)]
        below = [p, *rock_of(tables, kind, s)]
        kind, s, p = [jnp.where(even_row, face_a[n, at, :], face_b[n, at, :]) for n in range(3)]
        above = [p, *rock_of(tables, kind, s)]
        cur = [ref[0, at, :] for ref in (press, perm, frac)]
        depth_q, depth_w = flows(below, cur, gravity)
        told = jnp.where(
            (lane >= depth) & (lane < 2 * depth), spread(source[at, :], 127), 0.0
        )
        for d in range(depth):
            nxt = [ref[d + 1, at, :] for ref in (press, perm, frac)] if d + 1 < depth else above
            q, w = flows(cur, nxt, gravity)
            net_sum = w - depth_w
            out = jnp.maximum(q, 0.0) - jnp.minimum(depth_q, 0.0)
            depth_q, depth_w = q, w
            up = [
                pltpu.roll(jnp.where(sub == 0, ref[d, beyond, :], x), 7, 0)
                for ref, x in zip((press, perm, frac), cur)
            ]
            q, w = flows(cur, up, 0.0)
            q = jnp.where(outer, 0.0, q)
            w = jnp.where(outer, 0.0, w)
            q_roll, w_roll = pltpu.roll(q, 1, 0), pltpu.roll(w, 1, 0)
            low_q = jnp.where(sub == 0, rq[d], q_roll)
            low_w = jnp.where(sub == 0, rw[d], w_roll)
            rq[d] = q_roll
            rw[d] = w_roll
            net_sum = net_sum + (w - low_w)
            out = out + (jnp.maximum(q, 0.0) - jnp.minimum(low_q, 0.0))
            q, w = flows(cur, [pltpu.roll(x, 127, 1) for x in cur], 0.0)
            side_q = pltpu.roll(edge_q, 127 - 2 * d, 1)
            side_w = pltpu.roll(edge_w, 127 - 2 * d, 1)
            low_q = jnp.where(lane == 0, side_q, pltpu.roll(q, 1, 1))
            low_w = jnp.where(lane == 0, side_w, pltpu.roll(w, 1, 1))
            q = jnp.where(lane == 127, side_q, q)
            w = jnp.where(lane == 127, side_w, w)
            net_sum = 2.0 * (net_sum + (w - low_w))
            net[d, at, :] = net_sum
            told = jnp.where(lane == d, pltpu.roll(net_sum, d + 1, 1), told)
            out = out + (jnp.maximum(q, 0.0) - jnp.minimum(low_q, 0.0))
            top = jnp.maximum(top, out)
            cur = nxt
        ahead[at, :] = told
        return top

    top = lax.fori_loop(0, tiles, rows, jnp.zeros((8, 128), F32))

    def add(step, sums):
        at = step * 8
        return tuple(s + residual[at + n] for n, s in enumerate(sums))

    sums = lax.fori_loop(0, residual.shape[0] // 8, add, (jnp.zeros((8, 128), F32),) * 8)
    total = sum(sums[1:], sums[0])
    message[...] = jnp.where(
        lax.broadcasted_iota(jnp.int32, message.shape, 1) == 0,
        2.0 * jnp.max(top),
        jnp.sum(total),
    )


def update_kernel(
    place, gathered, table, sat, net, source, perm, wgain, ogain, got_a, got_b, beside,
    new_out, chunks, cell_sum, row_sum, col_sum, new, sem,
):
    lane = lane_iota()
    depth, rows_all, _ = sat.shape
    tiles = rows_all // 8
    stride = (depth + 1) * 8
    spot = lax.broadcasted_iota(jnp.int32, gathered.shape, 1)
    top = jnp.max(jnp.where(spot == 0, gathered[...], 0.0), keepdims=True)
    step_size = jnp.broadcast_to(courant / (top + tiny), (8, 128))
    even_col = place[0] % 2 == 0
    tables = [lane_table(table, n) for n in range(3)]

    def coefficient(k, wg, og, s):
        return k * (wg * s * s + og * (1.0 - s) * (1.0 - s))

    def rows(step, carry):
        at = pl.ds(pl.multiple_of(step * 8, 8), 8)
        begin = step * stride
        add = step_size * source[at, :]
        total = jnp.zeros((8, 128), F32)
        first = jnp.zeros((8, 128), F32)
        for d in range(depth):
            s = sat[d, at, :] - step_size * net[d, at, :] + add
            new[d, at, :] = s
            c = coefficient(perm[d, at, :], wgain[d, at, :], ogain[d, at, :], s)
            chunks[pl.ds(pl.multiple_of(begin + d * 8, 8), 8), :] = c
            total = total + c
            first = jnp.where(lane == d, pltpu.roll(c, d, 1) if d else c, first)
        cell_sum[at, :] = total
        tile = jnp.where(even_col, got_b[at, :], got_a[at, :])
        flow = beside[at, :]
        kind = jnp.where(lane < depth, tile, 0.0)
        index = jnp.maximum(kind.astype(jnp.int32) - 1, 0)
        k, wg, og = [lane_take(each, index) for each in tables]
        s = pltpu.roll(tile, 128 - depth, 1) - step_size * flow
        s = s + step_size * pltpu.roll(flow, 128 - depth, 1)
        c = coefficient(jnp.where(kind > 0.5, k, 0.0), wg, og, s)
        col_sum[at, :] = jnp.where(lane < depth, harmonic(c, first), 0.0)
        return carry

    def two_rows(step, carry):
        rows(2 * step + 1, rows(2 * step, carry))
        leave(step).start()
        return carry

    def leave(step):
        part = pl.ds(pl.multiple_of(step * 16, 16), 16)
        return pltpu.make_async_copy(new.at[:, part, :], new_out.at[:, part, :], sem.at[step])

    lax.fori_loop(0, tiles // 2, two_rows, 0)
    row_sum[0:8, :] = jnp.zeros((8, 128), F32)
    for p in range(1, tiles):
        total = jnp.zeros((8, 128), F32)
        for half in range(depth // 8):
            low = chunks[pl.ds((p - 1) * stride + half * 64 + 7, 8, stride=8), :]
            high = chunks[pl.ds(p * stride + half * 64, 8, stride=8), :]
            total = total + harmonic(low, high)
        row_sum[p * 8 : p * 8 + 8, :] = total
    brick = lax.broadcasted_iota(jnp.int32, (rows_all, 128), 0) // 8
    spot = lax.broadcasted_iota(jnp.int32, (rows_all, 128), 1)
    total = jnp.zeros((1, 128), F32)
    for n, part in enumerate((cell_sum, row_sum, col_sum)):
        each = jnp.sum(part[...], axis=1, keepdims=True)
        placed = jnp.where(spot == n * 16 + brick, each, 0.0)
        total = total + jnp.sum(placed, axis=0, keepdims=True)
    for p in range(tiles):
        chunks[p * stride + depth * 8 : (p + 1) * stride, :] = jnp.broadcast_to(total, (8, 128))
    for step in range(tiles // 2):
        leave(step).wait()


def relax_kernel(depth, place, got, residual, values, row_a, row_b, message, fd, fr, fc, gain, base):
    lane = lane_iota()
    sub = sub_iota()
    layers = residual.shape[0] // 8
    parts = layers // depth
    zero = jnp.zeros((8, 128), F32)
    fd[0:8, :] = zero
    values[layers * 8 :, :] = jnp.zeros((64, 128), F32)
    fc[layers * 8 :, :] = jnp.zeros((64, 128), F32)
    even_row = place[2] % 2 == 0

    def half_face(low, high):
        return low * high / (low + high)

    def part(w, carry):
        below, total = carry
        begin = w * (depth + 1) * 8
        place_w = w * depth * 8
        after = jnp.minimum(w + 1, parts - 1) * (depth + 1) * 8
        c = got[pl.ds(pl.multiple_of(begin, 8), 8), :]
        for d in range(depth):
            here = pl.ds(pl.multiple_of(place_w + d * 8, 8), 8)
            if d + 1 < depth:
                c_next = got[pl.ds(pl.multiple_of(begin + d * 8 + 8, 8), 8), :]
                above = half_face(c, c_next)
            else:
                c_next = got[pl.ds(pl.multiple_of(after, 8), 8), :]
                above = jnp.where(w + 1 < parts, half_face(c, c_next), 0.0)
            row = jnp.where(sub == 0, 0.0, half_face(pltpu.roll(c, 1, 0), c))
            col = jnp.where(lane == 0, 0.0, half_face(pltpu.roll(c, 1, 1), c))
            diag = (
                (0.5 * compress) * c + below + above
                + row + pltpu.roll(row, 7, 0) + col + pltpu.roll(col, 127, 1)
            )
            scale = relax / diag
            fd[pl.ds(pl.multiple_of(place_w + d * 8 + 8, 8), 8), :] = above
            fr[here, :] = row
            fc[here, :] = col
            gain[here, :] = scale
            first = (0.5 * scale) * residual[here, :]
            base[here, :] = first
            values[here, :] = first
            c, below = c_next, above
        total = total + got[pl.ds(pl.multiple_of(begin + depth * 8, 8), 8), :]
        return below, total

    def build(step, carry):
        return part(2 * step + 1, part(2 * step, carry))

    _, total = lax.fori_loop(0, parts // 2, build, (zero, zero))

    block = 32

    def sweep(number, carry):
        def some(step, prev):
            begin = step * (block * 8)
            v = values[pl.ds(pl.multiple_of(begin, 8), 8), :]
            for n in range(block):
                here = pl.ds(pl.multiple_of(begin + n * 8, 8), 8)
                above = pl.ds(pl.multiple_of(begin + n * 8 + 8, 8), 8)
                v_next = values[above, :]
                row = fr[here, :]
                col = fc[here, :]
                total = fd[here, :] * prev + fd[above, :] * v_next
                total = total + (row * pltpu.roll(v, 1, 0) + pltpu.roll(row * v, 7, 0))
                total = total + (col * pltpu.roll(v, 1, 1) + pltpu.roll(col * v, 127, 1))
                values[here, :] = ((1.0 - relax) * v + base[here, :]) + gain[here, :] * total
                prev, v = v, v_next
            return prev

        lax.fori_loop(0, layers // block, some, zero)
        return carry

    lax.fori_loop(0, SWEEPS - 1, sweep, 0)

    for w in range(parts):
        for half in range(depth // 8):
            at = w * (depth + 1) * 8 + half * 64
            spot = w * depth + half * 8
            pairs = []
            for row in (0, 7):
                c = got[pl.ds(at + row, 8, stride=8), :]
                v = values[pl.ds(spot * 8 + row, 8, stride=8), :]
                pairs.append((c * v, c))
            for n in range(2):
                low, high = pairs[0][n], pairs[1][n]
                rows = slice(n * layers + spot, n * layers + spot + 8)
                row_a[rows, :] = jnp.where(even_row, high, low)
                row_b[rows, :] = jnp.where(even_row, low, high)

    quarters = layers // 64
    per_tile = 64 // depth
    peers = message.shape[0] // (quarters * 16 + 8)

    def pack(quarter, carry):
        packed = [zero, zero]
        for l in range(64):
            part = quarter * per_tile + l // depth
            c = got[pl.ds(pl.multiple_of(part * (depth + 1) * 8 + l % depth * 8, 8), 8), :]
            v = values[pl.ds(pl.multiple_of(quarter * 512 + l * 8, 8), 8), :]
            spot = (2 * l + 2) % 128
            mark = (lane == 2 * l + 1) | (lane == spot)
            for n, tile in enumerate((c * v, c)):
                turned = pltpu.roll(tile, spot, 1) if spot else tile
                packed[n] = jnp.where(mark, turned, packed[n])
        for peer in range(peers):
            for n in range(2):
                begin = peer * (quarters * 16 + 8) + (n * quarters + quarter) * 8
                message[pl.ds(pl.multiple_of(begin, 8), 8), :] = packed[n]
        return carry

    lax.fori_loop(0, quarters, pack, 0)
    for peer in range(peers):
        begin = peer * (quarters * 16 + 8) + quarters * 16
        message[begin : begin + 8, :] = total


def coarse_kernel(count, place, news, gathered, out):
    lane = lane_iota()
    sub = sub_iota()
    inside = lane < count
    width = gathered.shape[0] // count
    stride = news.shape[0] // width
    sums = jnp.zeros((8, 128), F32)
    for k in range(width):
        sums = jnp.where(sub == k, news[(k + 1) * stride - 8 : (k + 1) * stride, :], sums)
    cells = jnp.where(inside, sums, 0.0)
    low_row = jnp.where(inside, pltpu.roll(sums, 128 - 16, 1), 0.0)
    low_col = jnp.where(inside, pltpu.roll(sums, 128 - 32, 1), 0.0)
    low_row = jnp.where(lane == 0, 0.0, low_row)
    low_col = jnp.where(sub == 0, 0.0, low_col)
    high_row = pltpu.roll(low_row, 127, 1)
    high_col = pltpu.roll(low_col, 7, 0)
    diagonal = jnp.where(inside, compress * cells + low_row + high_row + low_col + high_col, 1.0)
    rhs = jnp.zeros((8, 128), F32)
    for p in range(count):
        rhs = jnp.where(lane == p, spread(gathered[p * width : p * width + width, :], 1), rhs)

    def line(tile, k):
        return jnp.broadcast_to(tile[k : k + 1, :], (8, 128))

    zero = jnp.zeros((8, 128), F32)
    main, lower, upper, right = [], [], [], []
    for k in range(width):
        row = jnp.where(sub == k, line(diagonal, k), zero)
        if k > 0:
            row = jnp.where(sub == k - 1, -line(low_col, k), row)
        if k + 1 < width:
            row = jnp.where(sub == k + 1, -line(low_col, k + 1), row)
        main.append(row)
        lower.append(jnp.where(sub == k, -line(low_row, k), zero))
        upper.append(jnp.where(sub == k, -line(high_row, k), zero))
        right.append(line(rhs, k))

    def eliminate(main, others):
        main = list(main)
        others = [list(rows) for rows in others]
        for k in range(width):
            inverse = 1.0 / line(main[k], k)
            main[k] = main[k] * inverse
            for rows in others:
                rows[k] = rows[k] * inverse
            for j in range(width):
                if j != k:
                    factor = line(main[j], k)
                    main[j] = main[j] - factor * main[k]
                    for rows in others:
                        rows[j] = rows[j] - factor * rows[k]
        return others

    stride = 1
    while stride < count:
        solved = eliminate(main, [lower, upper, right])
        back = [[pltpu.roll(x, stride, 1) for x in rows] for rows in solved]
        ahead = [[pltpu.roll(x, 128 - stride, 1) for x in rows] for rows in solved]
        new_lower, new_upper, new_main, new_right = [], [], [], []
        for k in range(width):
            lo, up, mid, rt = zero, zero, main[k], right[k]
            for j in range(width):
                a = line(lower[k], j)
                b = line(upper[k], j)
                lo = lo - a * back[0][j]
                mid = mid - a * back[1][j] - b * ahead[0][j]
                up = up - b * ahead[1][j]
                rt = rt - a * back[2][j] - b * ahead[2][j]
            new_lower.append(lo)
            new_upper.append(up)
            new_main.append(mid)
            new_right.append(rt)
        lower, upper, main, right = new_lower, new_upper, new_main, new_right
        stride *= 2
    (right,) = eliminate(main, [right])
    mine = zero
    for k in range(width):
        mine = jnp.where(place[0] == k, right[k], mine)
    out[...] = lane_pick(mine, place[2])


def final_kernel(depth, place, got, values, row_a, row_b, news, coarse, result, packs, out, sem):
    lane = lane_iota()
    sub = sub_iota()
    layers = out.shape[0] // 8
    quarters = layers // 64
    per_tile = 64 // depth
    add = coarse[...]
    even_row = place[2] % 2 == 0
    stride = quarters * 16 + 8
    left = pl.multiple_of(jnp.maximum(place[0] - 1, 0) * stride, 8)
    right = pl.multiple_of(jnp.minimum(place[0] + 1, place[1] - 1) * stride, 8)
    odd = (lane & 1) == 1
    has_left = odd & (place[0] > 0)
    has_right = jnp.logical_not(odd) & (place[0] + 1 < place[1])
    for n in range(quarters * 2):
        low = news[pl.ds(left + n * 8, 8), :]
        high = pltpu.roll(news[pl.ds(right + n * 8, 8), :], 126, 1)
        packs[n * 8 : n * 8 + 8, :] = jnp.where(has_left, low, jnp.where(has_right, high, 0.0))
    ends = (lane == 0) | (lane == 127)

    def some(quarter, carry):
        sides = [
            packs[pl.ds(pl.multiple_of((n * quarters + quarter) * 8, 8), 8), :] for n in range(2)
        ]
        for l in range(64):
            g = quarter * 64 + l
            part = quarter * per_tile + l // depth
            here = pl.ds(pl.multiple_of(g * 8, 8), 8)
            c = got[pl.ds(pl.multiple_of(part * (depth + 1) * 8 + l % depth * 8, 8), 8), :]
            v = values[here, :]
            pair = []
            for n, tile in enumerate((c * v, c)):
                at = pl.ds(n * layers + g, 1)
                low = jnp.where(even_row, row_b[at, :], row_a[at, :])
                high = jnp.where(even_row, row_a[at, :], row_b[at, :])
                tile = tile + jnp.where(sub == 0, low, jnp.where(sub == 7, high, 0.0))
                tile = tile + jnp.where(ends, pltpu.roll(sides[n], 127 - 2 * l, 1), 0.0)
                pair.append(tile)
            out[here, :] = pair[0] / pair[1] + add
        leave(quarter).start()
        return carry

    def leave(quarter):
        part = pl.ds(pl.multiple_of(quarter * 512, 512), 512)
        return pltpu.make_async_copy(out.at[part, :], result.at[part, :], sem.at[quarter])

    lax.fori_loop(0, quarters, some, 0)
    for quarter in range(quarters):
        leave(quarter).wait()


def partners(array, axis, odd):
    count = lax.axis_size(axis)
    pairs = [(i, i + 1) for i in range(odd, count - 1, 2)]
    return lax.ppermute(array, axis, pairs + [(j, i) for i, j in pairs])


def forward(array, axis):
    count = lax.axis_size(axis)
    return lax.ppermute(array, axis, [(i, i + 1) for i in range(count - 1)])


def shards(saturation, pressure, rock_class, rock_table, well_columns, well_rates, residual):
    depth, rows_all, cols = saturation.shape
    layers, brick_rows, _ = residual.shape
    wide, narrow = lax.axis_size("wide"), lax.axis_size("narrow")
    block = (depth, rows_all, cols)
    plane = (rows_all, cols)
    place = jnp.stack(
        [lax.axis_index("narrow"), jnp.int32(narrow), lax.axis_index("wide")]
    ).astype(jnp.int32)
    vmem = pl.BlockSpec(memory_space=pltpu.VMEM)
    smem = pl.BlockSpec(memory_space=pltpu.SMEM)
    far = pl.BlockSpec(memory_space=pltpu.HBM)

    sat, press, kinds, face_a, face_b, pack_a, pack_b = call(
        faces_kernel,
        [block] * 3 + [(3,) + plane] * 2 + [plane] * 2,
        scratch=[pltpu.VMEM(block, jnp.int32), pltpu.SemaphoreType.DMA((12,))],
        in_specs=[smem] + [far] * 3,
        name="faces",
    )(
        place,
        *(
            pltpu.with_memory_space_constraint(array, pltpu.HBM)
            for array in (saturation, pressure, rock_class)
        ),
    )
    perm, wgain, ogain, frac = call(lookup_kernel, [block] * 4, name="lookup")(
        rock_table, kinds, sat
    )
    got_face_a = partners(face_a, "wide", 0)
    got_face_b = partners(face_b, "wide", 1)
    got_pack_a = partners(pack_a, "narrow", 0)
    got_pack_b = partners(pack_b, "narrow", 1)
    net, source, ahead, message = call(
        functools.partial(flow_kernel, narrow),
        [block, plane, plane, (wide * narrow, 128)],
        scratch=[pltpu.VMEM(plane, F32)] * 2 + [pltpu.VMEM((depth, 8, cols), F32)] * 2,
        in_specs=[smem] + [vmem] * 13,
        name="flow",
    )(
        place, rock_table, press, perm, frac, got_face_a, got_face_b, pack_a, pack_b, got_pack_a, got_pack_b,
        well_columns.reshape(1, -1), well_rates.reshape(1, -1), residual,
    )
    beside = forward(ahead, "narrow")
    gathered = lax.all_to_all(message, ("wide", "narrow"), 0, 0, tiled=True)
    chunk_rows = wide * (depth + 1) * 8
    sat_new, chunks = call(
        update_kernel,
        [block, (chunk_rows, 128)],
        scratch=[pltpu.VMEM(plane, F32)] * 3
        + [pltpu.VMEM(block, F32), pltpu.SemaphoreType.DMA((rows_all // 16,))],
        in_specs=[smem] + [vmem] * 11,
        out_specs=[far, vmem],
        name="update",
    )(
        place, gathered, rock_table, sat, net, source, perm, wgain, ogain, got_pack_a, got_pack_b,
        beside,
    )
    got = lax.all_to_all(chunks, "wide", 0, 0, tiled=True)
    message_rows = narrow * (layers // 4 + 8)
    values, row_a, row_b, message = call(
        functools.partial(relax_kernel, depth),
        [(layers * 8 + 64, 128)] + [(2 * layers, 128)] * 2 + [(message_rows, 128)],
        scratch=[pltpu.VMEM((layers * 8 + 64, 128), F32)] * 5,
        in_specs=[smem, vmem, vmem],
        name="relaxation",
    )(place, got, residual.reshape(layers * 8, 128))
    got_row_a = partners(row_a, "wide", 0)
    got_row_b = partners(row_b, "wide", 1)
    news = lax.all_to_all(message, "narrow", 0, 0, tiled=True)
    (coarse,) = call(
        functools.partial(coarse_kernel, wide),
        [(8, 128)],
        in_specs=[smem, vmem, vmem],
        name="coarse",
    )(place, news, gathered)
    (precond,) = call(
        functools.partial(final_kernel, depth),
        [(layers * 8, 128)],
        scratch=[
            pltpu.VMEM((layers // 4, 128), F32),
            pltpu.VMEM((layers * 8, 128), F32),
            pltpu.SemaphoreType.DMA((layers // 64,)),
        ],
        in_specs=[smem] + [vmem] * 6,
        out_specs=[far],
        name="final",
    )(place, got, values, got_row_a, got_row_b, news, coarse)
    return (sat_new, precond.reshape(layers, brick_rows, cols))


def solution(mesh):
    placed = (
        P("wide", None, "narrow"),
        P("wide", None, "narrow"),
        P("wide", None, "narrow"),
        P(),
        P(),
        P(),
        P(None, "wide", "narrow"),
    )
    return jax.shard_map(
        shards,
        mesh=mesh,
        in_specs=placed,
        out_specs=(P("wide", None, "narrow"), P(None, "wide", "narrow")),
        check_vma=False,
    )
```

```python
import functools

import jax
import jax.numpy as jnp
from jax import lax
from jax.experimental import pallas as pl
from jax.experimental.pallas import tpu as pltpu
from jax.sharding import PartitionSpec as P


SWEEPS = 6
compress = 0.05
relax = 0.8
gravity = 0.5
courant = 0.5
tiny = 1e-06

F32 = jnp.float32
HIGH = lax.Precision.HIGHEST
PARAMS = pltpu.CompilerParams(vmem_limit_bytes=16 * 1024 * 1024)


def harmonic(low, high):
    return 2.0 * low * high / (low + high)


def sub_iota():
    return lax.broadcasted_iota(jnp.int32, (8, 128), 0)


def lane_iota():
    return lax.broadcasted_iota(jnp.int32, (8, 128), 1)


def lane_pick(tile, index):
    return jnp.take_along_axis(tile, jnp.full((8, 128), index, jnp.int32), axis=1)


def lane_take(tile, index):
    return jnp.take_along_axis(tile, index, axis=1, mode="promise_in_bounds")


def mobility(wg, og, s):
    water = wg * s * s
    return water, water + og * (1.0 - s) * (1.0 - s)


def lane_table(table, n):
    row = jnp.concatenate([table[n : n + 1, :], jnp.zeros((1, 112), F32)], axis=1)
    return jnp.broadcast_to(row, (8, 128))


def spread(tile, lane):
    return jnp.broadcast_to(tile[:, lane : lane + 1], (8, 128))


def call(kernel, outs, scratch=(), aliases=None, out_specs=None, in_specs=None):
    def run(*args):
        return pl.pallas_call(
            kernel,
            out_shape=[jax.ShapeDtypeStruct(shape, F32) for shape in outs],
            in_specs=in_specs or [pl.BlockSpec(memory_space=pltpu.VMEM)] * len(args),
            out_specs=out_specs or [pl.BlockSpec(memory_space=pltpu.VMEM)] * len(outs),
            scratch_shapes=list(scratch),
            input_output_aliases=aliases or {},
            compiler_params=PARAMS,
        )(*args)

    return run


def faces_kernel(
    place, sat_in, press_in, rock_in, sat, press, kinds, face_a, face_b, pack_a, pack_b, rock, sem
):
    lane = lane_iota()
    depth, rows_all, _ = sat.shape
    groups = 4
    each = rows_all // groups
    copies = []
    for g in range(groups):
        part = pl.ds(g * each, each)
        for n, (src, dst) in enumerate(((rock_in, rock), (sat_in, sat), (press_in, press))):
            copies.append(
                pltpu.make_async_copy(src.at[:, part, :], dst.at[:, part, :], sem.at[g * 3 + n])
            )
            copies[-1].start()
    even_row = place[2] % 2 == 0
    even_col = place[0] % 2 == 0

    def rows(step, carry):
        at = pl.ds(pl.multiple_of(step * 8, 8), 8)
        first = jnp.zeros((8, 128), F32)
        last = jnp.zeros((8, 128), F32)
        for d in range(depth):
            kind = rock[d, at, :].astype(F32) + 1.0
            kinds[d, at, :] = kind
            fields = (kind, sat[d, at, :], press[d, at, :])
            for n, field in enumerate(fields):
                spot = n * depth + d
                turned = pltpu.roll(field, spot + 1, 1)
                first = jnp.where(lane == spot + 1, turned, first)
                last = jnp.where(lane == spot, turned, last)
                if d == 0:
                    face_a[n, at, :] = field
                if d + 1 == depth:
                    low = face_a[n, at, :]
                    face_a[n, at, :] = jnp.where(even_row, field, low)
                    face_b[n, at, :] = jnp.where(even_row, low, field)
        first = pltpu.roll(first, 127, 1)
        pack_a[at, :] = jnp.where(even_col, last, first)
        pack_b[at, :] = jnp.where(even_col, first, last)
        return carry

    def two_rows(step, carry):
        return rows(2 * step + 1, rows(2 * step, carry))

    for g in range(groups):
        for copy in copies[g * 3 : g * 3 + 3]:
            copy.wait()
        lax.fori_loop(g * (each // 16), (g + 1) * (each // 16), two_rows, 0)


def rock_of(tables, kind, s):
    index = jnp.maximum(kind.astype(jnp.int32) - 1, 0)
    k, wg, og = [lane_take(table, index) for table in tables]
    water, both = mobility(wg, og, s)
    return jnp.where(kind > 0.5, k, 0.0), water / both


def columns_of(tables, depth, pack):
    lane = lane_iota()
    kind = jnp.where(lane < depth, pack, 0.0)
    k, f = rock_of(tables, kind, pltpu.roll(pack, 128 - depth, 1))
    return [pltpu.roll(pack, 128 - 2 * depth, 1), k, f]


def lookup_kernel(table, kinds, sat, perm, wgain, ogain, frac):
    depth, rows_all, _ = sat.shape
    tables = [lane_table(table, n) for n in range(2)]
    entries = [jnp.broadcast_to(table[2:3, m : m + 1], (8, 128)) for m in range(16)]

    def rows(step, carry):
        at = pl.ds(pl.multiple_of(step * 8, 8), 8)
        for d in range(depth):
            kind = kinds[d, at, :].astype(jnp.int32) - 1
            k = lane_take(tables[0], kind)
            wg = lane_take(tables[1], kind)
            values = entries
            for bit in range(4):
                taken = (kind & (1 << bit)) != 0
                values = [
                    jnp.where(taken, values[m + 1], values[m]) for m in range(0, len(values), 2)
                ]
            og = values[0]
            water, both = mobility(wg, og, sat[d, at, :])
            perm[d, at, :] = k
            wgain[d, at, :] = wg
            ogain[d, at, :] = og
            frac[d, at, :] = water / both
        return carry

    lax.fori_loop(0, rows_all // 8, rows, 0)


def flows(low, high, lift):
    total = low[1] * high[1] / (low[1] + high[1]) * (low[0] - high[0] + lift)
    return total, total * jnp.where(total > 0, low[2], high[2])


def flow_kernel(
    bricks, place, table, press, perm, frac, face_a, face_b, pack_a, pack_b, got_a, got_b,
    columns, rates, residual, net, source, message, qp, wp, rq, rw,
):
    lane = lane_iota()
    sub = sub_iota()
    depth, rows_all, cols = perm.shape
    tiles = rows_all // 8
    even_row = place[2] % 2 == 0
    even_col = place[0] % 2 == 0
    half = lane >> 1
    odd = (lane & 1) == 1
    tables = [lane_table(table, n) for n in range(3)]

    wells = columns.shape[1]
    spot = lax.broadcasted_iota(jnp.int32, (rows_all, wells), 0)
    apart = columns[...] - spot * (cols * bricks)
    in_row = jnp.where((apart >= 0) & (apart < cols * bricks), 1.0, 0.0)
    number = columns[...]
    well_col = number & (cols * bricks - 1) if (cols * bricks) & (cols * bricks - 1) == 0 else number % (cols * bricks)
    spot = lax.broadcasted_iota(jnp.int32, (cols, wells), 0)
    in_col = jnp.where(well_col - place[0] * cols == spot, rates[...], 0.0)
    source[...] = lax.dot_general(
        in_row, in_col, (((1,), (1,)), ((), ())), precision=HIGH, preferred_element_type=F32
    )

    def edge(step, carry):
        at = pl.ds(pl.multiple_of(step * 8, 8), 8)

        mine_a, mine_b, other_a, other_b = [
            columns_of(tables, depth, ref[at, :]) for ref in (pack_a, pack_b, got_a, got_b)
        ]

        def choose(one, two):
            return [jnp.where(even_col, a, b) for a, b in zip(one, two)]

        left = flows(choose(other_b, other_a), choose(mine_b, mine_a), 0.0)
        right = flows(choose(mine_a, mine_b), choose(other_a, other_b), 0.0)
        for out, low, high in zip((qp, wp), left, right):
            out[at, :] = jnp.where(
                odd,
                jnp.take_along_axis(low, half, axis=1),
                jnp.take_along_axis(high, half, axis=1),
            )
        return carry

    def two_edges(step, carry):
        return edge(2 * step + 1, edge(2 * step, carry))

    lax.fori_loop(0, tiles // 2, two_edges, 0)
    rq[...] = jnp.zeros(rq.shape, F32)
    rw[...] = jnp.zeros(rw.shape, F32)

    def rows(step, top):
        begin = pl.multiple_of(step * 8, 8)
        at = pl.ds(begin, 8)
        beyond = pl.ds(pl.multiple_of(jnp.minimum(begin + 8, rows_all - 8), 8), 8)
        outer = (sub == 7) & (step == tiles - 1)
        edge_q, edge_w = qp[at, :], wp[at, :]
        kind, s, p = [jnp.where(even_row, face_b[n, at, :], face_a[n, at, :]) for n in range(3)]
        below = [p, *rock_of(tables, kind, s)]
        kind, s, p = [jnp.where(even_row, face_a[n, at, :], face_b[n, at, :]) for n in range(3)]
        above = [p, *rock_of(tables, kind, s)]
        cur = [ref[0, at, :] for ref in (press, perm, frac)]
        depth_q, depth_w = flows(below, cur, gravity)
        for d in range(depth):
            nxt = [ref[d + 1, at, :] for ref in (press, perm, frac)] if d + 1 < depth else above
            q, w = flows(cur, nxt, gravity)
            net_sum = w - depth_w
            out = jnp.maximum(q, 0.0) - jnp.minimum(depth_q, 0.0)
            depth_q, depth_w = q, w
            up = [
                pltpu.roll(jnp.where(sub == 0, ref[d, beyond, :], x), 7, 0)
                for ref, x in zip((press, perm, frac), cur)
            ]
            q, w = flows(cur, up, 0.0)
            q = jnp.where(outer, 0.0, q)
            w = jnp.where(outer, 0.0, w)
            q_roll, w_roll = pltpu.roll(q, 1, 0), pltpu.roll(w, 1, 0)
            low_q = jnp.where(sub == 0, rq[d], q_roll)
            low_w = jnp.where(sub == 0, rw[d], w_roll)
            rq[d] = q_roll
            rw[d] = w_roll
            net_sum = net_sum + (w - low_w)
            out = out + (jnp.maximum(q, 0.0) - jnp.minimum(low_q, 0.0))
            q, w = flows(cur, [pltpu.roll(x, 127, 1) for x in cur], 0.0)
            side_q = pltpu.roll(edge_q, 127 - 2 * d, 1)
            side_w = pltpu.roll(edge_w, 127 - 2 * d, 1)
            low_q = jnp.where(lane == 0, side_q, pltpu.roll(q, 1, 1))
            low_w = jnp.where(lane == 0, side_w, pltpu.roll(w, 1, 1))
            q = jnp.where(lane == 127, side_q, q)
            w = jnp.where(lane == 127, side_w, w)
            net_sum = 2.0 * (net_sum + (w - low_w))
            net[d, at, :] = net_sum
            out = out + (jnp.maximum(q, 0.0) - jnp.minimum(low_q, 0.0))
            top = jnp.maximum(top, out)
            cur = nxt
        return top

    top = lax.fori_loop(0, tiles, rows, jnp.zeros((8, 128), F32))

    def add(step, sums):
        at = step * 8
        return tuple(s + residual[at + n] for n, s in enumerate(sums))

    sums = lax.fori_loop(0, residual.shape[0] // 8, add, (jnp.zeros((8, 128), F32),) * 8)
    total = sum(sums[1:], sums[0])
    message[...] = jnp.where(
        lax.broadcasted_iota(jnp.int32, message.shape, 1) == 0,
        2.0 * jnp.max(top),
        jnp.sum(total),
    )


def told_kernel(net, source, ahead):
    lane = lane_iota()
    depth, rows_all, _ = net.shape

    def rows(step, carry):
        for n in range(4):
            at = pl.ds(pl.multiple_of(step * 32 + n * 8, 8), 8)
            told = jnp.where((lane >= depth) & (lane < 2 * depth), spread(source[at, :], 127), 0.0)
            for d in range(depth):
                told = jnp.where(lane == d, pltpu.roll(net[d, at, :], d + 1, 1), told)
            ahead[at, :] = told
        return carry

    lax.fori_loop(0, rows_all // 32, rows, 0)


def side_kernel(depth, place, table, got_a, got_b, side):
    lane = lane_iota()
    tables = [lane_table(table, n) for n in range(3)]
    even_col = place[0] % 2 == 0

    def rows(step, carry):
        for n in range(4):
            at = pl.ds(pl.multiple_of(step * 32 + n * 8, 8), 8)
            tile = jnp.where(even_col, got_b[at, :], got_a[at, :])
            kind = jnp.where(lane < depth, tile, 0.0)
            index = jnp.maximum(kind.astype(jnp.int32) - 1, 0)
            k, wg, og = [lane_take(each, index) for each in tables]
            side[0, at, :] = jnp.where(kind > 0.5, k, 0.0)
            side[1, at, :] = wg
            side[2, at, :] = og
            side[3, at, :] = pltpu.roll(tile, 128 - depth, 1)
        return carry

    lax.fori_loop(0, got_a.shape[0] // 32, rows, 0)


def update_kernel(
    gathered, sat, net, source, perm, wgain, ogain, side, beside,
    new_out, chunks, cell_sum, row_sum, col_sum, new, sem,
):
    lane = lane_iota()
    depth, rows_all, _ = sat.shape
    tiles = rows_all // 8
    stride = (depth + 1) * 8
    spot = lax.broadcasted_iota(jnp.int32, gathered.shape, 1)
    top = jnp.max(jnp.where(spot == 0, gathered[...], 0.0), keepdims=True)
    step_size = jnp.broadcast_to(courant / (top + tiny), (8, 128))

    def coefficient(k, wg, og, s):
        return k * (wg * s * s + og * (1.0 - s) * (1.0 - s))

    def rows(step, carry):
        at = pl.ds(pl.multiple_of(step * 8, 8), 8)
        begin = step * stride
        add = step_size * source[at, :]
        total = jnp.zeros((8, 128), F32)
        first = jnp.zeros((8, 128), F32)
        for d in range(depth):
            s = sat[d, at, :] - step_size * net[d, at, :] + add
            new[d, at, :] = s
            c = coefficient(perm[d, at, :], wgain[d, at, :], ogain[d, at, :], s)
            chunks[pl.ds(pl.multiple_of(begin + d * 8, 8), 8), :] = c
            total = total + c
            first = jnp.where(lane == d, pltpu.roll(c, d, 1) if d else c, first)
        cell_sum[at, :] = total
        flow = beside[at, :]
        s = side[3, at, :] - step_size * flow
        s = s + step_size * pltpu.roll(flow, 128 - depth, 1)
        c = coefficient(side[0, at, :], side[1, at, :], side[2, at, :], s)
        col_sum[at, :] = jnp.where(lane < depth, harmonic(c, first), 0.0)
        return carry

    def two_rows(step, carry):
        rows(2 * step + 1, rows(2 * step, carry))
        leave(step).start()
        return carry

    def leave(step):
        part = pl.ds(pl.multiple_of(step * 16, 16), 16)
        return pltpu.make_async_copy(new.at[:, part, :], new_out.at[:, part, :], sem.at[step])

    lax.fori_loop(0, tiles // 2, two_rows, 0)
    row_sum[0:8, :] = jnp.zeros((8, 128), F32)
    for p in range(1, tiles):
        total = jnp.zeros((8, 128), F32)
        for half in range(depth // 8):
            low = chunks[pl.ds((p - 1) * stride + half * 64 + 7, 8, stride=8), :]
            high = chunks[pl.ds(p * stride + half * 64, 8, stride=8), :]
            total = total + harmonic(low, high)
        row_sum[p * 8 : p * 8 + 8, :] = total
    brick = lax.broadcasted_iota(jnp.int32, (rows_all, 128), 0) // 8
    spot = lax.broadcasted_iota(jnp.int32, (rows_all, 128), 1)
    total = jnp.zeros((1, 128), F32)
    for n, part in enumerate((cell_sum, row_sum, col_sum)):
        each = jnp.sum(part[...], axis=1, keepdims=True)
        placed = jnp.where(spot == n * 16 + brick, each, 0.0)
        total = total + jnp.sum(placed, axis=0, keepdims=True)
    for p in range(tiles):
        chunks[p * stride + depth * 8 : (p + 1) * stride, :] = jnp.broadcast_to(total, (8, 128))
    for step in range(tiles // 2):
        leave(step).wait()


def relax_kernel(depth, place, got, residual, values, row_a, row_b, message, fd, fr, fc, gain, base):
    lane = lane_iota()
    sub = sub_iota()
    layers = residual.shape[0] // 8
    parts = layers // depth
    zero = jnp.zeros((8, 128), F32)
    fd[0:8, :] = zero
    values[layers * 8 :, :] = jnp.zeros((64, 128), F32)
    fc[layers * 8 :, :] = jnp.zeros((64, 128), F32)
    even_row = place[2] % 2 == 0

    def half_face(low, high):
        return low * high / (low + high)

    def part(w, carry):
        below, total = carry
        begin = w * (depth + 1) * 8
        place_w = w * depth * 8
        after = jnp.minimum(w + 1, parts - 1) * (depth + 1) * 8
        c = got[pl.ds(pl.multiple_of(begin, 8), 8), :]
        for d in range(depth):
            here = pl.ds(pl.multiple_of(place_w + d * 8, 8), 8)
            if d + 1 < depth:
                c_next = got[pl.ds(pl.multiple_of(begin + d * 8 + 8, 8), 8), :]
                above = half_face(c, c_next)
            else:
                c_next = got[pl.ds(pl.multiple_of(after, 8), 8), :]
                above = jnp.where(w + 1 < parts, half_face(c, c_next), 0.0)
            row = jnp.where(sub == 0, 0.0, half_face(pltpu.roll(c, 1, 0), c))
            col = jnp.where(lane == 0, 0.0, half_face(pltpu.roll(c, 1, 1), c))
            diag = (
                (0.5 * compress) * c + below + above
                + row + pltpu.roll(row, 7, 0) + col + pltpu.roll(col, 127, 1)
            )
            scale = relax / diag
            fd[pl.ds(pl.multiple_of(place_w + d * 8 + 8, 8), 8), :] = above
            fr[here, :] = row
            fc[here, :] = col
            gain[here, :] = scale
            first = (0.5 * scale) * residual[here, :]
            base[here, :] = first
            values[here, :] = first
            c, below = c_next, above
        total = total + got[pl.ds(pl.multiple_of(begin + depth * 8, 8), 8), :]
        return below, total

    def build(step, carry):
        return part(2 * step + 1, part(2 * step, carry))

    _, total = lax.fori_loop(0, parts // 2, build, (zero, zero))

    block = 32

    def sweep(number, carry):
        def some(step, prev):
            begin = step * (block * 8)
            v = values[pl.ds(pl.multiple_of(begin, 8), 8), :]
            for n in range(block):
                here = pl.ds(pl.multiple_of(begin + n * 8, 8), 8)
                above = pl.ds(pl.multiple_of(begin + n * 8 + 8, 8), 8)
                v_next = values[above, :]
                row = fr[here, :]
                col = fc[here, :]
                total = fd[here, :] * prev + fd[above, :] * v_next
                total = total + (row * pltpu.roll(v, 1, 0) + pltpu.roll(row * v, 7, 0))
                total = total + (col * pltpu.roll(v, 1, 1) + pltpu.roll(col * v, 127, 1))
                values[here, :] = ((1.0 - relax) * v + base[here, :]) + gain[here, :] * total
                prev, v = v, v_next
            return prev

        lax.fori_loop(0, layers // block, some, zero)
        return carry

    lax.fori_loop(0, SWEEPS - 1, sweep, 0)

    for w in range(parts):
        for half in range(depth // 8):
            at = w * (depth + 1) * 8 + half * 64
            spot = w * depth + half * 8
            pairs = []
            for row in (0, 7):
                c = got[pl.ds(at + row, 8, stride=8), :]
                v = values[pl.ds(spot * 8 + row, 8, stride=8), :]
                pairs.append((c * v, c))
            for n in range(2):
                low, high = pairs[0][n], pairs[1][n]
                rows = slice(n * layers + spot, n * layers + spot + 8)
                row_a[rows, :] = jnp.where(even_row, high, low)
                row_b[rows, :] = jnp.where(even_row, low, high)

    quarters = layers // 64
    per_tile = 64 // depth
    peers = message.shape[0] // (quarters * 16 + 8)

    def pack(quarter, carry):
        packed = [zero, zero]
        for l in range(64):
            part = quarter * per_tile + l // depth
            c = got[pl.ds(pl.multiple_of(part * (depth + 1) * 8 + l % depth * 8, 8), 8), :]
            v = values[pl.ds(pl.multiple_of(quarter * 512 + l * 8, 8), 8), :]
            spot = (2 * l + 2) % 128
            mark = (lane == 2 * l + 1) | (lane == spot)
            for n, tile in enumerate((c * v, c)):
                turned = pltpu.roll(tile, spot, 1) if spot else tile
                packed[n] = jnp.where(mark, turned, packed[n])
        for peer in range(peers):
            for n in range(2):
                begin = peer * (quarters * 16 + 8) + (n * quarters + quarter) * 8
                message[pl.ds(pl.multiple_of(begin, 8), 8), :] = packed[n]
        return carry

    lax.fori_loop(0, quarters, pack, 0)
    for peer in range(peers):
        begin = peer * (quarters * 16 + 8) + quarters * 16
        message[begin : begin + 8, :] = total


def rhs_kernel(count, gathered, out):
    lane = lane_iota()
    width = gathered.shape[0] // count
    rhs = jnp.zeros((8, 128), F32)
    for p in range(count):
        rhs = jnp.where(lane == p, spread(gathered[p * width : p * width + width, :], 1), rhs)
    out[...] = rhs


def coarse_kernel(count, width, place, news, rhs_ref, out):
    lane = lane_iota()
    sub = sub_iota()
    inside = lane < count
    stride = news.shape[0] // width
    sums = jnp.zeros((8, 128), F32)
    for k in range(width):
        sums = jnp.where(sub == k, news[(k + 1) * stride - 8 : (k + 1) * stride, :], sums)
    cells = jnp.where(inside, sums, 0.0)
    low_row = jnp.where(inside, pltpu.roll(sums, 128 - 16, 1), 0.0)
    low_col = jnp.where(inside, pltpu.roll(sums, 128 - 32, 1), 0.0)
    low_row = jnp.where(lane == 0, 0.0, low_row)
    low_col = jnp.where(sub == 0, 0.0, low_col)
    high_row = pltpu.roll(low_row, 127, 1)
    high_col = pltpu.roll(low_col, 7, 0)
    diagonal = jnp.where(inside, compress * cells + low_row + high_row + low_col + high_col, 1.0)
    rhs = rhs_ref[...]

    def line(tile, k):
        return jnp.broadcast_to(tile[k : k + 1, :], (8, 128))

    zero = jnp.zeros((8, 128), F32)
    main, lower, upper, right = [], [], [], []
    for k in range(width):
        row = jnp.where(sub == k, line(diagonal, k), zero)
        if k > 0:
            row = jnp.where(sub == k - 1, -line(low_col, k), row)
        if k + 1 < width:
            row = jnp.where(sub == k + 1, -line(low_col, k + 1), row)
        main.append(row)
        lower.append(jnp.where(sub == k, -line(low_row, k), zero))
        upper.append(jnp.where(sub == k, -line(high_row, k), zero))
        right.append(line(rhs, k))

    def eliminate(main, others):
        main = list(main)
        others = [list(rows) for rows in others]
        for k in range(width):
            inverse = 1.0 / line(main[k], k)
            main[k] = main[k] * inverse
            for rows in others:
                rows[k] = rows[k] * inverse
            for j in range(width):
                if j != k:
                    factor = line(main[j], k)
                    main[j] = main[j] - factor * main[k]
                    for rows in others:
                        rows[j] = rows[j] - factor * rows[k]
        return others

    stride = 1
    while stride < count:
        solved = eliminate(main, [lower, upper, right])
        back = [[pltpu.roll(x, stride, 1) for x in rows] for rows in solved]
        ahead = [[pltpu.roll(x, 128 - stride, 1) for x in rows] for rows in solved]
        new_lower, new_upper, new_main, new_right = [], [], [], []
        for k in range(width):
            lo, up, mid, rt = zero, zero, main[k], right[k]
            for j in range(width):
                a = line(lower[k], j)
                b = line(upper[k], j)
                lo = lo - a * back[0][j]
                mid = mid - a * back[1][j] - b * ahead[0][j]
                up = up - b * ahead[1][j]
                rt = rt - a * back[2][j] - b * ahead[2][j]
            new_lower.append(lo)
            new_upper.append(up)
            new_main.append(mid)
            new_right.append(rt)
        lower, upper, main, right = new_lower, new_upper, new_main, new_right
        stride *= 2
    (right,) = eliminate(main, [right])
    mine = zero
    for k in range(width):
        mine = jnp.where(place[0] == k, right[k], mine)
    out[...] = lane_pick(mine, place[2])


def final_kernel(depth, place, got, values, row_a, row_b, news, coarse, result, packs, out, sem):
    lane = lane_iota()
    sub = sub_iota()
    layers = out.shape[0] // 8
    quarters = layers // 64
    per_tile = 64 // depth
    add = coarse[...]
    even_row = place[2] % 2 == 0
    stride = quarters * 16 + 8
    left = pl.multiple_of(jnp.maximum(place[0] - 1, 0) * stride, 8)
    right = pl.multiple_of(jnp.minimum(place[0] + 1, place[1] - 1) * stride, 8)
    odd = (lane & 1) == 1
    has_left = odd & (place[0] > 0)
    has_right = jnp.logical_not(odd) & (place[0] + 1 < place[1])
    for n in range(quarters * 2):
        low = news[pl.ds(left + n * 8, 8), :]
        high = pltpu.roll(news[pl.ds(right + n * 8, 8), :], 126, 1)
        packs[n * 8 : n * 8 + 8, :] = jnp.where(has_left, low, jnp.where(has_right, high, 0.0))
    ends = (lane == 0) | (lane == 127)

    def some(quarter, carry):
        sides = [
            packs[pl.ds(pl.multiple_of((n * quarters + quarter) * 8, 8), 8), :] for n in range(2)
        ]
        for l in range(64):
            g = quarter * 64 + l
            part = quarter * per_tile + l // depth
            here = pl.ds(pl.multiple_of(g * 8, 8), 8)
            c = got[pl.ds(pl.multiple_of(part * (depth + 1) * 8 + l % depth * 8, 8), 8), :]
            v = values[here, :]
            pair = []
            for n, tile in enumerate((c * v, c)):
                at = pl.ds(n * layers + g, 1)
                low = jnp.where(even_row, row_b[at, :], row_a[at, :])
                high = jnp.where(even_row, row_a[at, :], row_b[at, :])
                tile = tile + jnp.where(sub == 0, low, jnp.where(sub == 7, high, 0.0))
                tile = tile + jnp.where(ends, pltpu.roll(sides[n], 127 - 2 * l, 1), 0.0)
                pair.append(tile)
            out[here, :] = pair[0] / pair[1] + add
        leave(quarter).start()
        return carry

    def leave(quarter):
        part = pl.ds(pl.multiple_of(quarter * 512, 512), 512)
        return pltpu.make_async_copy(out.at[part, :], result.at[part, :], sem.at[quarter])

    lax.fori_loop(0, quarters, some, 0)
    for quarter in range(quarters):
        leave(quarter).wait()


def partners(array, axis, odd):
    count = lax.axis_size(axis)
    pairs = [(i, i + 1) for i in range(odd, count - 1, 2)]
    return lax.ppermute(array, axis, pairs + [(j, i) for i, j in pairs])


def forward(array, axis):
    count = lax.axis_size(axis)
    return lax.ppermute(array, axis, [(i, i + 1) for i in range(count - 1)])


def shards(saturation, pressure, rock_class, rock_table, well_columns, well_rates, residual):
    depth, rows_all, cols = saturation.shape
    layers, brick_rows, _ = residual.shape
    wide, narrow = lax.axis_size("wide"), lax.axis_size("narrow")
    block = (depth, rows_all, cols)
    plane = (rows_all, cols)
    place = jnp.stack(
        [lax.axis_index("narrow"), jnp.int32(narrow), lax.axis_index("wide")]
    ).astype(jnp.int32)
    vmem = pl.BlockSpec(memory_space=pltpu.VMEM)
    smem = pl.BlockSpec(memory_space=pltpu.SMEM)
    far = pl.BlockSpec(memory_space=pltpu.HBM)

    sat, press, kinds, face_a, face_b, pack_a, pack_b = call(
        faces_kernel,
        [block] * 3 + [(3,) + plane] * 2 + [plane] * 2,
        scratch=[pltpu.VMEM(block, jnp.int32), pltpu.SemaphoreType.DMA((12,))],
        in_specs=[smem] + [far] * 3,
    )(
        place,
        *(
            pltpu.with_memory_space_constraint(array, pltpu.HBM)
            for array in (saturation, pressure, rock_class)
        ),
    )
    perm, wgain, ogain, frac = call(lookup_kernel, [block] * 4)(rock_table, kinds, sat)
    got_face_a = partners(face_a, "wide", 0)
    got_face_b = partners(face_b, "wide", 1)
    got_pack_a = partners(pack_a, "narrow", 0)
    got_pack_b = partners(pack_b, "narrow", 1)
    net, source, message = call(
        functools.partial(flow_kernel, narrow),
        [block, plane, (wide * narrow, 128)],
        scratch=[pltpu.VMEM(plane, F32)] * 2 + [pltpu.VMEM((depth, 8, cols), F32)] * 2,
        in_specs=[smem] + [vmem] * 13,
    )(
        place, rock_table, press, perm, frac, got_face_a, got_face_b, pack_a, pack_b, got_pack_a, got_pack_b,
        well_columns.reshape(1, -1), well_rates.reshape(1, -1), residual,
    )
    gathered = lax.all_to_all(message, ("wide", "narrow"), 0, 0, tiled=True)
    (ahead,) = call(told_kernel, [plane])(net, source)
    beside = forward(ahead, "narrow")
    (side,) = call(
        functools.partial(side_kernel, depth), [(4,) + plane], in_specs=[smem] + [vmem] * 3
    )(place, rock_table, got_pack_a, got_pack_b)
    chunk_rows = wide * (depth + 1) * 8
    sat_new, chunks = call(
        update_kernel,
        [block, (chunk_rows, 128)],
        scratch=[pltpu.VMEM(plane, F32)] * 3
        + [pltpu.VMEM(block, F32), pltpu.SemaphoreType.DMA((rows_all // 16,))],
        out_specs=[far, vmem],
    )(gathered, sat, net, source, perm, wgain, ogain, side, beside)
    got = lax.all_to_all(chunks, "wide", 0, 0, tiled=True)
    message_rows = narrow * (layers // 4 + 8)
    values, row_a, row_b, message = call(
        functools.partial(relax_kernel, depth),
        [(layers * 8 + 64, 128)] + [(2 * layers, 128)] * 2 + [(message_rows, 128)],
        scratch=[pltpu.VMEM((layers * 8 + 64, 128), F32)] * 5,
        in_specs=[smem, vmem, vmem],
    )(place, got, residual.reshape(layers * 8, 128))
    news = lax.all_to_all(message, "narrow", 0, 0, tiled=True)
    got_row_a = partners(row_a, "wide", 0)
    got_row_b = partners(row_b, "wide", 1)
    (rhs,) = call(functools.partial(rhs_kernel, wide), [(8, 128)])(gathered)
    (coarse,) = call(
        functools.partial(coarse_kernel, wide, narrow), [(8, 128)], in_specs=[smem, vmem, vmem]
    )(place, news, rhs)
    (precond,) = call(
        functools.partial(final_kernel, depth),
        [(layers * 8, 128)],
        scratch=[
            pltpu.VMEM((layers // 4, 128), F32),
            pltpu.VMEM((layers * 8, 128), F32),
            pltpu.SemaphoreType.DMA((layers // 64,)),
        ],
        in_specs=[smem] + [vmem] * 6,
        out_specs=[far],
    )(place, got, values, got_row_a, got_row_b, news, coarse)
    return (sat_new, precond.reshape(layers, brick_rows, cols))


def solution(mesh):
    placed = (
        P("wide", None, "narrow"),
        P("wide", None, "narrow"),
        P("wide", None, "narrow"),
        P(),
        P(),
        P(),
        P(None, "wide", "narrow"),
    )
    return jax.shard_map(
        shards,
        mesh=mesh,
        in_specs=placed,
        out_specs=(P("wide", None, "narrow"), P(None, "wide", "narrow")),
        check_vma=False,
    )
```

```python
import functools

import jax
import jax.numpy as jnp
from jax import lax
from jax.experimental import pallas as pl
from jax.experimental.pallas import tpu as pltpu
from jax.sharding import PartitionSpec as P

SWEEPS = 6
compress = 0.05
relax = 0.8
gravity = 0.5
courant = 0.5
tiny = 1e-06

F32 = jnp.float32
HIGH = lax.Precision.HIGHEST
PARAMS = pltpu.CompilerParams(vmem_limit_bytes=16 * 1024 * 1024)


def harmonic(low, high):
    return 2.0 * low * high / (low + high)


def sub_iota():
    return lax.broadcasted_iota(jnp.int32, (8, 128), 0)


def lane_iota():
    return lax.broadcasted_iota(jnp.int32, (8, 128), 1)


def lane_pick(tile, index):
    return jnp.take_along_axis(tile, jnp.full((8, 128), index, jnp.int32), axis=1)


def lane_take(tile, index):
    return jnp.take_along_axis(tile, index, axis=1, mode="promise_in_bounds")


def mobility(wg, og, s):
    water = wg * s * s
    return water, water + og * (1.0 - s) * (1.0 - s)


def lane_table(table, n):
    row = jnp.concatenate([table[n : n + 1, :], jnp.zeros((1, 112), F32)], axis=1)
    return jnp.broadcast_to(row, (8, 128))


def spread(tile, lane):
    return jnp.broadcast_to(tile[:, lane : lane + 1], (8, 128))


def call(kernel, outs, scratch=(), aliases=None, out_specs=None, in_specs=None, name=None):
    def run(*args):
        return pl.pallas_call(
            kernel,
            out_shape=[jax.ShapeDtypeStruct(shape, F32) for shape in outs],
            in_specs=in_specs or [pl.BlockSpec(memory_space=pltpu.VMEM)] * len(args),
            out_specs=out_specs or [pl.BlockSpec(memory_space=pltpu.VMEM)] * len(outs),
            scratch_shapes=list(scratch),
            input_output_aliases=aliases or {},
            compiler_params=PARAMS,
            name=name,
        )(*args)

    return run


def faces_kernel(
    place, sat_in, press_in, rock_in, sat, press, kinds, face_a, face_b, pack_a, pack_b, rock, sem
):
    lane = lane_iota()
    depth, rows_all, _ = sat.shape
    groups = 8
    each = rows_all // groups
    copies = []
    for g in range(groups):
        part = pl.ds(g * each, each)
        for n, (src, dst) in enumerate(((rock_in, rock), (sat_in, sat), (press_in, press))):
            copies.append(
                pltpu.make_async_copy(src.at[:, part, :], dst.at[:, part, :], sem.at[g * 3 + n])
            )
            copies[-1].start()
    even_row = place[2] % 2 == 0
    even_col = place[0] % 2 == 0

    def rows(step, carry):
        at = pl.ds(pl.multiple_of(step * 8, 8), 8)
        first = jnp.zeros((8, 128), F32)
        last = jnp.zeros((8, 128), F32)
        for d in range(depth):
            kind = rock[d, at, :].astype(F32) + 1.0
            kinds[d, at, :] = kind
            fields = (kind, sat[d, at, :], press[d, at, :])
            for n, field in enumerate(fields):
                spot = n * depth + d
                turned = pltpu.roll(field, spot + 1, 1)
                first = jnp.where(lane == spot + 1, turned, first)
                last = jnp.where(lane == spot, turned, last)
                if d == 0:
                    face_a[n, at, :] = field
                if d + 1 == depth:
                    low = face_a[n, at, :]
                    face_a[n, at, :] = jnp.where(even_row, field, low)
                    face_b[n, at, :] = jnp.where(even_row, low, field)
        first = pltpu.roll(first, 127, 1)
        pack_a[at, :] = jnp.where(even_col, last, first)
        pack_b[at, :] = jnp.where(even_col, first, last)
        return carry

    def two_rows(step, carry):
        return rows(2 * step + 1, rows(2 * step, carry))

    for g in range(groups):
        for copy in copies[g * 3 : g * 3 + 3]:
            copy.wait()
        lax.fori_loop(g * (each // 16), (g + 1) * (each // 16), two_rows, 0)


def rock_of(tables, kind, s):
    index = jnp.maximum(kind.astype(jnp.int32) - 1, 0)
    k, wg, og = [lane_take(table, index) for table in tables]
    water, both = mobility(wg, og, s)
    return jnp.where(kind > 0.5, k, 0.0), water / both


def columns_of(tables, depth, pack):
    lane = lane_iota()
    kind = jnp.where(lane < depth, pack, 0.0)
    k, f = rock_of(tables, kind, pltpu.roll(pack, 128 - depth, 1))
    return [pltpu.roll(pack, 128 - 2 * depth, 1), k, f]


def lookup_kernel(
    bricks, place, table, kinds, sat, pack_a, pack_b, columns, rates, residual,
    perm, wgain, ogain, frac, own_a, own_b, source, rest,
):
    depth, rows_all, cols = sat.shape
    tables = [lane_table(table, n) for n in range(3)]
    entries = [jnp.broadcast_to(table[2:3, m : m + 1], (8, 128)) for m in range(16)]

    def rows(step, carry):
        at = pl.ds(pl.multiple_of(step * 8, 8), 8)
        for d in range(depth):
            kind = kinds[d, at, :].astype(jnp.int32) - 1
            k = lane_take(tables[0], kind)
            wg = lane_take(tables[1], kind)
            values = entries
            for bit in range(4):
                taken = (kind & (1 << bit)) != 0
                values = [
                    jnp.where(taken, values[m + 1], values[m]) for m in range(0, len(values), 2)
                ]
            og = values[0]
            water, both = mobility(wg, og, sat[d, at, :])
            perm[d, at, :] = k
            wgain[d, at, :] = wg
            ogain[d, at, :] = og
            frac[d, at, :] = water / both
        for pack, own in ((pack_a, own_a), (pack_b, own_b)):
            for n, field in enumerate(columns_of(tables, depth, pack[at, :])):
                own[n, at, :] = field
        return carry

    lax.fori_loop(0, rows_all // 8, rows, 0)

    def add(step, sums):
        at = step * 8
        return tuple(s + residual[at + n] for n, s in enumerate(sums))

    sums = lax.fori_loop(0, residual.shape[0] // 8, add, (jnp.zeros((8, 128), F32),) * 8)
    total = sum(sums[1:], sums[0])
    rest[...] = jnp.broadcast_to(jnp.sum(total, keepdims=True), (8, 128))

    wells = columns.shape[1]
    spot = lax.broadcasted_iota(jnp.int32, (rows_all, wells), 0)
    apart = columns[...] - spot * (cols * bricks)
    in_row = jnp.where((apart >= 0) & (apart < cols * bricks), 1.0, 0.0)
    number = columns[...]
    well_col = number & (cols * bricks - 1) if (cols * bricks) & (cols * bricks - 1) == 0 else number % (cols * bricks)
    spot = lax.broadcasted_iota(jnp.int32, (cols, wells), 0)
    in_col = jnp.where(well_col - place[0] * cols == spot, rates[...], 0.0)
    source[...] = lax.dot_general(
        in_row, in_col, (((1,), (1,)), ((), ())), precision=HIGH, preferred_element_type=F32
    )


def flows(low, high, lift, keep=None):
    total = low[1] * high[1] / (low[1] + high[1]) * (low[0] - high[0] + lift)
    if keep is not None:
        total = jnp.where(keep, total, 0.0)
    return total, total * jnp.where(total > 0, low[2], high[2])


def flow_kernel(
    place, table, press, perm, frac, face_a, face_b, own_a, own_b, got_a, got_b,
    source, rest, net, ahead, message, qp, wp, rq, rw,
):
    lane = lane_iota()
    sub = sub_iota()
    depth, rows_all, cols = perm.shape
    tiles = rows_all // 8
    even_row = place[2] % 2 == 0
    even_col = place[0] % 2 == 0
    half = lane >> 1
    odd = (lane & 1) == 1
    tables = [lane_table(table, n) for n in range(3)]

    def edge(step, carry):
        at = pl.ds(pl.multiple_of(step * 8, 8), 8)

        mine_a, mine_b = [[ref[n, at, :] for n in range(3)] for ref in (own_a, own_b)]
        other_a, other_b = [columns_of(tables, depth, ref[at, :]) for ref in (got_a, got_b)]

        def choose(one, two):
            return [jnp.where(even_col, a, b) for a, b in zip(one, two)]

        left = flows(choose(other_b, other_a), choose(mine_b, mine_a), 0.0)
        right = flows(choose(mine_a, mine_b), choose(other_a, other_b), 0.0)
        for out, low, high in zip((qp, wp), left, right):
            out[at, :] = jnp.where(
                odd,
                jnp.take_along_axis(low, half, axis=1),
                jnp.take_along_axis(high, half, axis=1),
            )
        return carry

    def two_edges(step, carry):
        return edge(2 * step + 1, edge(2 * step, carry))

    lax.fori_loop(0, tiles // 2, two_edges, 0)
    rq[...] = jnp.zeros(rq.shape, F32)
    rw[...] = jnp.zeros(rw.shape, F32)

    def rows(step, top):
        begin = pl.multiple_of(step * 8, 8)
        at = pl.ds(begin, 8)
        beyond = pl.ds(pl.multiple_of(jnp.minimum(begin + 8, rows_all - 8), 8), 8)
        inner = (sub < 7) | (step < tiles - 1)
        edge_q, edge_w = qp[at, :], wp[at, :]
        kind, s, p = [jnp.where(even_row, face_b[n, at, :], face_a[n, at, :]) for n in range(3)]
        below = [p, *rock_of(tables, kind, s)]
        kind, s, p = [jnp.where(even_row, face_a[n, at, :], face_b[n, at, :]) for n in range(3)]
        above = [p, *rock_of(tables, kind, s)]
        cur = [ref[0, at, :] for ref in (press, perm, frac)]
        depth_q, depth_w = flows(below, cur, gravity)
        told = jnp.where(
            (lane >= depth) & (lane < 2 * depth), spread(source[at, :], 127), 0.0
        )
        for d in range(depth):
            nxt = [ref[d + 1, at, :] for ref in (press, perm, frac)] if d + 1 < depth else above
            q, w = flows(cur, nxt, gravity)
            net_sum = w - depth_w
            out = jnp.maximum(q, 0.0) - jnp.minimum(depth_q, 0.0)
            depth_q, depth_w = q, w
            up = [
                pltpu.roll(jnp.where(sub == 0, ref[d, beyond, :], x), 7, 0)
                for ref, x in zip((press, perm, frac), cur)
            ]
            q, w = flows(cur, up, 0.0, inner)
            q_roll, w_roll = pltpu.roll(q, 1, 0), pltpu.roll(w, 1, 0)
            low_q = jnp.where(sub == 0, rq[d], q_roll)
            low_w = jnp.where(sub == 0, rw[d], w_roll)
            rq[d] = q_roll
            rw[d] = w_roll
            net_sum = net_sum + (w - low_w)
            out = out + (jnp.maximum(q, 0.0) - jnp.minimum(low_q, 0.0))
            q, w = flows(cur, [pltpu.roll(x, 127, 1) for x in cur], 0.0)
            side_q = pltpu.roll(edge_q, 127 - 2 * d, 1)
            side_w = pltpu.roll(edge_w, 127 - 2 * d, 1)
            low_q = jnp.where(lane == 0, side_q, pltpu.roll(q, 1, 1))
            low_w = jnp.where(lane == 0, side_w, pltpu.roll(w, 1, 1))
            q = jnp.where(lane == 127, side_q, q)
            w = jnp.where(lane == 127, side_w, w)
            net_sum = 2.0 * (net_sum + (w - low_w))
            net[d, at, :] = net_sum
            told = jnp.where(lane == d, pltpu.roll(net_sum, d + 1, 1), told)
            out = out + (jnp.maximum(q, 0.0) - jnp.minimum(low_q, 0.0))
            top = jnp.maximum(top, out)
            cur = nxt
        ahead[at, :] = told
        return top

    top = lax.fori_loop(0, tiles, rows, jnp.zeros((8, 128), F32))

    message[...] = jnp.where(
        lax.broadcasted_iota(jnp.int32, message.shape, 1) == 0,
        2.0 * jnp.max(top),
        rest[0:1, :],
    )


def update_kernel(
    place, gathered, table, sat, net, source, perm, wgain, ogain, got_a, got_b, beside,
    new_out, chunks, cell_sum, row_sum, col_sum, new, sem,
):
    lane = lane_iota()
    depth, rows_all, _ = sat.shape
    tiles = rows_all // 8
    stride = (depth + 1) * 8
    spot = lax.broadcasted_iota(jnp.int32, gathered.shape, 1)
    top = jnp.max(jnp.where(spot == 0, gathered[...], 0.0), keepdims=True)
    step_size = jnp.broadcast_to(courant / (top + tiny), (8, 128))
    even_col = place[0] % 2 == 0
    tables = [lane_table(table, n) for n in range(3)]

    def coefficient(k, wg, og, s):
        return k * (wg * s * s + og * (1.0 - s) * (1.0 - s))

    def rows(step, carry):
        at = pl.ds(pl.multiple_of(step * 8, 8), 8)
        begin = step * stride
        add = step_size * source[at, :]
        total = jnp.zeros((8, 128), F32)
        first = jnp.zeros((8, 128), F32)
        for d in range(depth):
            s = sat[d, at, :] - step_size * net[d, at, :] + add
            new[d, at, :] = s
            c = coefficient(perm[d, at, :], wgain[d, at, :], ogain[d, at, :], s)
            chunks[pl.ds(pl.multiple_of(begin + d * 8, 8), 8), :] = c
            total = total + c
            first = jnp.where(lane == d, pltpu.roll(c, d, 1) if d else c, first)
        cell_sum[at, :] = total
        tile = jnp.where(even_col, got_b[at, :], got_a[at, :])
        flow = beside[at, :]
        kind = jnp.where(lane < depth, tile, 0.0)
        index = jnp.maximum(kind.astype(jnp.int32) - 1, 0)
        k, wg, og = [lane_take(each, index) for each in tables]
        s = pltpu.roll(tile, 128 - depth, 1) - step_size * flow
        s = s + step_size * pltpu.roll(flow, 128 - depth, 1)
        c = coefficient(jnp.where(kind > 0.5, k, 0.0), wg, og, s)
        col_sum[at, :] = jnp.where(lane < depth, harmonic(c, first), 0.0)
        return carry

    def two_rows(step, carry):
        rows(2 * step + 1, rows(2 * step, carry))
        leave(step).start()
        return carry

    def leave(step):
        part = pl.ds(pl.multiple_of(step * 16, 16), 16)
        return pltpu.make_async_copy(new.at[:, part, :], new_out.at[:, part, :], sem.at[step])

    lax.fori_loop(0, tiles // 2, two_rows, 0)
    row_sum[0:8, :] = jnp.zeros((8, 128), F32)
    for p in range(1, tiles):
        total = jnp.zeros((8, 128), F32)
        for half in range(depth // 8):
            low = chunks[pl.ds((p - 1) * stride + half * 64 + 7, 8, stride=8), :]
            high = chunks[pl.ds(p * stride + half * 64, 8, stride=8), :]
            total = total + harmonic(low, high)
        row_sum[p * 8 : p * 8 + 8, :] = total
    brick = lax.broadcasted_iota(jnp.int32, (rows_all, 128), 0) // 8
    spot = lax.broadcasted_iota(jnp.int32, (rows_all, 128), 1)
    total = jnp.zeros((1, 128), F32)
    for n, part in enumerate((cell_sum, row_sum, col_sum)):
        each = jnp.sum(part[...], axis=1, keepdims=True)
        placed = jnp.where(spot == n * 16 + brick, each, 0.0)
        total = total + jnp.sum(placed, axis=0, keepdims=True)
    for p in range(tiles):
        chunks[p * stride + depth * 8 : (p + 1) * stride, :] = jnp.broadcast_to(total, (8, 128))
    for step in range(tiles // 2):
        leave(step).wait()


def relax_kernel(depth, place, got, residual, values, row_a, row_b, message, fd, fr, fc, gain, base):
    lane = lane_iota()
    sub = sub_iota()
    layers = residual.shape[0] // 8
    parts = layers // depth
    zero = jnp.zeros((8, 128), F32)
    fd[0:8, :] = zero
    values[layers * 8 :, :] = jnp.zeros((64, 128), F32)
    fc[layers * 8 :, :] = jnp.zeros((64, 128), F32)
    even_row = place[2] % 2 == 0

    def half_face(low, high):
        return low * high / (low + high)

    def part(w, carry):
        below, total = carry
        begin = w * (depth + 1) * 8
        place_w = w * depth * 8
        after = jnp.minimum(w + 1, parts - 1) * (depth + 1) * 8
        c = got[pl.ds(pl.multiple_of(begin, 8), 8), :]
        for d in range(depth):
            here = pl.ds(pl.multiple_of(place_w + d * 8, 8), 8)
            if d + 1 < depth:
                c_next = got[pl.ds(pl.multiple_of(begin + d * 8 + 8, 8), 8), :]
                above = half_face(c, c_next)
            else:
                c_next = got[pl.ds(pl.multiple_of(after, 8), 8), :]
                above = jnp.where(w + 1 < parts, half_face(c, c_next), 0.0)
            row = jnp.where(sub == 0, 0.0, half_face(pltpu.roll(c, 1, 0), c))
            col = jnp.where(lane == 0, 0.0, half_face(pltpu.roll(c, 1, 1), c))
            diag = (
                (0.5 * compress) * c + below + above
                + row + pltpu.roll(row, 7, 0) + col + pltpu.roll(col, 127, 1)
            )
            scale = relax / diag
            fd[pl.ds(pl.multiple_of(place_w + d * 8 + 8, 8), 8), :] = above
            fr[here, :] = row
            fc[here, :] = col
            gain[here, :] = scale
            first = (0.5 * scale) * residual[here, :]
            base[here, :] = first
            values[here, :] = first
            c, below = c_next, above
        total = total + got[pl.ds(pl.multiple_of(begin + depth * 8, 8), 8), :]
        return below, total

    def build(step, carry):
        return part(2 * step + 1, part(2 * step, carry))

    _, total = lax.fori_loop(0, parts // 2, build, (zero, zero))

    block = 32

    def sweep(number, carry):
        def some(step, prev):
            begin = step * (block * 8)
            v = values[pl.ds(pl.multiple_of(begin, 8), 8), :]
            for n in range(block):
                here = pl.ds(pl.multiple_of(begin + n * 8, 8), 8)
                above = pl.ds(pl.multiple_of(begin + n * 8 + 8, 8), 8)
                v_next = values[above, :]
                row = fr[here, :]
                col = fc[here, :]
                total = fd[here, :] * prev + fd[above, :] * v_next
                total = total + (row * pltpu.roll(v, 1, 0) + pltpu.roll(row * v, 7, 0))
                total = total + (col * pltpu.roll(v, 1, 1) + pltpu.roll(col * v, 127, 1))
                values[here, :] = ((1.0 - relax) * v + base[here, :]) + gain[here, :] * total
                prev, v = v, v_next
            return prev

        lax.fori_loop(0, layers // block, some, zero)
        return carry

    lax.fori_loop(0, SWEEPS - 1, sweep, 0)

    for w in range(parts):
        for half in range(depth // 8):
            at = w * (depth + 1) * 8 + half * 64
            spot = w * depth + half * 8
            pairs = []
            for row in (0, 7):
                c = got[pl.ds(at + row, 8, stride=8), :]
                v = values[pl.ds(spot * 8 + row, 8, stride=8), :]
                pairs.append((c * v, c))
            for n in range(2):
                low, high = pairs[0][n], pairs[1][n]
                rows = slice(n * layers + spot, n * layers + spot + 8)
                row_a[rows, :] = jnp.where(even_row, high, low)
                row_b[rows, :] = jnp.where(even_row, low, high)

    quarters = layers // 64
    per_tile = 64 // depth
    peers = message.shape[0] // (quarters * 16 + 8)

    def pack(quarter, carry):
        packed = [zero, zero]
        for l in range(64):
            part = quarter * per_tile + l // depth
            c = got[pl.ds(pl.multiple_of(part * (depth + 1) * 8 + l % depth * 8, 8), 8), :]
            v = values[pl.ds(pl.multiple_of(quarter * 512 + l * 8, 8), 8), :]
            spot = (2 * l + 2) % 128
            mark = (lane == 2 * l + 1) | (lane == spot)
            for n, tile in enumerate((c * v, c)):
                turned = pltpu.roll(tile, spot, 1) if spot else tile
                packed[n] = jnp.where(mark, turned, packed[n])
        for peer in range(peers):
            for n in range(2):
                begin = peer * (quarters * 16 + 8) + (n * quarters + quarter) * 8
                message[pl.ds(pl.multiple_of(begin, 8), 8), :] = packed[n]
        return carry

    lax.fori_loop(0, quarters, pack, 0)
    for peer in range(peers):
        begin = peer * (quarters * 16 + 8) + quarters * 16
        message[begin : begin + 8, :] = total


def coarse_kernel(count, place, news, gathered, out):
    lane = lane_iota()
    sub = sub_iota()
    inside = lane < count
    width = gathered.shape[0] // count
    stride = news.shape[0] // width
    sums = jnp.zeros((8, 128), F32)
    for k in range(width):
        sums = jnp.where(sub == k, news[(k + 1) * stride - 8 : (k + 1) * stride, :], sums)
    cells = jnp.where(inside, sums, 0.0)
    low_row = jnp.where(inside, pltpu.roll(sums, 128 - 16, 1), 0.0)
    low_col = jnp.where(inside, pltpu.roll(sums, 128 - 32, 1), 0.0)
    low_row = jnp.where(lane == 0, 0.0, low_row)
    low_col = jnp.where(sub == 0, 0.0, low_col)
    high_row = pltpu.roll(low_row, 127, 1)
    high_col = pltpu.roll(low_col, 7, 0)
    diagonal = jnp.where(inside, compress * cells + low_row + high_row + low_col + high_col, 1.0)
    rhs = jnp.zeros((8, 128), F32)
    for p in range(count):
        rhs = jnp.where(lane == p, spread(gathered[p * width : p * width + width, :], 1), rhs)

    def line(tile, k):
        return jnp.broadcast_to(tile[k : k + 1, :], (8, 128))

    zero = jnp.zeros((8, 128), F32)
    main, lower, upper, right = [], [], [], []
    for k in range(width):
        row = jnp.where(sub == k, line(diagonal, k), zero)
        if k > 0:
            row = jnp.where(sub == k - 1, -line(low_col, k), row)
        if k + 1 < width:
            row = jnp.where(sub == k + 1, -line(low_col, k + 1), row)
        main.append(row)
        lower.append(jnp.where(sub == k, -line(low_row, k), zero))
        upper.append(jnp.where(sub == k, -line(high_row, k), zero))
        right.append(line(rhs, k))

    def eliminate(main, others):
        main = list(main)
        others = [list(rows) for rows in others]
        for k in range(width):
            inverse = 1.0 / line(main[k], k)
            main[k] = main[k] * inverse
            for rows in others:
                rows[k] = rows[k] * inverse
            for j in range(width):
                if j != k:
                    factor = line(main[j], k)
                    main[j] = main[j] - factor * main[k]
                    for rows in others:
                        rows[j] = rows[j] - factor * rows[k]
        return others

    stride = 1
    while stride < count:
        solved = eliminate(main, [lower, upper, right])
        back = [[pltpu.roll(x, stride, 1) for x in rows] for rows in solved]
        ahead = [[pltpu.roll(x, 128 - stride, 1) for x in rows] for rows in solved]
        new_lower, new_upper, new_main, new_right = [], [], [], []
        for k in range(width):
            lo, up, mid, rt = zero, zero, main[k], right[k]
            for j in [k] if stride == 1 else range(width):
                a = line(lower[k], j)
                b = line(upper[k], j)
                if 2 * stride < count:
                    lo = lo - a * back[0][j]
                    up = up - b * ahead[1][j]
                mid = mid - a * back[1][j] - b * ahead[0][j]
                rt = rt - a * back[2][j] - b * ahead[2][j]
            new_lower.append(lo)
            new_upper.append(up)
            new_main.append(mid)
            new_right.append(rt)
        lower, upper, main, right = new_lower, new_upper, new_main, new_right
        stride *= 2
    (right,) = eliminate(main, [right])
    mine = zero
    for k in range(width):
        mine = jnp.where(place[0] == k, right[k], mine)
    out[...] = lane_pick(mine, place[2])


def final_kernel(depth, place, got, values, row_a, row_b, news, coarse, result, packs, out, sem):
    lane = lane_iota()
    sub = sub_iota()
    layers = out.shape[0] // 8
    quarters = layers // 64
    per_tile = 64 // depth
    add = coarse[...]
    even_row = place[2] % 2 == 0
    stride = quarters * 16 + 8
    left = pl.multiple_of(jnp.maximum(place[0] - 1, 0) * stride, 8)
    right = pl.multiple_of(jnp.minimum(place[0] + 1, place[1] - 1) * stride, 8)
    odd = (lane & 1) == 1
    has_left = odd & (place[0] > 0)
    has_right = jnp.logical_not(odd) & (place[0] + 1 < place[1])
    for n in range(quarters * 2):
        low = news[pl.ds(left + n * 8, 8), :]
        high = pltpu.roll(news[pl.ds(right + n * 8, 8), :], 126, 1)
        packs[n * 8 : n * 8 + 8, :] = jnp.where(has_left, low, jnp.where(has_right, high, 0.0))
    ends = (lane == 0) | (lane == 127)

    def some(quarter, carry):
        sides = [
            packs[pl.ds(pl.multiple_of((n * quarters + quarter) * 8, 8), 8), :] for n in range(2)
        ]
        for l in range(64):
            g = quarter * 64 + l
            part = quarter * per_tile + l // depth
            here = pl.ds(pl.multiple_of(g * 8, 8), 8)
            c = got[pl.ds(pl.multiple_of(part * (depth + 1) * 8 + l % depth * 8, 8), 8), :]
            v = values[here, :]
            pair = []
            for n, tile in enumerate((c * v, c)):
                at = pl.ds(n * layers + g, 1)
                low = jnp.where(even_row, row_b[at, :], row_a[at, :])
                high = jnp.where(even_row, row_a[at, :], row_b[at, :])
                tile = tile + jnp.where(sub == 0, low, jnp.where(sub == 7, high, 0.0))
                tile = tile + jnp.where(ends, pltpu.roll(sides[n], 127 - 2 * l, 1), 0.0)
                pair.append(tile)
            out[here, :] = pair[0] / pair[1] + add
        leave(quarter).start()
        return carry

    def leave(quarter):
        part = pl.ds(pl.multiple_of(quarter * 512, 512), 512)
        return pltpu.make_async_copy(out.at[part, :], result.at[part, :], sem.at[quarter])

    lax.fori_loop(0, quarters, some, 0)
    for quarter in range(quarters):
        leave(quarter).wait()


def partners(array, axis, odd):
    count = lax.axis_size(axis)
    pairs = [(i, i + 1) for i in range(odd, count - 1, 2)]
    return lax.ppermute(array, axis, pairs + [(j, i) for i, j in pairs])


def forward(array, axis):
    count = lax.axis_size(axis)
    return lax.ppermute(array, axis, [(i, i + 1) for i in range(count - 1)])


def shards(saturation, pressure, rock_class, rock_table, well_columns, well_rates, residual):
    depth, rows_all, cols = saturation.shape
    layers, brick_rows, _ = residual.shape
    wide, narrow = lax.axis_size("wide"), lax.axis_size("narrow")
    block = (depth, rows_all, cols)
    plane = (rows_all, cols)
    place = jnp.stack(
        [lax.axis_index("narrow"), jnp.int32(narrow), lax.axis_index("wide")]
    ).astype(jnp.int32)
    vmem = pl.BlockSpec(memory_space=pltpu.VMEM)
    smem = pl.BlockSpec(memory_space=pltpu.SMEM)
    far = pl.BlockSpec(memory_space=pltpu.HBM)

    sat, press, kinds, face_a, face_b, pack_a, pack_b = call(
        faces_kernel,
        [block] * 3 + [(3,) + plane] * 2 + [plane] * 2,
        scratch=[pltpu.VMEM(block, jnp.int32), pltpu.SemaphoreType.DMA((24,))],
        in_specs=[smem] + [far] * 3,
        name="faces",
    )(
        place,
        *(
            pltpu.with_memory_space_constraint(array, pltpu.HBM)
            for array in (saturation, pressure, rock_class)
        ),
    )
    perm, wgain, ogain, frac, own_a, own_b, source, rest = call(
        functools.partial(lookup_kernel, narrow),
        [block] * 4 + [(3,) + plane] * 2 + [plane, (8, 128)],
        in_specs=[smem] + [vmem] * 8,
        name="lookup",
    )(
        place, rock_table, kinds, sat, pack_a, pack_b,
        well_columns.reshape(1, -1), well_rates.reshape(1, -1), residual,
    )
    got_face_a = partners(face_a, "wide", 0)
    got_face_b = partners(face_b, "wide", 1)
    got_pack_b = partners(pack_b, "narrow", 1)
    got_pack_a = partners(pack_a, "narrow", 0)
    net, ahead, message = call(
        flow_kernel,
        [block, plane, (wide * narrow, 128)],
        scratch=[pltpu.VMEM(plane, F32)] * 2 + [pltpu.VMEM((depth, 8, cols), F32)] * 2,
        in_specs=[smem] + [vmem] * 12,
        name="flow",
    )(
        place, rock_table, press, perm, frac, got_face_a, got_face_b, own_a, own_b,
        got_pack_a, got_pack_b, source, rest,
    )
    beside = forward(ahead, "narrow")
    gathered = lax.all_to_all(message, ("wide", "narrow"), 0, 0, tiled=True)
    chunk_rows = wide * (depth + 1) * 8
    sat_new, chunks = call(
        update_kernel,
        [block, (chunk_rows, 128)],
        scratch=[pltpu.VMEM(plane, F32)] * 3
        + [pltpu.VMEM(block, F32), pltpu.SemaphoreType.DMA((rows_all // 16,))],
        in_specs=[smem] + [vmem] * 11,
        out_specs=[far, vmem],
        name="update",
    )(
        place, gathered, rock_table, sat, net, source, perm, wgain, ogain, got_pack_a, got_pack_b,
        beside,
    )
    got = lax.all_to_all(chunks, "wide", 0, 0, tiled=True)
    message_rows = narrow * (layers // 4 + 8)
    values, row_a, row_b, message = call(
        functools.partial(relax_kernel, depth),
        [(layers * 8 + 64, 128)] + [(2 * layers, 128)] * 2 + [(message_rows, 128)],
        scratch=[pltpu.VMEM((layers * 8 + 64, 128), F32)] * 5,
        in_specs=[smem, vmem, vmem],
        name="relaxation",
    )(place, got, residual.reshape(layers * 8, 128))
    got_row_a = partners(row_a, "wide", 0)
    got_row_b = partners(row_b, "wide", 1)
    news = lax.all_to_all(message, "narrow", 0, 0, tiled=True)
    (coarse,) = call(
        functools.partial(coarse_kernel, wide),
        [(8, 128)],
        in_specs=[smem, vmem, vmem],
        name="coarse",
    )(place, news, gathered)
    (precond,) = call(
        functools.partial(final_kernel, depth),
        [(layers * 8, 128)],
        scratch=[
            pltpu.VMEM((layers // 4, 128), F32),
            pltpu.VMEM((layers * 8, 128), F32),
            pltpu.SemaphoreType.DMA((layers // 64,)),
        ],
        in_specs=[smem] + [vmem] * 6,
        out_specs=[far],
        name="final",
    )(place, got, values, got_row_a, got_row_b, news, coarse)
    return (sat_new, precond.reshape(layers, brick_rows, cols))


def solution(mesh):
    placed = (
        P("wide", None, "narrow"),
        P("wide", None, "narrow"),
        P("wide", None, "narrow"),
        P(),
        P(),
        P(),
        P(None, "wide", "narrow"),
    )
    return jax.shard_map(
        shards,
        mesh=mesh,
        in_specs=placed,
        out_specs=(P("wide", None, "narrow"), P(None, "wide", "narrow")),
        check_vma=False,
    )
```

```python
import functools

import jax
import jax.numpy as jnp
from jax import lax
from jax.experimental import pallas as pl
from jax.experimental.pallas import tpu as pltpu
from jax.sharding import PartitionSpec as P


SWEEPS = 6
compress = 0.05
relax = 0.8
gravity = 0.5
courant = 0.5
tiny = 1e-06

F32 = jnp.float32
HIGH = lax.Precision.HIGHEST
PARAMS = pltpu.CompilerParams(vmem_limit_bytes=16 * 1024 * 1024)


def harmonic(low, high):
    return 2.0 * low * high / (low + high)


def sub_iota():
    return lax.broadcasted_iota(jnp.int32, (8, 128), 0)


def lane_iota():
    return lax.broadcasted_iota(jnp.int32, (8, 128), 1)


def lane_pick(tile, index):
    return jnp.take_along_axis(tile, jnp.full((8, 128), index, jnp.int32), axis=1)


def lane_take(tile, index):
    return jnp.take_along_axis(tile, index, axis=1, mode="promise_in_bounds")


def mobility(wg, og, s):
    water = wg * s * s
    return water, water + og * (1.0 - s) * (1.0 - s)


def lane_table(table, n):
    row = jnp.concatenate([table[n : n + 1, :], jnp.zeros((1, 112), F32)], axis=1)
    return jnp.broadcast_to(row, (8, 128))


def spread(tile, lane):
    return jnp.broadcast_to(tile[:, lane : lane + 1], (8, 128))


def call(kernel, outs, scratch=(), aliases=None, out_specs=None, in_specs=None):
    def run(*args):
        return pl.pallas_call(
            kernel,
            out_shape=[jax.ShapeDtypeStruct(shape, F32) for shape in outs],
            in_specs=in_specs or [pl.BlockSpec(memory_space=pltpu.VMEM)] * len(args),
            out_specs=out_specs or [pl.BlockSpec(memory_space=pltpu.VMEM)] * len(outs),
            scratch_shapes=list(scratch),
            input_output_aliases=aliases or {},
            compiler_params=PARAMS,
        )(*args)

    return run


def faces_kernel(
    place, sat_in, press_in, rock_in, sat, press, kinds, face_a, face_b, pack_a, pack_b, rock, sem
):
    lane = lane_iota()
    depth, rows_all, _ = sat.shape
    groups = 8
    each = rows_all // groups
    copies = []
    for g in range(groups):
        part = pl.ds(g * each, each)
        for n, (src, dst) in enumerate(((rock_in, rock), (sat_in, sat), (press_in, press))):
            copies.append(
                pltpu.make_async_copy(src.at[:, part, :], dst.at[:, part, :], sem.at[g * 3 + n])
            )
            copies[-1].start()
    even_row = place[2] % 2 == 0
    even_col = place[0] % 2 == 0

    def rows(step, carry):
        at = pl.ds(pl.multiple_of(step * 8, 8), 8)
        first = jnp.zeros((8, 128), F32)
        last = jnp.zeros((8, 128), F32)
        for d in range(depth):
            kind = rock[d, at, :].astype(F32) + 1.0
            kinds[d, at, :] = kind
            fields = (kind, sat[d, at, :], press[d, at, :])
            for n, field in enumerate(fields):
                spot = n * depth + d
                turned = pltpu.roll(field, spot + 1, 1)
                first = jnp.where(lane == spot + 1, turned, first)
                last = jnp.where(lane == spot, turned, last)
                if d == 0:
                    face_a[n, at, :] = field
                if d + 1 == depth:
                    low = face_a[n, at, :]
                    face_a[n, at, :] = jnp.where(even_row, field, low)
                    face_b[n, at, :] = jnp.where(even_row, low, field)
        first = pltpu.roll(first, 127, 1)
        pack_a[at, :] = jnp.where(even_col, last, first)
        pack_b[at, :] = jnp.where(even_col, first, last)
        return carry

    def two_rows(step, carry):
        return rows(2 * step + 1, rows(2 * step, carry))

    for g in range(groups):
        for copy in copies[g * 3 : g * 3 + 3]:
            copy.wait()
        lax.fori_loop(g * (each // 16), (g + 1) * (each // 16), two_rows, 0)


def rock_of(tables, kind, s):
    index = jnp.maximum(kind.astype(jnp.int32) - 1, 0)
    k, wg, og = [lane_take(table, index) for table in tables]
    water, both = mobility(wg, og, s)
    return jnp.where(kind > 0.5, k, 0.0), water / both


def columns_of(tables, depth, pack):
    lane = lane_iota()
    kind = jnp.where(lane < depth, pack, 0.0)
    k, f = rock_of(tables, kind, pltpu.roll(pack, 128 - depth, 1))
    return [pltpu.roll(pack, 128 - 2 * depth, 1), k, f]


def lookup_kernel(
    bricks, place, table, kinds, sat, pack_a, pack_b, columns, rates, residual,
    perm, wgain, ogain, frac, own_a, own_b, source, rest,
):
    depth, rows_all, cols = sat.shape
    tables = [lane_table(table, n) for n in range(3)]
    entries = [jnp.broadcast_to(table[2:3, m : m + 1], (8, 128)) for m in range(16)]

    def rows(step, carry):
        at = pl.ds(pl.multiple_of(step * 8, 8), 8)
        for d in range(depth):
            kind = kinds[d, at, :].astype(jnp.int32) - 1
            k = lane_take(tables[0], kind)
            wg = lane_take(tables[1], kind)
            values = entries
            for bit in range(4):
                taken = (kind & (1 << bit)) != 0
                values = [
                    jnp.where(taken, values[m + 1], values[m]) for m in range(0, len(values), 2)
                ]
            og = values[0]
            water, both = mobility(wg, og, sat[d, at, :])
            perm[d, at, :] = k
            wgain[d, at, :] = wg
            ogain[d, at, :] = og
            frac[d, at, :] = water / both
        for pack, own in ((pack_a, own_a), (pack_b, own_b)):
            for n, field in enumerate(columns_of(tables, depth, pack[at, :])):
                own[n, at, :] = field
        return carry

    lax.fori_loop(0, rows_all // 8, rows, 0)

    def add(step, sums):
        at = step * 8
        return tuple(s + residual[at + n] for n, s in enumerate(sums))

    sums = lax.fori_loop(0, residual.shape[0] // 8, add, (jnp.zeros((8, 128), F32),) * 8)
    total = sum(sums[1:], sums[0])
    rest[...] = jnp.broadcast_to(jnp.sum(total, keepdims=True), (8, 128))

    wells = columns.shape[1]
    spot = lax.broadcasted_iota(jnp.int32, (rows_all, wells), 0)
    apart = columns[...] - spot * (cols * bricks)
    in_row = jnp.where((apart >= 0) & (apart < cols * bricks), 1.0, 0.0)
    number = columns[...]
    well_col = number & (cols * bricks - 1) if (cols * bricks) & (cols * bricks - 1) == 0 else number % (cols * bricks)
    spot = lax.broadcasted_iota(jnp.int32, (cols, wells), 0)
    in_col = jnp.where(well_col - place[0] * cols == spot, rates[...], 0.0)
    source[...] = lax.dot_general(
        in_row, in_col, (((1,), (1,)), ((), ())), precision=HIGH, preferred_element_type=F32
    )


def flows(low, high, lift, keep=None):
    total = low[1] * high[1] / (low[1] + high[1]) * (low[0] - high[0] + lift)
    if keep is not None:
        total = jnp.where(keep, total, 0.0)
    return total, total * jnp.where(total > 0, low[2], high[2])


def flow_kernel(
    place, table, press, perm, frac, face_a, face_b, own_a, own_b, got_a, got_b,
    source, rest, net, ahead, message, qp, wp, rq, rw,
):
    lane = lane_iota()
    sub = sub_iota()
    depth, rows_all, _ = perm.shape
    tiles = rows_all // 8
    even_row = place[2] % 2 == 0
    even_col = place[0] % 2 == 0
    half = lane >> 1
    odd = (lane & 1) == 1
    tables = [lane_table(table, n) for n in range(3)]

    def edge(step, carry):
        at = pl.ds(pl.multiple_of(step * 8, 8), 8)

        mine_a, mine_b = [[ref[n, at, :] for n in range(3)] for ref in (own_a, own_b)]
        other_a, other_b = [columns_of(tables, depth, ref[at, :]) for ref in (got_a, got_b)]

        def choose(one, two):
            return [jnp.where(even_col, a, b) for a, b in zip(one, two)]

        left = flows(choose(other_b, other_a), choose(mine_b, mine_a), 0.0)
        right = flows(choose(mine_a, mine_b), choose(other_a, other_b), 0.0)
        for out, low, high in zip((qp, wp), left, right):
            out[at, :] = jnp.where(
                odd,
                jnp.take_along_axis(low, half, axis=1),
                jnp.take_along_axis(high, half, axis=1),
            )
        return carry

    def two_edges(step, carry):
        return edge(2 * step + 1, edge(2 * step, carry))

    lax.fori_loop(0, tiles // 2, two_edges, 0)
    rq[...] = jnp.zeros(rq.shape, F32)
    rw[...] = jnp.zeros(rw.shape, F32)

    def rows(step, top):
        begin = pl.multiple_of(step * 8, 8)
        at = pl.ds(begin, 8)
        beyond = pl.ds(pl.multiple_of(jnp.minimum(begin + 8, rows_all - 8), 8), 8)
        inner = (sub < 7) | (step < tiles - 1)
        edge_q, edge_w = qp[at, :], wp[at, :]
        kind, s, p = [jnp.where(even_row, face_b[n, at, :], face_a[n, at, :]) for n in range(3)]
        below = [p, *rock_of(tables, kind, s)]
        kind, s, p = [jnp.where(even_row, face_a[n, at, :], face_b[n, at, :]) for n in range(3)]
        above = [p, *rock_of(tables, kind, s)]
        cur = [ref[0, at, :] for ref in (press, perm, frac)]
        depth_q, depth_w = flows(below, cur, gravity)
        told = jnp.where(
            (lane >= depth) & (lane < 2 * depth), spread(source[at, :], 127), 0.0
        )
        for d in range(depth):
            nxt = [ref[d + 1, at, :] for ref in (press, perm, frac)] if d + 1 < depth else above
            q, w = flows(cur, nxt, gravity)
            net_sum = w - depth_w
            out = jnp.maximum(q, 0.0) - jnp.minimum(depth_q, 0.0)
            depth_q, depth_w = q, w
            up = [
                pltpu.roll(jnp.where(sub == 0, ref[d, beyond, :], x), 7, 0)
                for ref, x in zip((press, perm, frac), cur)
            ]
            q, w = flows(cur, up, 0.0, inner)
            q_roll, w_roll = pltpu.roll(q, 1, 0), pltpu.roll(w, 1, 0)
            low_q = jnp.where(sub == 0, rq[d], q_roll)
            low_w = jnp.where(sub == 0, rw[d], w_roll)
            rq[d] = q_roll
            rw[d] = w_roll
            net_sum = net_sum + (w - low_w)
            out = out + (jnp.maximum(q, 0.0) - jnp.minimum(low_q, 0.0))
            q, w = flows(cur, [pltpu.roll(x, 127, 1) for x in cur], 0.0)
            side_q = pltpu.roll(edge_q, 127 - 2 * d, 1)
            side_w = pltpu.roll(edge_w, 127 - 2 * d, 1)
            low_q = jnp.where(lane == 0, side_q, pltpu.roll(q, 1, 1))
            low_w = jnp.where(lane == 0, side_w, pltpu.roll(w, 1, 1))
            q = jnp.where(lane == 127, side_q, q)
            w = jnp.where(lane == 127, side_w, w)
            net_sum = 2.0 * (net_sum + (w - low_w))
            net[d, at, :] = net_sum
            told = jnp.where(lane == d, pltpu.roll(net_sum, d + 1, 1), told)
            out = out + (jnp.maximum(q, 0.0) - jnp.minimum(low_q, 0.0))
            top = jnp.maximum(top, out)
            cur = nxt
        ahead[at, :] = told
        return top

    top = lax.fori_loop(0, tiles, rows, jnp.zeros((8, 128), F32))

    message[...] = jnp.where(
        lax.broadcasted_iota(jnp.int32, message.shape, 1) == 0,
        2.0 * jnp.max(top),
        rest[0:1, :],
    )


def update_kernel(
    place, gathered, table, sat, net, source, perm, wgain, ogain, got_a, got_b, beside,
    new, chunks, cell_sum, row_sum, col_sum,
):
    lane = lane_iota()
    depth, rows_all, _ = sat.shape
    tiles = rows_all // 8
    stride = (depth + 1) * 8
    spot = lax.broadcasted_iota(jnp.int32, gathered.shape, 1)
    top = jnp.max(jnp.where(spot == 0, gathered[...], 0.0), keepdims=True)
    step_size = jnp.broadcast_to(courant / (top + tiny), (8, 128))
    even_col = place[0] % 2 == 0
    tables = [lane_table(table, n) for n in range(3)]

    def coefficient(k, wg, og, s):
        return k * (wg * s * s + og * (1.0 - s) * (1.0 - s))

    def rows(step, carry):
        at = pl.ds(pl.multiple_of(step * 8, 8), 8)
        begin = step * stride
        add = step_size * source[at, :]
        total = jnp.zeros((8, 128), F32)
        first = jnp.zeros((8, 128), F32)
        for d in range(depth):
            s = sat[d, at, :] - step_size * net[d, at, :] + add
            new[d, at, :] = s
            c = coefficient(perm[d, at, :], wgain[d, at, :], ogain[d, at, :], s)
            chunks[pl.ds(pl.multiple_of(begin + d * 8, 8), 8), :] = c
            total = total + c
            first = jnp.where(lane == d, pltpu.roll(c, d, 1) if d else c, first)
        cell_sum[at, :] = total
        tile = jnp.where(even_col, got_b[at, :], got_a[at, :])
        flow = beside[at, :]
        kind = jnp.where(lane < depth, tile, 0.0)
        index = jnp.maximum(kind.astype(jnp.int32) - 1, 0)
        k, wg, og = [lane_take(each, index) for each in tables]
        s = pltpu.roll(tile, 128 - depth, 1) - step_size * flow
        s = s + step_size * pltpu.roll(flow, 128 - depth, 1)
        c = coefficient(jnp.where(kind > 0.5, k, 0.0), wg, og, s)
        col_sum[at, :] = jnp.where(lane < depth, harmonic(c, first), 0.0)
        return carry

    def two_rows(step, carry):
        return rows(2 * step + 1, rows(2 * step, carry))

    lax.fori_loop(0, tiles // 2, two_rows, 0)
    row_sum[0:8, :] = jnp.zeros((8, 128), F32)
    for p in range(1, tiles):
        total = jnp.zeros((8, 128), F32)
        for half in range(depth // 8):
            low = chunks[pl.ds((p - 1) * stride + half * 64 + 7, 8, stride=8), :]
            high = chunks[pl.ds(p * stride + half * 64, 8, stride=8), :]
            total = total + harmonic(low, high)
        row_sum[p * 8 : p * 8 + 8, :] = total
    brick = lax.broadcasted_iota(jnp.int32, (rows_all, 128), 0) // 8
    spot = lax.broadcasted_iota(jnp.int32, (rows_all, 128), 1)
    total = jnp.zeros((1, 128), F32)
    for n, part in enumerate((cell_sum, row_sum, col_sum)):
        each = jnp.sum(part[...], axis=1, keepdims=True)
        placed = jnp.where(spot == n * 16 + brick, each, 0.0)
        total = total + jnp.sum(placed, axis=0, keepdims=True)
    for p in range(tiles):
        chunks[p * stride + depth * 8 : (p + 1) * stride, :] = jnp.broadcast_to(total, (8, 128))


def relax_kernel(
    depth, place, got, residual, new, values, row_a, row_b, message, new_out, fd, fr, fc, gain, base, sem
):
    leave = pltpu.make_async_copy(new, new_out, sem.at[0])
    leave.start()
    lane = lane_iota()
    sub = sub_iota()
    layers = residual.shape[0] // 8
    parts = layers // depth
    zero = jnp.zeros((8, 128), F32)
    fd[0:8, :] = zero
    values[layers * 8 :, :] = jnp.zeros((64, 128), F32)
    fc[layers * 8 :, :] = jnp.zeros((64, 128), F32)
    even_row = place[2] % 2 == 0

    def half_face(low, high):
        return low * high / (low + high)

    def part(w, carry):
        below, total = carry
        begin = w * (depth + 1) * 8
        place_w = w * depth * 8
        after = jnp.minimum(w + 1, parts - 1) * (depth + 1) * 8
        c = got[pl.ds(pl.multiple_of(begin, 8), 8), :]
        for d in range(depth):
            here = pl.ds(pl.multiple_of(place_w + d * 8, 8), 8)
            if d + 1 < depth:
                c_next = got[pl.ds(pl.multiple_of(begin + d * 8 + 8, 8), 8), :]
                above = half_face(c, c_next)
            else:
                c_next = got[pl.ds(pl.multiple_of(after, 8), 8), :]
                above = jnp.where(w + 1 < parts, half_face(c, c_next), 0.0)
            row = jnp.where(sub == 0, 0.0, half_face(pltpu.roll(c, 1, 0), c))
            col = jnp.where(lane == 0, 0.0, half_face(pltpu.roll(c, 1, 1), c))
            diag = (
                (0.5 * compress) * c + below + above
                + row + pltpu.roll(row, 7, 0) + col + pltpu.roll(col, 127, 1)
            )
            scale = relax / diag
            fd[pl.ds(pl.multiple_of(place_w + d * 8 + 8, 8), 8), :] = above
            fr[here, :] = row
            fc[here, :] = col
            gain[here, :] = scale
            first = (0.5 * scale) * residual[here, :]
            base[here, :] = first
            values[here, :] = first
            c, below = c_next, above
        total = total + got[pl.ds(pl.multiple_of(begin + depth * 8, 8), 8), :]
        return below, total

    def build(step, carry):
        return part(2 * step + 1, part(2 * step, carry))

    _, total = lax.fori_loop(0, parts // 2, build, (zero, zero))

    block = 32

    def sweep(number, carry):
        def some(step, prev):
            begin = step * (block * 8)
            v = values[pl.ds(pl.multiple_of(begin, 8), 8), :]
            for n in range(block):
                here = pl.ds(pl.multiple_of(begin + n * 8, 8), 8)
                above = pl.ds(pl.multiple_of(begin + n * 8 + 8, 8), 8)
                v_next = values[above, :]
                row = fr[here, :]
                col = fc[here, :]
                total = fd[here, :] * prev + fd[above, :] * v_next
                total = total + (row * pltpu.roll(v, 1, 0) + pltpu.roll(row * v, 7, 0))
                total = total + (col * pltpu.roll(v, 1, 1) + pltpu.roll(col * v, 127, 1))
                values[here, :] = ((1.0 - relax) * v + base[here, :]) + gain[here, :] * total
                prev, v = v, v_next
            return prev

        lax.fori_loop(0, layers // block, some, zero)
        return carry

    lax.fori_loop(0, SWEEPS - 1, sweep, 0)

    for w in range(parts):
        for half in range(depth // 8):
            at = w * (depth + 1) * 8 + half * 64
            spot = w * depth + half * 8
            pairs = []
            for row in (0, 7):
                c = got[pl.ds(at + row, 8, stride=8), :]
                v = values[pl.ds(spot * 8 + row, 8, stride=8), :]
                pairs.append((c * v, c))
            for n in range(2):
                low, high = pairs[0][n], pairs[1][n]
                rows = slice(n * layers + spot, n * layers + spot + 8)
                row_a[rows, :] = jnp.where(even_row, high, low)
                row_b[rows, :] = jnp.where(even_row, low, high)

    quarters = layers // 64
    per_tile = 64 // depth
    peers = message.shape[0] // (quarters * 16 + 8)

    def pack(quarter, carry):
        packed = [zero, zero]
        for l in range(64):
            part = quarter * per_tile + l // depth
            c = got[pl.ds(pl.multiple_of(part * (depth + 1) * 8 + l % depth * 8, 8), 8), :]
            v = values[pl.ds(pl.multiple_of(quarter * 512 + l * 8, 8), 8), :]
            spot = (2 * l + 2) % 128
            mark = (lane == 2 * l + 1) | (lane == spot)
            for n, tile in enumerate((c * v, c)):
                turned = pltpu.roll(tile, spot, 1) if spot else tile
                packed[n] = jnp.where(mark, turned, packed[n])
        for peer in range(peers):
            for n in range(2):
                begin = peer * (quarters * 16 + 8) + (n * quarters + quarter) * 8
                message[pl.ds(pl.multiple_of(begin, 8), 8), :] = packed[n]
        return carry

    lax.fori_loop(0, quarters, pack, 0)
    for peer in range(peers):
        begin = peer * (quarters * 16 + 8) + quarters * 16
        message[begin : begin + 8, :] = total
    leave.wait()


def coarse_kernel(count, place, news, gathered, out):
    lane = lane_iota()
    sub = sub_iota()
    inside = lane < count
    width = gathered.shape[0] // count
    stride = news.shape[0] // width
    sums = jnp.zeros((8, 128), F32)
    for k in range(width):
        sums = jnp.where(sub == k, news[(k + 1) * stride - 8 : (k + 1) * stride, :], sums)
    cells = jnp.where(inside, sums, 0.0)
    low_row = jnp.where(inside, pltpu.roll(sums, 128 - 16, 1), 0.0)
    low_col = jnp.where(inside, pltpu.roll(sums, 128 - 32, 1), 0.0)
    low_row = jnp.where(lane == 0, 0.0, low_row)
    low_col = jnp.where(sub == 0, 0.0, low_col)
    high_row = pltpu.roll(low_row, 127, 1)
    high_col = pltpu.roll(low_col, 7, 0)
    diagonal = jnp.where(inside, compress * cells + low_row + high_row + low_col + high_col, 1.0)
    rhs = jnp.zeros((8, 128), F32)
    for p in range(count):
        rhs = jnp.where(lane == p, spread(gathered[p * width : p * width + width, :], 1), rhs)

    def line(tile, k):
        return jnp.broadcast_to(tile[k : k + 1, :], (8, 128))

    zero = jnp.zeros((8, 128), F32)
    main, lower, upper, right = [], [], [], []
    for k in range(width):
        row = jnp.where(sub == k, line(diagonal, k), zero)
        if k > 0:
            row = jnp.where(sub == k - 1, -line(low_col, k), row)
        if k + 1 < width:
            row = jnp.where(sub == k + 1, -line(low_col, k + 1), row)
        main.append(row)
        lower.append(jnp.where(sub == k, -line(low_row, k), zero))
        upper.append(jnp.where(sub == k, -line(high_row, k), zero))
        right.append(line(rhs, k))

    def eliminate(main, others):
        main = list(main)
        others = [list(rows) for rows in others]
        for k in range(width):
            inverse = 1.0 / line(main[k], k)
            main[k] = main[k] * inverse
            for rows in others:
                rows[k] = rows[k] * inverse
            for j in range(width):
                if j != k:
                    factor = line(main[j], k)
                    main[j] = main[j] - factor * main[k]
                    for rows in others:
                        rows[j] = rows[j] - factor * rows[k]
        return others

    stride = 1
    while stride < count:
        solved = eliminate(main, [lower, upper, right])
        back = [[pltpu.roll(x, stride, 1) for x in rows] for rows in solved]
        ahead = [[pltpu.roll(x, 128 - stride, 1) for x in rows] for rows in solved]
        new_lower, new_upper, new_main, new_right = [], [], [], []
        for k in range(width):
            lo, up, mid, rt = zero, zero, main[k], right[k]
            for j in [k] if stride == 1 else range(width):
                a = line(lower[k], j)
                b = line(upper[k], j)
                if 2 * stride < count:
                    lo = lo - a * back[0][j]
                    up = up - b * ahead[1][j]
                mid = mid - a * back[1][j] - b * ahead[0][j]
                rt = rt - a * back[2][j] - b * ahead[2][j]
            new_lower.append(lo)
            new_upper.append(up)
            new_main.append(mid)
            new_right.append(rt)
        lower, upper, main, right = new_lower, new_upper, new_main, new_right
        stride *= 2
    (right,) = eliminate(main, [right])
    mine = zero
    for k in range(width):
        mine = jnp.where(place[0] == k, right[k], mine)
    out[...] = lane_pick(mine, place[2])


def final_kernel(depth, place, got, values, row_a, row_b, news, coarse, result, packs, out, sem):
    lane = lane_iota()
    sub = sub_iota()
    layers = out.shape[0] // 8
    quarters = layers // 64
    per_tile = 64 // depth
    add = coarse[...]
    even_row = place[2] % 2 == 0
    stride = quarters * 16 + 8
    left = pl.multiple_of(jnp.maximum(place[0] - 1, 0) * stride, 8)
    right = pl.multiple_of(jnp.minimum(place[0] + 1, place[1] - 1) * stride, 8)
    odd = (lane & 1) == 1
    has_left = odd & (place[0] > 0)
    has_right = jnp.logical_not(odd) & (place[0] + 1 < place[1])
    for n in range(quarters * 2):
        low = news[pl.ds(left + n * 8, 8), :]
        high = pltpu.roll(news[pl.ds(right + n * 8, 8), :], 126, 1)
        packs[n * 8 : n * 8 + 8, :] = jnp.where(has_left, low, jnp.where(has_right, high, 0.0))
    ends = (lane == 0) | (lane == 127)

    def some(quarter, carry):
        sides = [
            packs[pl.ds(pl.multiple_of((n * quarters + quarter) * 8, 8), 8), :] for n in range(2)
        ]
        for l in range(64):
            g = quarter * 64 + l
            part = quarter * per_tile + l // depth
            here = pl.ds(pl.multiple_of(g * 8, 8), 8)
            c = got[pl.ds(pl.multiple_of(part * (depth + 1) * 8 + l % depth * 8, 8), 8), :]
            v = values[here, :]
            pair = []
            for n, tile in enumerate((c * v, c)):
                at = pl.ds(n * layers + g, 1)
                low = jnp.where(even_row, row_b[at, :], row_a[at, :])
                high = jnp.where(even_row, row_a[at, :], row_b[at, :])
                tile = tile + jnp.where(sub == 0, low, jnp.where(sub == 7, high, 0.0))
                tile = tile + jnp.where(ends, pltpu.roll(sides[n], 127 - 2 * l, 1), 0.0)
                pair.append(tile)
            out[here, :] = pair[0] / pair[1] + add
        leave(quarter).start()
        return carry

    def leave(quarter):
        part = pl.ds(pl.multiple_of(quarter * 512, 512), 512)
        return pltpu.make_async_copy(out.at[part, :], result.at[part, :], sem.at[quarter])

    lax.fori_loop(0, quarters, some, 0)
    for quarter in range(quarters):
        leave(quarter).wait()


def partners(array, axis, odd):
    count = lax.axis_size(axis)
    pairs = [(i, i + 1) for i in range(odd, count - 1, 2)]
    return lax.ppermute(array, axis, pairs + [(j, i) for i, j in pairs])


def forward(array, axis):
    count = lax.axis_size(axis)
    return lax.ppermute(array, axis, [(i, i + 1) for i in range(count - 1)])


def shards(saturation, pressure, rock_class, rock_table, well_columns, well_rates, residual):
    depth, rows_all, cols = saturation.shape
    layers, brick_rows, _ = residual.shape
    wide, narrow = lax.axis_size("wide"), lax.axis_size("narrow")
    block = (depth, rows_all, cols)
    plane = (rows_all, cols)
    place = jnp.stack(
        [lax.axis_index("narrow"), jnp.int32(narrow), lax.axis_index("wide")]
    ).astype(jnp.int32)
    vmem = pl.BlockSpec(memory_space=pltpu.VMEM)
    smem = pl.BlockSpec(memory_space=pltpu.SMEM)
    far = pl.BlockSpec(memory_space=pltpu.HBM)

    sat, press, kinds, face_a, face_b, pack_a, pack_b = call(
        faces_kernel,
        [block] * 3 + [(3,) + plane] * 2 + [plane] * 2,
        scratch=[pltpu.VMEM(block, jnp.int32), pltpu.SemaphoreType.DMA((24,))],
        in_specs=[smem] + [far] * 3,
    )(
        place,
        *(
            pltpu.with_memory_space_constraint(array, pltpu.HBM)
            for array in (saturation, pressure, rock_class)
        ),
    )
    perm, wgain, ogain, frac, own_a, own_b, source, rest = call(
        functools.partial(lookup_kernel, narrow),
        [block] * 4 + [(3,) + plane] * 2 + [plane, (8, 128)],
        in_specs=[smem] + [vmem] * 8,
    )(
        place, rock_table, kinds, sat, pack_a, pack_b,
        well_columns.reshape(1, -1), well_rates.reshape(1, -1), residual,
    )
    got_face_a = partners(face_a, "wide", 0)
    got_face_b = partners(face_b, "wide", 1)
    got_pack_b = partners(pack_b, "narrow", 1)
    got_pack_a = partners(pack_a, "narrow", 0)
    net, ahead, message = call(
        flow_kernel,
        [block, plane, (wide * narrow, 128)],
        scratch=[pltpu.VMEM(plane, F32)] * 2 + [pltpu.VMEM((depth, 8, cols), F32)] * 2,
        in_specs=[smem] + [vmem] * 12,
    )(
        place, rock_table, press, perm, frac, got_face_a, got_face_b, own_a, own_b,
        got_pack_a, got_pack_b, source, rest,
    )
    beside = forward(ahead, "narrow")
    gathered = lax.all_to_all(message, ("wide", "narrow"), 0, 0, tiled=True)
    chunk_rows = wide * (depth + 1) * 8
    new, chunks = call(
        update_kernel,
        [block, (chunk_rows, 128)],
        scratch=[pltpu.VMEM(plane, F32)] * 3,
        in_specs=[smem] + [vmem] * 11,
    )(
        place, gathered, rock_table, sat, net, source, perm, wgain, ogain, got_pack_a, got_pack_b,
        beside,
    )
    got = lax.all_to_all(chunks, "wide", 0, 0, tiled=True)
    message_rows = narrow * (layers // 4 + 8)
    values, row_a, row_b, message, sat_new = call(
        functools.partial(relax_kernel, depth),
        [(layers * 8 + 64, 128)] + [(2 * layers, 128)] * 2 + [(message_rows, 128), block],
        scratch=[pltpu.VMEM((layers * 8 + 64, 128), F32)] * 5 + [pltpu.SemaphoreType.DMA((1,))],
        in_specs=[smem] + [vmem] * 3,
        out_specs=[vmem] * 4 + [far],
    )(place, got, residual.reshape(layers * 8, 128), new)
    got_row_a = partners(row_a, "wide", 0)
    got_row_b = partners(row_b, "wide", 1)
    news = lax.all_to_all(message, "narrow", 0, 0, tiled=True)
    (coarse,) = call(
        functools.partial(coarse_kernel, wide), [(8, 128)], in_specs=[smem, vmem, vmem]
    )(place, news, gathered)
    (precond,) = call(
        functools.partial(final_kernel, depth),
        [(layers * 8, 128)],
        scratch=[
            pltpu.VMEM((layers // 4, 128), F32),
            pltpu.VMEM((layers * 8, 128), F32),
            pltpu.SemaphoreType.DMA((layers // 64,)),
        ],
        in_specs=[smem] + [vmem] * 6,
        out_specs=[far],
    )(place, got, values, got_row_a, got_row_b, news, coarse)
    return (sat_new, precond.reshape(layers, brick_rows, cols))


def solution(mesh):
    placed = (
        P("wide", None, "narrow"),
        P("wide", None, "narrow"),
        P("wide", None, "narrow"),
        P(),
        P(),
        P(),
        P(None, "wide", "narrow"),
    )
    return jax.shard_map(
        shards,
        mesh=mesh,
        in_specs=placed,
        out_specs=(P("wide", None, "narrow"), P(None, "wide", "narrow")),
        check_vma=False,
    )
```

```python
import functools

import jax
import jax.numpy as jnp
from jax import lax
from jax.experimental import pallas as pl
from jax.experimental.pallas import tpu as pltpu
from jax.sharding import PartitionSpec as P


SWEEPS = 6
compress = 0.05
relax = 0.8
gravity = 0.5
courant = 0.5
tiny = 1e-06

F32 = jnp.float32
HIGH = lax.Precision.HIGHEST
PARAMS = pltpu.CompilerParams(vmem_limit_bytes=16 * 1024 * 1024)


def harmonic(low, high):
    return 2.0 * low * high / (low + high)


def sub_iota():
    return lax.broadcasted_iota(jnp.int32, (8, 128), 0)


def lane_iota():
    return lax.broadcasted_iota(jnp.int32, (8, 128), 1)


def lane_pick(tile, index):
    return jnp.take_along_axis(tile, jnp.full((8, 128), index, jnp.int32), axis=1)


def lane_take(tile, index):
    return jnp.take_along_axis(tile, index, axis=1, mode="promise_in_bounds")


def mobility(wg, og, s):
    water = wg * s * s
    return water, water + og * (1.0 - s) * (1.0 - s)


def lane_table(table, n):
    row = jnp.concatenate([table[n : n + 1, :], jnp.zeros((1, 112), F32)], axis=1)
    return jnp.broadcast_to(row, (8, 128))


def spread(tile, lane):
    return jnp.broadcast_to(tile[:, lane : lane + 1], (8, 128))


def call(kernel, outs, scratch=(), aliases=None, out_specs=None, in_specs=None):
    def run(*args):
        return pl.pallas_call(
            kernel,
            out_shape=[jax.ShapeDtypeStruct(shape, F32) for shape in outs],
            in_specs=in_specs or [pl.BlockSpec(memory_space=pltpu.VMEM)] * len(args),
            out_specs=out_specs or [pl.BlockSpec(memory_space=pltpu.VMEM)] * len(outs),
            scratch_shapes=list(scratch),
            input_output_aliases=aliases or {},
            compiler_params=PARAMS,
        )(*args)

    return run


def faces_kernel(
    place, sat_in, press_in, rock_in, sat, press, kinds, face_a, face_b, pack_a, pack_b, rock, sem
):
    lane = lane_iota()
    depth, rows_all, _ = sat.shape
    groups = 8
    each = rows_all // groups
    copies = []
    for g in range(groups):
        part = pl.ds(g * each, each)
        for n, (src, dst) in enumerate(((rock_in, rock), (sat_in, sat), (press_in, press))):
            copies.append(
                pltpu.make_async_copy(src.at[:, part, :], dst.at[:, part, :], sem.at[g * 3 + n])
            )
            copies[-1].start()
    even_row = place[2] % 2 == 0
    even_col = place[0] % 2 == 0

    def rows(step, carry):
        at = pl.ds(pl.multiple_of(step * 8, 8), 8)
        first = jnp.zeros((8, 128), F32)
        last = jnp.zeros((8, 128), F32)
        for d in range(depth):
            kind = rock[d, at, :].astype(F32) + 1.0
            kinds[d, at, :] = kind
            fields = (kind, sat[d, at, :], press[d, at, :])
            for n, field in enumerate(fields):
                spot = n * depth + d
                turned = pltpu.roll(field, spot + 1, 1)
                first = jnp.where(lane == spot + 1, turned, first)
                last = jnp.where(lane == spot, turned, last)
                if d == 0:
                    face_a[n, at, :] = field
                if d + 1 == depth:
                    low = face_a[n, at, :]
                    face_a[n, at, :] = jnp.where(even_row, field, low)
                    face_b[n, at, :] = jnp.where(even_row, low, field)
        first = pltpu.roll(first, 127, 1)
        pack_a[at, :] = jnp.where(even_col, last, first)
        pack_b[at, :] = jnp.where(even_col, first, last)
        return carry

    def two_rows(step, carry):
        return rows(2 * step + 1, rows(2 * step, carry))

    for g in range(groups):
        for copy in copies[g * 3 : g * 3 + 3]:
            copy.wait()
        lax.fori_loop(g * (each // 16), (g + 1) * (each // 16), two_rows, 0)


def rock_of(tables, kind, s):
    index = jnp.maximum(kind.astype(jnp.int32) - 1, 0)
    k, wg, og = [lane_take(table, index) for table in tables]
    water, both = mobility(wg, og, s)
    return jnp.where(kind > 0.5, k, 0.0), water / both


def columns_of(tables, depth, pack):
    lane = lane_iota()
    kind = jnp.where(lane < depth, pack, 0.0)
    k, f = rock_of(tables, kind, pltpu.roll(pack, 128 - depth, 1))
    return [pltpu.roll(pack, 128 - 2 * depth, 1), k, f]


def lookup_kernel(
    bricks, place, table, kinds, sat, pack_a, pack_b, columns, rates, residual,
    perm, wgain, ogain, frac, own_a, own_b, source, rest,
):
    depth, rows_all, cols = sat.shape
    tables = [lane_table(table, n) for n in range(3)]
    entries = [jnp.broadcast_to(table[2:3, m : m + 1], (8, 128)) for m in range(16)]

    def rows(step, carry):
        at = pl.ds(pl.multiple_of(step * 8, 8), 8)
        for d in range(depth):
            kind = kinds[d, at, :].astype(jnp.int32) - 1
            k = lane_take(tables[0], kind)
            wg = lane_take(tables[1], kind)
            values = entries
            for bit in range(4):
                taken = (kind & (1 << bit)) != 0
                values = [
                    jnp.where(taken, values[m + 1], values[m]) for m in range(0, len(values), 2)
                ]
            og = values[0]
            water, both = mobility(wg, og, sat[d, at, :])
            perm[d, at, :] = k
            wgain[d, at, :] = wg
            ogain[d, at, :] = og
            frac[d, at, :] = water / both
        for pack, own in ((pack_a, own_a), (pack_b, own_b)):
            for n, field in enumerate(columns_of(tables, depth, pack[at, :])):
                own[n, at, :] = field
        return carry

    def two_rows(step, carry):
        return rows(2 * step + 1, rows(2 * step, carry))

    lax.fori_loop(0, rows_all // 16, two_rows, 0)

    def add(step, sums):
        at = step * 8
        return tuple(s + residual[at + n] for n, s in enumerate(sums))

    sums = lax.fori_loop(0, residual.shape[0] // 8, add, (jnp.zeros((8, 128), F32),) * 8)
    total = sum(sums[1:], sums[0])
    rest[...] = jnp.broadcast_to(jnp.sum(total, keepdims=True), (8, 128))

    wells = columns.shape[1]
    spot = lax.broadcasted_iota(jnp.int32, (rows_all, wells), 0)
    apart = columns[...] - spot * (cols * bricks)
    in_row = jnp.where((apart >= 0) & (apart < cols * bricks), 1.0, 0.0)
    number = columns[...]
    well_col = number & (cols * bricks - 1) if (cols * bricks) & (cols * bricks - 1) == 0 else number % (cols * bricks)
    spot = lax.broadcasted_iota(jnp.int32, (cols, wells), 0)
    in_col = jnp.where(well_col - place[0] * cols == spot, rates[...], 0.0)
    source[...] = lax.dot_general(
        in_row, in_col, (((1,), (1,)), ((), ())), precision=HIGH, preferred_element_type=F32
    )


def flows(low, high, lift, keep=None):
    total = low[1] * high[1] / (low[1] + high[1]) * (low[0] - high[0] + lift)
    if keep is not None:
        total = jnp.where(keep, total, 0.0)
    return total, total * jnp.where(total > 0, low[2], high[2])


def flow_kernel(
    place, table, press, perm, frac, face_a, face_b, own_a, own_b, got_a, got_b,
    source, rest, net, ahead, message, qp, wp, rq, rw,
):
    lane = lane_iota()
    sub = sub_iota()
    depth, rows_all, _ = perm.shape
    tiles = rows_all // 8
    even_row = place[2] % 2 == 0
    even_col = place[0] % 2 == 0
    half = lane >> 1
    odd = (lane & 1) == 1
    tables = [lane_table(table, n) for n in range(3)]

    def edge(step, carry):
        at = pl.ds(pl.multiple_of(step * 8, 8), 8)

        mine_a, mine_b = [[ref[n, at, :] for n in range(3)] for ref in (own_a, own_b)]
        other_a, other_b = [columns_of(tables, depth, ref[at, :]) for ref in (got_a, got_b)]

        def choose(one, two):
            return [jnp.where(even_col, a, b) for a, b in zip(one, two)]

        left = flows(choose(other_b, other_a), choose(mine_b, mine_a), 0.0)
        right = flows(choose(mine_a, mine_b), choose(other_a, other_b), 0.0)
        for out, low, high in zip((qp, wp), left, right):
            out[at, :] = jnp.where(
                odd,
                jnp.take_along_axis(low, half, axis=1),
                jnp.take_along_axis(high, half, axis=1),
            )
        return carry

    def two_edges(step, carry):
        return edge(2 * step + 1, edge(2 * step, carry))

    lax.fori_loop(0, tiles // 2, two_edges, 0)
    rq[...] = jnp.zeros(rq.shape, F32)
    rw[...] = jnp.zeros(rw.shape, F32)

    def rows(step, top):
        begin = pl.multiple_of(step * 8, 8)
        at = pl.ds(begin, 8)
        beyond = pl.ds(pl.multiple_of(jnp.minimum(begin + 8, rows_all - 8), 8), 8)
        inner = (sub < 7) | (step < tiles - 1)
        edge_q, edge_w = qp[at, :], wp[at, :]
        kind, s, p = [jnp.where(even_row, face_b[n, at, :], face_a[n, at, :]) for n in range(3)]
        below = [p, *rock_of(tables, kind, s)]
        kind, s, p = [jnp.where(even_row, face_a[n, at, :], face_b[n, at, :]) for n in range(3)]
        above = [p, *rock_of(tables, kind, s)]
        cur = [ref[0, at, :] for ref in (press, perm, frac)]
        depth_q, depth_w = flows(below, cur, gravity)
        told = jnp.where(
            (lane >= depth) & (lane < 2 * depth), spread(source[at, :], 127), 0.0
        )
        for d in range(depth):
            nxt = [ref[d + 1, at, :] for ref in (press, perm, frac)] if d + 1 < depth else above
            q, w = flows(cur, nxt, gravity)
            net_sum = w - depth_w
            out = jnp.maximum(q, 0.0) - jnp.minimum(depth_q, 0.0)
            depth_q, depth_w = q, w
            up = [
                pltpu.roll(jnp.where(sub == 0, ref[d, beyond, :], x), 7, 0)
                for ref, x in zip((press, perm, frac), cur)
            ]
            q, w = flows(cur, up, 0.0, inner)
            q_roll, w_roll = pltpu.roll(q, 1, 0), pltpu.roll(w, 1, 0)
            low_q = jnp.where(sub == 0, rq[d], q_roll)
            low_w = jnp.where(sub == 0, rw[d], w_roll)
            rq[d] = q_roll
            rw[d] = w_roll
            net_sum = net_sum + (w - low_w)
            out = out + (jnp.maximum(q, 0.0) - jnp.minimum(low_q, 0.0))
            q, w = flows(cur, [pltpu.roll(x, 127, 1) for x in cur], 0.0)
            side_q = pltpu.roll(edge_q, 127 - 2 * d, 1)
            side_w = pltpu.roll(edge_w, 127 - 2 * d, 1)
            low_q = jnp.where(lane == 0, side_q, pltpu.roll(q, 1, 1))
            low_w = jnp.where(lane == 0, side_w, pltpu.roll(w, 1, 1))
            q = jnp.where(lane == 127, side_q, q)
            w = jnp.where(lane == 127, side_w, w)
            net_sum = 2.0 * (net_sum + (w - low_w))
            net[d, at, :] = net_sum
            told = jnp.where(lane == d, pltpu.roll(net_sum, d + 1, 1), told)
            out = out + (jnp.maximum(q, 0.0) - jnp.minimum(low_q, 0.0))
            top = jnp.maximum(top, out)
            cur = nxt
        ahead[at, :] = told
        return top

    top = lax.fori_loop(0, tiles, rows, jnp.zeros((8, 128), F32))

    message[...] = jnp.where(
        lax.broadcasted_iota(jnp.int32, message.shape, 1) == 0,
        2.0 * jnp.max(top),
        rest[0:1, :],
    )


def update_kernel(
    place, gathered, table, sat, net, source, perm, wgain, ogain, got_a, got_b, beside,
    new, chunks, cell_sum, row_sum, col_sum,
):
    lane = lane_iota()
    depth, rows_all, _ = sat.shape
    tiles = rows_all // 8
    stride = (depth + 1) * 8
    spot = lax.broadcasted_iota(jnp.int32, gathered.shape, 1)
    top = jnp.max(jnp.where(spot == 0, gathered[...], 0.0), keepdims=True)
    step_size = jnp.broadcast_to(courant / (top + tiny), (8, 128))
    even_col = place[0] % 2 == 0
    tables = [lane_table(table, n) for n in range(3)]

    def coefficient(k, wg, og, s):
        return k * (wg * s * s + og * (1.0 - s) * (1.0 - s))

    def rows(step, carry):
        at = pl.ds(pl.multiple_of(step * 8, 8), 8)
        begin = step * stride
        add = step_size * source[at, :]
        total = jnp.zeros((8, 128), F32)
        first = jnp.zeros((8, 128), F32)
        for d in range(depth):
            s = sat[d, at, :] - step_size * net[d, at, :] + add
            new[d, at, :] = s
            c = coefficient(perm[d, at, :], wgain[d, at, :], ogain[d, at, :], s)
            chunks[pl.ds(pl.multiple_of(begin + d * 8, 8), 8), :] = c
            total = total + c
            first = jnp.where(lane == d, pltpu.roll(c, d, 1) if d else c, first)
        cell_sum[at, :] = total
        tile = jnp.where(even_col, got_b[at, :], got_a[at, :])
        flow = beside[at, :]
        kind = jnp.where(lane < depth, tile, 0.0)
        index = jnp.maximum(kind.astype(jnp.int32) - 1, 0)
        k, wg, og = [lane_take(each, index) for each in tables]
        s = pltpu.roll(tile, 128 - depth, 1) - step_size * flow
        s = s + step_size * pltpu.roll(flow, 128 - depth, 1)
        c = coefficient(jnp.where(kind > 0.5, k, 0.0), wg, og, s)
        col_sum[at, :] = jnp.where(lane < depth, harmonic(c, first), 0.0)
        return carry

    def two_rows(step, carry):
        return rows(2 * step + 1, rows(2 * step, carry))

    lax.fori_loop(0, tiles // 2, two_rows, 0)
    row_sum[0:8, :] = jnp.zeros((8, 128), F32)
    for p in range(1, tiles):
        total = jnp.zeros((8, 128), F32)
        for half in range(depth // 8):
            low = chunks[pl.ds((p - 1) * stride + half * 64 + 7, 8, stride=8), :]
            high = chunks[pl.ds(p * stride + half * 64, 8, stride=8), :]
            total = total + harmonic(low, high)
        row_sum[p * 8 : p * 8 + 8, :] = total
    brick = lax.broadcasted_iota(jnp.int32, (rows_all, 128), 0) // 8
    spot = lax.broadcasted_iota(jnp.int32, (rows_all, 128), 1)
    total = jnp.zeros((1, 128), F32)
    for n, part in enumerate((cell_sum, row_sum, col_sum)):
        each = jnp.sum(part[...], axis=1, keepdims=True)
        placed = jnp.where(spot == n * 16 + brick, each, 0.0)
        total = total + jnp.sum(placed, axis=0, keepdims=True)
    for p in range(tiles):
        chunks[p * stride + depth * 8 : (p + 1) * stride, :] = jnp.broadcast_to(total, (8, 128))


def relax_kernel(
    depth, place, got, residual, new, values, row_a, row_b, message, new_out, fd, fr, fc, gain, base, sem
):
    leave = pltpu.make_async_copy(new, new_out, sem.at[0])
    leave.start()
    lane = lane_iota()
    sub = sub_iota()
    layers = residual.shape[0] // 8
    parts = layers // depth
    zero = jnp.zeros((8, 128), F32)
    fd[0:8, :] = zero
    values[layers * 8 :, :] = jnp.zeros((64, 128), F32)
    fc[layers * 8 :, :] = jnp.zeros((64, 128), F32)
    even_row = place[2] % 2 == 0

    def half_face(low, high):
        return low * high / (low + high)

    def part(w, carry):
        below, total = carry
        begin = w * (depth + 1) * 8
        place_w = w * depth * 8
        after = jnp.minimum(w + 1, parts - 1) * (depth + 1) * 8
        c = got[pl.ds(pl.multiple_of(begin, 8), 8), :]
        for d in range(depth):
            here = pl.ds(pl.multiple_of(place_w + d * 8, 8), 8)
            if d + 1 < depth:
                c_next = got[pl.ds(pl.multiple_of(begin + d * 8 + 8, 8), 8), :]
                above = half_face(c, c_next)
            else:
                c_next = got[pl.ds(pl.multiple_of(after, 8), 8), :]
                above = jnp.where(w + 1 < parts, half_face(c, c_next), 0.0)
            row = jnp.where(sub == 0, 0.0, half_face(pltpu.roll(c, 1, 0), c))
            col = jnp.where(lane == 0, 0.0, half_face(pltpu.roll(c, 1, 1), c))
            diag = (
                (0.5 * compress) * c + below + above
                + row + pltpu.roll(row, 7, 0) + col + pltpu.roll(col, 127, 1)
            )
            scale = relax / diag
            fd[pl.ds(pl.multiple_of(place_w + d * 8 + 8, 8), 8), :] = above
            fr[here, :] = row
            fc[here, :] = col
            gain[here, :] = scale
            first = (0.5 * scale) * residual[here, :]
            base[here, :] = first
            values[here, :] = first
            c, below = c_next, above
        total = total + got[pl.ds(pl.multiple_of(begin + depth * 8, 8), 8), :]
        return below, total

    def build(step, carry):
        for n in range(4):
            carry = part(4 * step + n, carry)
        return carry

    _, total = lax.fori_loop(0, parts // 4, build, (zero, zero))

    block = 256

    def sweep(number, carry):
        def some(step, prev):
            begin = step * (block * 8)
            v = values[pl.ds(pl.multiple_of(begin, 8), 8), :]
            for n in range(block):
                here = pl.ds(pl.multiple_of(begin + n * 8, 8), 8)
                above = pl.ds(pl.multiple_of(begin + n * 8 + 8, 8), 8)
                v_next = values[above, :]
                row = fr[here, :]
                col = fc[here, :]
                total = fd[here, :] * prev + fd[above, :] * v_next
                total = total + (row * pltpu.roll(v, 1, 0) + pltpu.roll(row * v, 7, 0))
                total = total + (col * pltpu.roll(v, 1, 1) + pltpu.roll(col * v, 127, 1))
                values[here, :] = ((1.0 - relax) * v + base[here, :]) + gain[here, :] * total
                prev, v = v, v_next
            return prev

        lax.fori_loop(0, layers // block, some, zero)
        return carry

    lax.fori_loop(0, SWEEPS - 1, sweep, 0)

    for w in range(parts):
        for half in range(depth // 8):
            at = w * (depth + 1) * 8 + half * 64
            spot = w * depth + half * 8
            pairs = []
            for row in (0, 7):
                c = got[pl.ds(at + row, 8, stride=8), :]
                v = values[pl.ds(spot * 8 + row, 8, stride=8), :]
                pairs.append((c * v, c))
            for n in range(2):
                low, high = pairs[0][n], pairs[1][n]
                rows = slice(n * layers + spot, n * layers + spot + 8)
                row_a[rows, :] = jnp.where(even_row, high, low)
                row_b[rows, :] = jnp.where(even_row, low, high)

    quarters = layers // 64
    per_tile = 64 // depth
    peers = message.shape[0] // (quarters * 16 + 8)

    def pack(quarter, carry):
        packed = [zero, zero]
        for l in range(64):
            part = quarter * per_tile + l // depth
            c = got[pl.ds(pl.multiple_of(part * (depth + 1) * 8 + l % depth * 8, 8), 8), :]
            v = values[pl.ds(pl.multiple_of(quarter * 512 + l * 8, 8), 8), :]
            spot = (2 * l + 2) % 128
            mark = (lane == 2 * l + 1) | (lane == spot)
            for n, tile in enumerate((c * v, c)):
                turned = pltpu.roll(tile, spot, 1) if spot else tile
                packed[n] = jnp.where(mark, turned, packed[n])
        for peer in range(peers):
            for n in range(2):
                begin = peer * (quarters * 16 + 8) + (n * quarters + quarter) * 8
                message[pl.ds(pl.multiple_of(begin, 8), 8), :] = packed[n]
        return carry

    lax.fori_loop(0, quarters, pack, 0)
    for peer in range(peers):
        begin = peer * (quarters * 16 + 8) + quarters * 16
        message[begin : begin + 8, :] = total
    leave.wait()


def coarse_kernel(count, place, news, gathered, out):
    lane = lane_iota()
    sub = sub_iota()
    inside = lane < count
    width = gathered.shape[0] // count
    stride = news.shape[0] // width
    sums = jnp.zeros((8, 128), F32)
    for k in range(width):
        sums = jnp.where(sub == k, news[(k + 1) * stride - 8 : (k + 1) * stride, :], sums)
    cells = jnp.where(inside, sums, 0.0)
    low_row = jnp.where(inside, pltpu.roll(sums, 128 - 16, 1), 0.0)
    low_col = jnp.where(inside, pltpu.roll(sums, 128 - 32, 1), 0.0)
    low_row = jnp.where(lane == 0, 0.0, low_row)
    low_col = jnp.where(sub == 0, 0.0, low_col)
    high_row = pltpu.roll(low_row, 127, 1)
    high_col = pltpu.roll(low_col, 7, 0)
    diagonal = jnp.where(inside, compress * cells + low_row + high_row + low_col + high_col, 1.0)
    rhs = jnp.zeros((8, 128), F32)
    for p in range(count):
        rhs = jnp.where(lane == p, spread(gathered[p * width : p * width + width, :], 1), rhs)

    def line(tile, k):
        return jnp.broadcast_to(tile[k : k + 1, :], (8, 128))

    zero = jnp.zeros((8, 128), F32)
    main, lower, upper, right = [], [], [], []
    for k in range(width):
        row = jnp.where(sub == k, line(diagonal, k), zero)
        if k > 0:
            row = jnp.where(sub == k - 1, -line(low_col, k), row)
        if k + 1 < width:
            row = jnp.where(sub == k + 1, -line(low_col, k + 1), row)
        main.append(row)
        lower.append(jnp.where(sub == k, -line(low_row, k), zero))
        upper.append(jnp.where(sub == k, -line(high_row, k), zero))
        right.append(line(rhs, k))

    def eliminate(main, others):
        main = list(main)
        others = [list(rows) for rows in others]
        for k in range(width):
            inverse = 1.0 / line(main[k], k)
            main[k] = main[k] * inverse
            for rows in others:
                rows[k] = rows[k] * inverse
            for j in range(width):
                if j != k:
                    factor = line(main[j], k)
                    main[j] = main[j] - factor * main[k]
                    for rows in others:
                        rows[j] = rows[j] - factor * rows[k]
        return others

    stride = 1
    while stride < count:
        solved = eliminate(main, [lower, upper, right])
        back = [[pltpu.roll(x, stride, 1) for x in rows] for rows in solved]
        ahead = [[pltpu.roll(x, 128 - stride, 1) for x in rows] for rows in solved]
        new_lower, new_upper, new_main, new_right = [], [], [], []
        for k in range(width):
            lo, up, mid, rt = zero, zero, main[k], right[k]
            for j in [k] if stride == 1 else range(width):
                a = line(lower[k], j)
                b = line(upper[k], j)
                if 2 * stride < count:
                    lo = lo - a * back[0][j]
                    up = up - b * ahead[1][j]
                mid = mid - a * back[1][j] - b * ahead[0][j]
                rt = rt - a * back[2][j] - b * ahead[2][j]
            new_lower.append(lo)
            new_upper.append(up)
            new_main.append(mid)
            new_right.append(rt)
        lower, upper, main, right = new_lower, new_upper, new_main, new_right
        stride *= 2
    (right,) = eliminate(main, [right])
    mine = zero
    for k in range(width):
        mine = jnp.where(place[0] == k, right[k], mine)
    out[...] = lane_pick(mine, place[2])


def final_kernel(depth, place, got, values, row_a, row_b, news, coarse, result, packs, out, sem):
    lane = lane_iota()
    sub = sub_iota()
    layers = out.shape[0] // 8
    quarters = layers // 64
    per_tile = 64 // depth
    add = coarse[...]
    even_row = place[2] % 2 == 0
    stride = quarters * 16 + 8
    left = pl.multiple_of(jnp.maximum(place[0] - 1, 0) * stride, 8)
    right = pl.multiple_of(jnp.minimum(place[0] + 1, place[1] - 1) * stride, 8)
    odd = (lane & 1) == 1
    has_left = odd & (place[0] > 0)
    has_right = jnp.logical_not(odd) & (place[0] + 1 < place[1])
    for n in range(quarters * 2):
        low = news[pl.ds(left + n * 8, 8), :]
        high = pltpu.roll(news[pl.ds(right + n * 8, 8), :], 126, 1)
        packs[n * 8 : n * 8 + 8, :] = jnp.where(has_left, low, jnp.where(has_right, high, 0.0))
    ends = (lane == 0) | (lane == 127)

    def some(quarter, carry):
        sides = [
            packs[pl.ds(pl.multiple_of((n * quarters + quarter) * 8, 8), 8), :] for n in range(2)
        ]
        for l in range(64):
            g = quarter * 64 + l
            part = quarter * per_tile + l // depth
            here = pl.ds(pl.multiple_of(g * 8, 8), 8)
            c = got[pl.ds(pl.multiple_of(part * (depth + 1) * 8 + l % depth * 8, 8), 8), :]
            v = values[here, :]
            pair = []
            for n, tile in enumerate((c * v, c)):
                at = pl.ds(n * layers + g, 1)
                low = jnp.where(even_row, row_b[at, :], row_a[at, :])
                high = jnp.where(even_row, row_a[at, :], row_b[at, :])
                tile = tile + jnp.where(sub == 0, low, jnp.where(sub == 7, high, 0.0))
                tile = tile + jnp.where(ends, pltpu.roll(sides[n], 127 - 2 * l, 1), 0.0)
                pair.append(tile)
            out[here, :] = pair[0] / pair[1] + add
        leave(quarter).start()
        return carry

    def leave(quarter):
        part = pl.ds(pl.multiple_of(quarter * 512, 512), 512)
        return pltpu.make_async_copy(out.at[part, :], result.at[part, :], sem.at[quarter])

    lax.fori_loop(0, quarters, some, 0)
    for quarter in range(quarters):
        leave(quarter).wait()


def partners(array, axis, odd):
    count = lax.axis_size(axis)
    pairs = [(i, i + 1) for i in range(odd, count - 1, 2)]
    return lax.ppermute(array, axis, pairs + [(j, i) for i, j in pairs])


def forward(array, axis):
    count = lax.axis_size(axis)
    return lax.ppermute(array, axis, [(i, i + 1) for i in range(count - 1)])


def shards(saturation, pressure, rock_class, rock_table, well_columns, well_rates, residual):
    depth, rows_all, cols = saturation.shape
    layers, brick_rows, _ = residual.shape
    wide, narrow = lax.axis_size("wide"), lax.axis_size("narrow")
    block = (depth, rows_all, cols)
    plane = (rows_all, cols)
    place = jnp.stack(
        [lax.axis_index("narrow"), jnp.int32(narrow), lax.axis_index("wide")]
    ).astype(jnp.int32)
    vmem = pl.BlockSpec(memory_space=pltpu.VMEM)
    smem = pl.BlockSpec(memory_space=pltpu.SMEM)
    far = pl.BlockSpec(memory_space=pltpu.HBM)

    sat, press, kinds, face_a, face_b, pack_a, pack_b = call(
        faces_kernel,
        [block] * 3 + [(3,) + plane] * 2 + [plane] * 2,
        scratch=[pltpu.VMEM(block, jnp.int32), pltpu.SemaphoreType.DMA((24,))],
        in_specs=[smem] + [far] * 3,
    )(
        place,
        *(
            pltpu.with_memory_space_constraint(array, pltpu.HBM)
            for array in (saturation, pressure, rock_class)
        ),
    )
    perm, wgain, ogain, frac, own_a, own_b, source, rest = call(
        functools.partial(lookup_kernel, narrow),
        [block] * 4 + [(3,) + plane] * 2 + [plane, (8, 128)],
        in_specs=[smem] + [vmem] * 8,
    )(
        place, rock_table, kinds, sat, pack_a, pack_b,
        well_columns.reshape(1, -1), well_rates.reshape(1, -1), residual,
    )
    got_face_a = partners(face_a, "wide", 0)
    got_face_b = partners(face_b, "wide", 1)
    got_pack_b = partners(pack_b, "narrow", 1)
    got_pack_a = partners(pack_a, "narrow", 0)
    net, ahead, message = call(
        flow_kernel,
        [block, plane, (wide * narrow, 128)],
        scratch=[pltpu.VMEM(plane, F32)] * 2 + [pltpu.VMEM((depth, 8, cols), F32)] * 2,
        in_specs=[smem] + [vmem] * 12,
    )(
        place, rock_table, press, perm, frac, got_face_a, got_face_b, own_a, own_b,
        got_pack_a, got_pack_b, source, rest,
    )
    beside = forward(ahead, "narrow")
    gathered = lax.all_to_all(message, ("wide", "narrow"), 0, 0, tiled=True)
    chunk_rows = wide * (depth + 1) * 8
    new, chunks = call(
        update_kernel,
        [block, (chunk_rows, 128)],
        scratch=[pltpu.VMEM(plane, F32)] * 3,
        in_specs=[smem] + [vmem] * 11,
    )(
        place, gathered, rock_table, sat, net, source, perm, wgain, ogain, got_pack_a, got_pack_b,
        beside,
    )
    got = lax.all_to_all(chunks, "wide", 0, 0, tiled=True)
    message_rows = narrow * (layers // 4 + 8)
    values, row_a, row_b, message, sat_new = call(
        functools.partial(relax_kernel, depth),
        [(layers * 8 + 64, 128)] + [(2 * layers, 128)] * 2 + [(message_rows, 128), block],
        scratch=[pltpu.VMEM((layers * 8 + 64, 128), F32)] * 5 + [pltpu.SemaphoreType.DMA((1,))],
        in_specs=[smem] + [vmem] * 3,
        out_specs=[vmem] * 4 + [far],
    )(place, got, residual.reshape(layers * 8, 128), new)
    got_row_a = partners(row_a, "wide", 0)
    got_row_b = partners(row_b, "wide", 1)
    news = lax.all_to_all(message, "narrow", 0, 0, tiled=True)
    (coarse,) = call(
        functools.partial(coarse_kernel, wide), [(8, 128)], in_specs=[smem, vmem, vmem]
    )(place, news, gathered)
    (precond,) = call(
        functools.partial(final_kernel, depth),
        [(layers * 8, 128)],
        scratch=[
            pltpu.VMEM((layers // 4, 128), F32),
            pltpu.VMEM((layers * 8, 128), F32),
            pltpu.SemaphoreType.DMA((layers // 64,)),
        ],
        in_specs=[smem] + [vmem] * 6,
        out_specs=[far],
    )(place, got, values, got_row_a, got_row_b, news, coarse)
    return (sat_new, precond.reshape(layers, brick_rows, cols))


def solution(mesh):
    placed = (
        P("wide", None, "narrow"),
        P("wide", None, "narrow"),
        P("wide", None, "narrow"),
        P(),
        P(),
        P(),
        P(None, "wide", "narrow"),
    )
    return jax.shard_map(
        shards,
        mesh=mesh,
        in_specs=placed,
        out_specs=(P("wide", None, "narrow"), P(None, "wide", "narrow")),
        check_vma=False,
    )
```

```python
import functools

import jax
import jax.numpy as jnp
from jax import lax
from jax.experimental import pallas as pl
from jax.experimental.pallas import tpu as pltpu
from jax.sharding import PartitionSpec as P


SWEEPS = 6
compress = 0.05
relax = 0.8
gravity = 0.5
courant = 0.5
tiny = 1e-06

F32 = jnp.float32
HIGH = lax.Precision.HIGHEST
PARAMS = pltpu.CompilerParams(vmem_limit_bytes=16 * 1024 * 1024)


def harmonic(low, high):
    return 2.0 * low * high / (low + high)


def sub_iota():
    return lax.broadcasted_iota(jnp.int32, (8, 128), 0)


def lane_iota():
    return lax.broadcasted_iota(jnp.int32, (8, 128), 1)


def lane_pick(tile, index):
    return jnp.take_along_axis(tile, jnp.full((8, 128), index, jnp.int32), axis=1)


def lane_take(tile, index):
    return jnp.take_along_axis(tile, index, axis=1, mode="promise_in_bounds")


def mobility(wg, og, s):
    water = wg * s * s
    return water, water + og * (1.0 - s) * (1.0 - s)


def lane_table(table, n):
    row = jnp.concatenate([table[n : n + 1, :], jnp.zeros((1, 112), F32)], axis=1)
    return jnp.broadcast_to(row, (8, 128))


def spread(tile, lane):
    return jnp.broadcast_to(tile[:, lane : lane + 1], (8, 128))


def call(kernel, outs, scratch=(), aliases=None, out_specs=None, in_specs=None):
    def run(*args):
        return pl.pallas_call(
            kernel,
            out_shape=[jax.ShapeDtypeStruct(shape, F32) for shape in outs],
            in_specs=in_specs or [pl.BlockSpec(memory_space=pltpu.VMEM)] * len(args),
            out_specs=out_specs or [pl.BlockSpec(memory_space=pltpu.VMEM)] * len(outs),
            scratch_shapes=list(scratch),
            input_output_aliases=aliases or {},
            compiler_params=PARAMS,
        )(*args)

    return run


def faces_kernel(
    place, sat_in, press_in, rock_in, sat, press, kinds, face_a, face_b, pack_a, pack_b, rock, sem
):
    lane = lane_iota()
    depth, rows_all, _ = sat.shape
    groups = 8
    each = rows_all // groups
    copies = []
    for g in range(groups):
        part = pl.ds(g * each, each)
        for n, (src, dst) in enumerate(((rock_in, rock), (sat_in, sat), (press_in, press))):
            copies.append(
                pltpu.make_async_copy(src.at[:, part, :], dst.at[:, part, :], sem.at[g * 3 + n])
            )
            copies[-1].start()
    even_row = place[2] % 2 == 0
    even_col = place[0] % 2 == 0

    def rows(step, carry):
        at = pl.ds(pl.multiple_of(step * 8, 8), 8)
        first = jnp.zeros((8, 128), F32)
        last = jnp.zeros((8, 128), F32)
        for d in range(depth):
            kind = rock[d, at, :].astype(F32) + 1.0
            kinds[d, at, :] = kind
            fields = (kind, sat[d, at, :], press[d, at, :])
            for n, field in enumerate(fields):
                spot = n * depth + d
                turned = pltpu.roll(field, spot + 1, 1)
                first = jnp.where(lane == spot + 1, turned, first)
                last = jnp.where(lane == spot, turned, last)
                if d == 0:
                    face_a[n, at, :] = field
                if d + 1 == depth:
                    low = face_a[n, at, :]
                    face_a[n, at, :] = jnp.where(even_row, field, low)
                    face_b[n, at, :] = jnp.where(even_row, low, field)
        first = pltpu.roll(first, 127, 1)
        pack_a[at, :] = jnp.where(even_col, last, first)
        pack_b[at, :] = jnp.where(even_col, first, last)
        return carry

    def two_rows(step, carry):
        return rows(2 * step + 1, rows(2 * step, carry))

    for g in range(groups):
        for copy in copies[g * 3 : g * 3 + 3]:
            copy.wait()
        lax.fori_loop(g * (each // 16), (g + 1) * (each // 16), two_rows, 0)


def rock_of(tables, kind, s):
    index = jnp.maximum(kind.astype(jnp.int32) - 1, 0)
    k, wg, og = [lane_take(table, index) for table in tables]
    water, both = mobility(wg, og, s)
    return jnp.where(kind > 0.5, k, 0.0), water / both


def columns_of(tables, depth, pack):
    lane = lane_iota()
    kind = jnp.where(lane < depth, pack, 0.0)
    k, f = rock_of(tables, kind, pltpu.roll(pack, 128 - depth, 1))
    return [pltpu.roll(pack, 128 - 2 * depth, 1), k, f]


def lookup_kernel(
    bricks, place, table, kinds, sat, pack_a, pack_b, columns, rates, residual,
    perm, wgain, ogain, frac, own_a, own_b, source, rest,
):
    depth, rows_all, cols = sat.shape
    tables = [lane_table(table, n) for n in range(3)]
    entries = [jnp.broadcast_to(table[2:3, m : m + 1], (8, 128)) for m in range(16)]

    def rows(step, carry):
        at = pl.ds(pl.multiple_of(step * 8, 8), 8)
        for d in range(depth):
            kind = kinds[d, at, :].astype(jnp.int32) - 1
            k = lane_take(tables[0], kind)
            wg = lane_take(tables[1], kind)
            values = entries
            for bit in range(4):
                taken = (kind & (1 << bit)) != 0
                values = [
                    jnp.where(taken, values[m + 1], values[m]) for m in range(0, len(values), 2)
                ]
            og = values[0]
            water, both = mobility(wg, og, sat[d, at, :])
            perm[d, at, :] = k
            wgain[d, at, :] = wg
            ogain[d, at, :] = og
            frac[d, at, :] = water / both
        for pack, own in ((pack_a, own_a), (pack_b, own_b)):
            for n, field in enumerate(columns_of(tables, depth, pack[at, :])):
                own[n, at, :] = field
        return carry

    def some_rows(step, carry):
        for n in range(8):
            carry = rows(8 * step + n, carry)
        return carry

    lax.fori_loop(0, rows_all // 64, some_rows, 0)

    def add(step, sums):
        at = step * 8
        return tuple(s + residual[at + n] for n, s in enumerate(sums))

    sums = lax.fori_loop(0, residual.shape[0] // 8, add, (jnp.zeros((8, 128), F32),) * 8)
    total = sum(sums[1:], sums[0])
    rest[...] = jnp.broadcast_to(jnp.sum(total, keepdims=True), (8, 128))

    wells = columns.shape[1]
    spot = lax.broadcasted_iota(jnp.int32, (rows_all, wells), 0)
    apart = columns[...] - spot * (cols * bricks)
    in_row = jnp.where((apart >= 0) & (apart < cols * bricks), 1.0, 0.0)
    number = columns[...]
    well_col = number & (cols * bricks - 1) if (cols * bricks) & (cols * bricks - 1) == 0 else number % (cols * bricks)
    spot = lax.broadcasted_iota(jnp.int32, (cols, wells), 0)
    in_col = jnp.where(well_col - place[0] * cols == spot, rates[...], 0.0)
    source[...] = lax.dot_general(
        in_row, in_col, (((1,), (1,)), ((), ())), precision=HIGH, preferred_element_type=F32
    )


def flows(low, high, lift, keep=None):
    total = low[1] * high[1] / (low[1] + high[1]) * (low[0] - high[0] + lift)
    if keep is not None:
        total = jnp.where(keep, total, 0.0)
    return total, total * jnp.where(total > 0, low[2], high[2])


def flow_kernel(
    place, table, press, perm, frac, face_a, face_b, own_a, own_b, got_a, got_b,
    source, rest, net, ahead, message, qp, wp, rq, rw,
):
    lane = lane_iota()
    sub = sub_iota()
    depth, rows_all, _ = perm.shape
    tiles = rows_all // 8
    even_row = place[2] % 2 == 0
    even_col = place[0] % 2 == 0
    half = lane >> 1
    odd = (lane & 1) == 1
    tables = [lane_table(table, n) for n in range(3)]

    def edge(step, carry):
        at = pl.ds(pl.multiple_of(step * 8, 8), 8)

        mine_a, mine_b = [[ref[n, at, :] for n in range(3)] for ref in (own_a, own_b)]
        other_a, other_b = [columns_of(tables, depth, ref[at, :]) for ref in (got_a, got_b)]

        def choose(one, two):
            return [jnp.where(even_col, a, b) for a, b in zip(one, two)]

        left = flows(choose(other_b, other_a), choose(mine_b, mine_a), 0.0)
        right = flows(choose(mine_a, mine_b), choose(other_a, other_b), 0.0)
        for out, low, high in zip((qp, wp), left, right):
            out[at, :] = jnp.where(
                odd,
                jnp.take_along_axis(low, half, axis=1),
                jnp.take_along_axis(high, half, axis=1),
            )
        return carry

    def two_edges(step, carry):
        return edge(2 * step + 1, edge(2 * step, carry))

    lax.fori_loop(0, tiles // 2, two_edges, 0)
    rq[...] = jnp.zeros(rq.shape, F32)
    rw[...] = jnp.zeros(rw.shape, F32)

    def rows(step, top):
        begin = pl.multiple_of(step * 8, 8)
        at = pl.ds(begin, 8)
        beyond = pl.ds(pl.multiple_of(jnp.minimum(begin + 8, rows_all - 8), 8), 8)
        inner = (sub < 7) | (step < tiles - 1)
        edge_q, edge_w = qp[at, :], wp[at, :]
        kind, s, p = [jnp.where(even_row, face_b[n, at, :], face_a[n, at, :]) for n in range(3)]
        below = [p, *rock_of(tables, kind, s)]
        kind, s, p = [jnp.where(even_row, face_a[n, at, :], face_b[n, at, :]) for n in range(3)]
        above = [p, *rock_of(tables, kind, s)]
        cur = [ref[0, at, :] for ref in (press, perm, frac)]
        depth_q, depth_w = flows(below, cur, gravity)
        told = jnp.where(
            (lane >= depth) & (lane < 2 * depth), spread(source[at, :], 127), 0.0
        )
        for d in range(depth):
            nxt = [ref[d + 1, at, :] for ref in (press, perm, frac)] if d + 1 < depth else above
            q, w = flows(cur, nxt, gravity)
            net_sum = w - depth_w
            out = jnp.maximum(q, 0.0) - jnp.minimum(depth_q, 0.0)
            depth_q, depth_w = q, w
            up = [
                pltpu.roll(jnp.where(sub == 0, ref[d, beyond, :], x), 7, 0)
                for ref, x in zip((press, perm, frac), cur)
            ]
            q, w = flows(cur, up, 0.0, inner)
            q_roll, w_roll = pltpu.roll(q, 1, 0), pltpu.roll(w, 1, 0)
            low_q = jnp.where(sub == 0, rq[d], q_roll)
            low_w = jnp.where(sub == 0, rw[d], w_roll)
            rq[d] = q_roll
            rw[d] = w_roll
            net_sum = net_sum + (w - low_w)
            out = out + (jnp.maximum(q, 0.0) - jnp.minimum(low_q, 0.0))
            q, w = flows(cur, [pltpu.roll(x, 127, 1) for x in cur], 0.0)
            side_q = pltpu.roll(edge_q, 127 - 2 * d, 1)
            side_w = pltpu.roll(edge_w, 127 - 2 * d, 1)
            low_q = jnp.where(lane == 0, side_q, pltpu.roll(q, 1, 1))
            low_w = jnp.where(lane == 0, side_w, pltpu.roll(w, 1, 1))
            q = jnp.where(lane == 127, side_q, q)
            w = jnp.where(lane == 127, side_w, w)
            net_sum = 2.0 * (net_sum + (w - low_w))
            net[d, at, :] = net_sum
            told = jnp.where(lane == d, pltpu.roll(net_sum, d + 1, 1), told)
            out = out + (jnp.maximum(q, 0.0) - jnp.minimum(low_q, 0.0))
            top = jnp.maximum(top, out)
            cur = nxt
        ahead[at, :] = told
        return top

    top = lax.fori_loop(0, tiles, rows, jnp.zeros((8, 128), F32))

    message[...] = jnp.where(
        lax.broadcasted_iota(jnp.int32, message.shape, 1) == 0,
        2.0 * jnp.max(top),
        rest[0:1, :],
    )


def update_kernel(
    place, gathered, table, sat, net, source, perm, wgain, ogain, got_a, got_b, beside,
    new, chunks, cell_sum, row_sum, col_sum,
):
    lane = lane_iota()
    depth, rows_all, _ = sat.shape
    tiles = rows_all // 8
    stride = (depth + 1) * 8
    spot = lax.broadcasted_iota(jnp.int32, gathered.shape, 1)
    top = jnp.max(jnp.where(spot == 0, gathered[...], 0.0), keepdims=True)
    step_size = jnp.broadcast_to(courant / (top + tiny), (8, 128))
    even_col = place[0] % 2 == 0
    tables = [lane_table(table, n) for n in range(3)]

    def coefficient(k, wg, og, s):
        return k * (wg * s * s + og * (1.0 - s) * (1.0 - s))

    def rows(step, carry):
        at = pl.ds(pl.multiple_of(step * 8, 8), 8)
        begin = step * stride
        add = step_size * source[at, :]
        total = jnp.zeros((8, 128), F32)
        first = jnp.zeros((8, 128), F32)
        for d in range(depth):
            s = sat[d, at, :] - step_size * net[d, at, :] + add
            new[d, at, :] = s
            c = coefficient(perm[d, at, :], wgain[d, at, :], ogain[d, at, :], s)
            chunks[pl.ds(pl.multiple_of(begin + d * 8, 8), 8), :] = c
            total = total + c
            first = jnp.where(lane == d, pltpu.roll(c, d, 1) if d else c, first)
        cell_sum[at, :] = total
        tile = jnp.where(even_col, got_b[at, :], got_a[at, :])
        flow = beside[at, :]
        kind = jnp.where(lane < depth, tile, 0.0)
        index = jnp.maximum(kind.astype(jnp.int32) - 1, 0)
        k, wg, og = [lane_take(each, index) for each in tables]
        s = pltpu.roll(tile, 128 - depth, 1) - step_size * flow
        s = s + step_size * pltpu.roll(flow, 128 - depth, 1)
        c = coefficient(jnp.where(kind > 0.5, k, 0.0), wg, og, s)
        col_sum[at, :] = jnp.where(lane < depth, harmonic(c, first), 0.0)
        return carry

    def some_rows(step, carry):
        for n in range(8):
            carry = rows(8 * step + n, carry)
        return carry

    lax.fori_loop(0, tiles // 8, some_rows, 0)
    row_sum[0:8, :] = jnp.zeros((8, 128), F32)
    for p in range(1, tiles):
        total = jnp.zeros((8, 128), F32)
        for half in range(depth // 8):
            low = chunks[pl.ds((p - 1) * stride + half * 64 + 7, 8, stride=8), :]
            high = chunks[pl.ds(p * stride + half * 64, 8, stride=8), :]
            total = total + harmonic(low, high)
        row_sum[p * 8 : p * 8 + 8, :] = total
    brick = lax.broadcasted_iota(jnp.int32, (rows_all, 128), 0) // 8
    spot = lax.broadcasted_iota(jnp.int32, (rows_all, 128), 1)
    total = jnp.zeros((1, 128), F32)
    for n, part in enumerate((cell_sum, row_sum, col_sum)):
        each = jnp.sum(part[...], axis=1, keepdims=True)
        placed = jnp.where(spot == n * 16 + brick, each, 0.0)
        total = total + jnp.sum(placed, axis=0, keepdims=True)
    for p in range(tiles):
        chunks[p * stride + depth * 8 : (p + 1) * stride, :] = jnp.broadcast_to(total, (8, 128))


def relax_kernel(
    depth, place, got, residual, new, values, row_a, row_b, message, new_out, fd, fr, fc, gain, base, sem
):
    leave = pltpu.make_async_copy(new, new_out, sem.at[0])
    leave.start()
    lane = lane_iota()
    sub = sub_iota()
    layers = residual.shape[0] // 8
    parts = layers // depth
    zero = jnp.zeros((8, 128), F32)
    fd[0:8, :] = zero
    values[layers * 8 :, :] = jnp.zeros((64, 128), F32)
    fc[layers * 8 :, :] = jnp.zeros((64, 128), F32)
    even_row = place[2] % 2 == 0

    def half_face(low, high):
        return low * high / (low + high)

    def part(w, carry):
        below, total = carry
        begin = w * (depth + 1) * 8
        place_w = w * depth * 8
        after = jnp.minimum(w + 1, parts - 1) * (depth + 1) * 8
        c = got[pl.ds(pl.multiple_of(begin, 8), 8), :]
        for d in range(depth):
            here = pl.ds(pl.multiple_of(place_w + d * 8, 8), 8)
            if d + 1 < depth:
                c_next = got[pl.ds(pl.multiple_of(begin + d * 8 + 8, 8), 8), :]
                above = half_face(c, c_next)
            else:
                c_next = got[pl.ds(pl.multiple_of(after, 8), 8), :]
                above = jnp.where(w + 1 < parts, half_face(c, c_next), 0.0)
            row = jnp.where(sub == 0, 0.0, half_face(pltpu.roll(c, 1, 0), c))
            col = jnp.where(lane == 0, 0.0, half_face(pltpu.roll(c, 1, 1), c))
            diag = (
                (0.5 * compress) * c + below + above
                + row + pltpu.roll(row, 7, 0) + col + pltpu.roll(col, 127, 1)
            )
            scale = relax / diag
            fd[pl.ds(pl.multiple_of(place_w + d * 8 + 8, 8), 8), :] = above
            fr[here, :] = row
            fc[here, :] = col
            gain[here, :] = scale
            first = (0.5 * scale) * residual[here, :]
            base[here, :] = first
            values[here, :] = first
            c, below = c_next, above
        total = total + got[pl.ds(pl.multiple_of(begin + depth * 8, 8), 8), :]
        return below, total

    def build(step, carry):
        for n in range(4):
            carry = part(4 * step + n, carry)
        return carry

    _, total = lax.fori_loop(0, parts // 4, build, (zero, zero))

    block = 256

    def sweep(number, carry):
        def some(step, prev):
            begin = step * (block * 8)
            v = values[pl.ds(pl.multiple_of(begin, 8), 8), :]
            for n in range(block):
                here = pl.ds(pl.multiple_of(begin + n * 8, 8), 8)
                above = pl.ds(pl.multiple_of(begin + n * 8 + 8, 8), 8)
                v_next = values[above, :]
                row = fr[here, :]
                col = fc[here, :]
                total = fd[here, :] * prev + fd[above, :] * v_next
                total = total + (row * pltpu.roll(v, 1, 0) + pltpu.roll(row * v, 7, 0))
                total = total + (col * pltpu.roll(v, 1, 1) + pltpu.roll(col * v, 127, 1))
                values[here, :] = ((1.0 - relax) * v + base[here, :]) + gain[here, :] * total
                prev, v = v, v_next
            return prev

        lax.fori_loop(0, layers // block, some, zero)
        return carry

    lax.fori_loop(0, SWEEPS - 1, sweep, 0)

    for w in range(parts):
        for half in range(depth // 8):
            at = w * (depth + 1) * 8 + half * 64
            spot = w * depth + half * 8
            pairs = []
            for row in (0, 7):
                c = got[pl.ds(at + row, 8, stride=8), :]
                v = values[pl.ds(spot * 8 + row, 8, stride=8), :]
                pairs.append((c * v, c))
            for n in range(2):
                low, high = pairs[0][n], pairs[1][n]
                rows = slice(n * layers + spot, n * layers + spot + 8)
                row_a[rows, :] = jnp.where(even_row, high, low)
                row_b[rows, :] = jnp.where(even_row, low, high)

    quarters = layers // 64
    per_tile = 64 // depth
    peers = message.shape[0] // (quarters * 16 + 8)

    def pack(quarter, carry):
        packed = [zero, zero]
        for l in range(64):
            part = quarter * per_tile + l // depth
            c = got[pl.ds(pl.multiple_of(part * (depth + 1) * 8 + l % depth * 8, 8), 8), :]
            v = values[pl.ds(pl.multiple_of(quarter * 512 + l * 8, 8), 8), :]
            spot = (2 * l + 2) % 128
            mark = (lane == 2 * l + 1) | (lane == spot)
            for n, tile in enumerate((c * v, c)):
                turned = pltpu.roll(tile, spot, 1) if spot else tile
                packed[n] = jnp.where(mark, turned, packed[n])
        for peer in range(peers):
            for n in range(2):
                begin = peer * (quarters * 16 + 8) + (n * quarters + quarter) * 8
                message[pl.ds(pl.multiple_of(begin, 8), 8), :] = packed[n]
        return carry

    lax.fori_loop(0, quarters, pack, 0)
    for peer in range(peers):
        begin = peer * (quarters * 16 + 8) + quarters * 16
        message[begin : begin + 8, :] = total
    leave.wait()


def coarse_kernel(count, place, news, gathered, out):
    lane = lane_iota()
    sub = sub_iota()
    inside = lane < count
    width = gathered.shape[0] // count
    stride = news.shape[0] // width
    sums = jnp.zeros((8, 128), F32)
    for k in range(width):
        sums = jnp.where(sub == k, news[(k + 1) * stride - 8 : (k + 1) * stride, :], sums)
    cells = jnp.where(inside, sums, 0.0)
    low_row = jnp.where(inside, pltpu.roll(sums, 128 - 16, 1), 0.0)
    low_col = jnp.where(inside, pltpu.roll(sums, 128 - 32, 1), 0.0)
    low_row = jnp.where(lane == 0, 0.0, low_row)
    low_col = jnp.where(sub == 0, 0.0, low_col)
    high_row = pltpu.roll(low_row, 127, 1)
    high_col = pltpu.roll(low_col, 7, 0)
    diagonal = jnp.where(inside, compress * cells + low_row + high_row + low_col + high_col, 1.0)
    rhs = jnp.zeros((8, 128), F32)
    for p in range(count):
        rhs = jnp.where(lane == p, spread(gathered[p * width : p * width + width, :], 1), rhs)

    def line(tile, k):
        return jnp.broadcast_to(tile[k : k + 1, :], (8, 128))

    zero = jnp.zeros((8, 128), F32)
    main, lower, upper, right = [], [], [], []
    for k in range(width):
        row = jnp.where(sub == k, line(diagonal, k), zero)
        if k > 0:
            row = jnp.where(sub == k - 1, -line(low_col, k), row)
        if k + 1 < width:
            row = jnp.where(sub == k + 1, -line(low_col, k + 1), row)
        main.append(row)
        lower.append(jnp.where(sub == k, -line(low_row, k), zero))
        upper.append(jnp.where(sub == k, -line(high_row, k), zero))
        right.append(line(rhs, k))

    def eliminate(main, others):
        main = list(main)
        others = [list(rows) for rows in others]
        for k in range(width):
            inverse = 1.0 / line(main[k], k)
            main[k] = main[k] * inverse
            for rows in others:
                rows[k] = rows[k] * inverse
            for j in range(width):
                if j != k:
                    factor = line(main[j], k)
                    main[j] = main[j] - factor * main[k]
                    for rows in others:
                        rows[j] = rows[j] - factor * rows[k]
        return others

    stride = 1
    while stride < count:
        solved = eliminate(main, [lower, upper, right])
        back = [[pltpu.roll(x, stride, 1) for x in rows] for rows in solved]
        ahead = [[pltpu.roll(x, 128 - stride, 1) for x in rows] for rows in solved]
        new_lower, new_upper, new_main, new_right = [], [], [], []
        for k in range(width):
            lo, up, mid, rt = zero, zero, main[k], right[k]
            for j in [k] if stride == 1 else range(width):
                a = line(lower[k], j)
                b = line(upper[k], j)
                if 2 * stride < count:
                    lo = lo - a * back[0][j]
                    up = up - b * ahead[1][j]
                mid = mid - a * back[1][j] - b * ahead[0][j]
                rt = rt - a * back[2][j] - b * ahead[2][j]
            new_lower.append(lo)
            new_upper.append(up)
            new_main.append(mid)
            new_right.append(rt)
        lower, upper, main, right = new_lower, new_upper, new_main, new_right
        stride *= 2
    (right,) = eliminate(main, [right])
    mine = zero
    for k in range(width):
        mine = jnp.where(place[0] == k, right[k], mine)
    out[...] = lane_pick(mine, place[2])


def final_kernel(depth, place, got, values, row_a, row_b, news, coarse, result, packs, out, sem):
    lane = lane_iota()
    sub = sub_iota()
    layers = out.shape[0] // 8
    quarters = layers // 64
    per_tile = 64 // depth
    add = coarse[...]
    even_row = place[2] % 2 == 0
    stride = quarters * 16 + 8
    left = pl.multiple_of(jnp.maximum(place[0] - 1, 0) * stride, 8)
    right = pl.multiple_of(jnp.minimum(place[0] + 1, place[1] - 1) * stride, 8)
    odd = (lane & 1) == 1
    has_left = odd & (place[0] > 0)
    has_right = jnp.logical_not(odd) & (place[0] + 1 < place[1])
    for n in range(quarters * 2):
        low = news[pl.ds(left + n * 8, 8), :]
        high = pltpu.roll(news[pl.ds(right + n * 8, 8), :], 126, 1)
        packs[n * 8 : n * 8 + 8, :] = jnp.where(has_left, low, jnp.where(has_right, high, 0.0))
    ends = (lane == 0) | (lane == 127)

    def some(quarter, carry):
        sides = [
            packs[pl.ds(pl.multiple_of((n * quarters + quarter) * 8, 8), 8), :] for n in range(2)
        ]
        for l in range(64):
            g = quarter * 64 + l
            part = quarter * per_tile + l // depth
            here = pl.ds(pl.multiple_of(g * 8, 8), 8)
            c = got[pl.ds(pl.multiple_of(part * (depth + 1) * 8 + l % depth * 8, 8), 8), :]
            v = values[here, :]
            pair = []
            for n, tile in enumerate((c * v, c)):
                at = pl.ds(n * layers + g, 1)
                low = jnp.where(even_row, row_b[at, :], row_a[at, :])
                high = jnp.where(even_row, row_a[at, :], row_b[at, :])
                tile = tile + jnp.where(sub == 0, low, jnp.where(sub == 7, high, 0.0))
                tile = tile + jnp.where(ends, pltpu.roll(sides[n], 127 - 2 * l, 1), 0.0)
                pair.append(tile)
            out[here, :] = pair[0] / pair[1] + add
        leave(quarter).start()
        return carry

    def leave(quarter):
        part = pl.ds(pl.multiple_of(quarter * 512, 512), 512)
        return pltpu.make_async_copy(out.at[part, :], result.at[part, :], sem.at[quarter])

    def several(step, carry):
        for n in range(4):
            carry = some(4 * step + n, carry)
        return carry

    lax.fori_loop(0, quarters // 4, several, 0)
    for quarter in range(quarters):
        leave(quarter).wait()


def partners(array, axis, odd):
    count = lax.axis_size(axis)
    pairs = [(i, i + 1) for i in range(odd, count - 1, 2)]
    return lax.ppermute(array, axis, pairs + [(j, i) for i, j in pairs])


def forward(array, axis):
    count = lax.axis_size(axis)
    return lax.ppermute(array, axis, [(i, i + 1) for i in range(count - 1)])


def shards(saturation, pressure, rock_class, rock_table, well_columns, well_rates, residual):
    depth, rows_all, cols = saturation.shape
    layers, brick_rows, _ = residual.shape
    wide, narrow = lax.axis_size("wide"), lax.axis_size("narrow")
    block = (depth, rows_all, cols)
    plane = (rows_all, cols)
    place = jnp.stack(
        [lax.axis_index("narrow"), jnp.int32(narrow), lax.axis_index("wide")]
    ).astype(jnp.int32)
    vmem = pl.BlockSpec(memory_space=pltpu.VMEM)
    smem = pl.BlockSpec(memory_space=pltpu.SMEM)
    far = pl.BlockSpec(memory_space=pltpu.HBM)

    sat, press, kinds, face_a, face_b, pack_a, pack_b = call(
        faces_kernel,
        [block] * 3 + [(3,) + plane] * 2 + [plane] * 2,
        scratch=[pltpu.VMEM(block, jnp.int32), pltpu.SemaphoreType.DMA((24,))],
        in_specs=[smem] + [far] * 3,
    )(
        place,
        *(
            pltpu.with_memory_space_constraint(array, pltpu.HBM)
            for array in (saturation, pressure, rock_class)
        ),
    )
    perm, wgain, ogain, frac, own_a, own_b, source, rest = call(
        functools.partial(lookup_kernel, narrow),
        [block] * 4 + [(3,) + plane] * 2 + [plane, (8, 128)],
        in_specs=[smem] + [vmem] * 8,
    )(
        place, rock_table, kinds, sat, pack_a, pack_b,
        well_columns.reshape(1, -1), well_rates.reshape(1, -1), residual,
    )
    got_face_a = partners(face_a, "wide", 0)
    got_face_b = partners(face_b, "wide", 1)
    got_pack_b = partners(pack_b, "narrow", 1)
    got_pack_a = partners(pack_a, "narrow", 0)
    net, ahead, message = call(
        flow_kernel,
        [block, plane, (wide * narrow, 128)],
        scratch=[pltpu.VMEM(plane, F32)] * 2 + [pltpu.VMEM((depth, 8, cols), F32)] * 2,
        in_specs=[smem] + [vmem] * 12,
    )(
        place, rock_table, press, perm, frac, got_face_a, got_face_b, own_a, own_b,
        got_pack_a, got_pack_b, source, rest,
    )
    beside = forward(ahead, "narrow")
    gathered = lax.all_to_all(message, ("wide", "narrow"), 0, 0, tiled=True)
    chunk_rows = wide * (depth + 1) * 8
    new, chunks = call(
        update_kernel,
        [block, (chunk_rows, 128)],
        scratch=[pltpu.VMEM(plane, F32)] * 3,
        in_specs=[smem] + [vmem] * 11,
    )(
        place, gathered, rock_table, sat, net, source, perm, wgain, ogain, got_pack_a, got_pack_b,
        beside,
    )
    got = lax.all_to_all(chunks, "wide", 0, 0, tiled=True)
    message_rows = narrow * (layers // 4 + 8)
    values, row_a, row_b, message, sat_new = call(
        functools.partial(relax_kernel, depth),
        [(layers * 8 + 64, 128)] + [(2 * layers, 128)] * 2 + [(message_rows, 128), block],
        scratch=[pltpu.VMEM((layers * 8 + 64, 128), F32)] * 5 + [pltpu.SemaphoreType.DMA((1,))],
        in_specs=[smem] + [vmem] * 3,
        out_specs=[vmem] * 4 + [far],
    )(place, got, residual.reshape(layers * 8, 128), new)
    got_row_a = partners(row_a, "wide", 0)
    got_row_b = partners(row_b, "wide", 1)
    news = lax.all_to_all(message, "narrow", 0, 0, tiled=True)
    (coarse,) = call(
        functools.partial(coarse_kernel, wide), [(8, 128)], in_specs=[smem, vmem, vmem]
    )(place, news, gathered)
    (precond,) = call(
        functools.partial(final_kernel, depth),
        [(layers * 8, 128)],
        scratch=[
            pltpu.VMEM((layers // 4, 128), F32),
            pltpu.VMEM((layers * 8, 128), F32),
            pltpu.SemaphoreType.DMA((layers // 64,)),
        ],
        in_specs=[smem] + [vmem] * 6,
        out_specs=[far],
    )(place, got, values, got_row_a, got_row_b, news, coarse)
    return (sat_new, precond.reshape(layers, brick_rows, cols))


def solution(mesh):
    placed = (
        P("wide", None, "narrow"),
        P("wide", None, "narrow"),
        P("wide", None, "narrow"),
        P(),
        P(),
        P(),
        P(None, "wide", "narrow"),
    )
    return jax.shard_map(
        shards,
        mesh=mesh,
        in_specs=placed,
        out_specs=(P("wide", None, "narrow"), P(None, "wide", "narrow")),
        check_vma=False,
    )
```

```python
import functools

import jax
import jax.numpy as jnp
from jax import lax
from jax.experimental import pallas as pl
from jax.experimental.pallas import tpu as pltpu
from jax.sharding import PartitionSpec as P


SWEEPS = 6
compress = 0.05
relax = 0.8
gravity = 0.5
courant = 0.5
tiny = 1e-06

F32 = jnp.float32
HIGH = lax.Precision.HIGHEST
PARAMS = pltpu.CompilerParams(vmem_limit_bytes=16 * 1024 * 1024)


def harmonic(low, high):
    return 2.0 * low * high / (low + high)


def sub_iota():
    return lax.broadcasted_iota(jnp.int32, (8, 128), 0)


def lane_iota():
    return lax.broadcasted_iota(jnp.int32, (8, 128), 1)


def lane_pick(tile, index):
    return jnp.take_along_axis(tile, jnp.full((8, 128), index, jnp.int32), axis=1)


def lane_take(tile, index):
    return jnp.take_along_axis(tile, index, axis=1, mode="promise_in_bounds")


def mobility(wg, og, s):
    water = wg * s * s
    return water, water + og * (1.0 - s) * (1.0 - s)


def lane_table(table, n):
    row = jnp.concatenate([table[n : n + 1, :], jnp.zeros((1, 112), F32)], axis=1)
    return jnp.broadcast_to(row, (8, 128))


def here():
    return lax.axis_index("narrow"), lax.axis_size("narrow"), lax.axis_index("wide")


def spread(tile, lane):
    return jnp.broadcast_to(tile[:, lane : lane + 1], (8, 128))


def call(kernel, outs, scratch=(), aliases=None, out_specs=None, in_specs=None):
    def run(*args):
        return pl.pallas_call(
            kernel,
            out_shape=[jax.ShapeDtypeStruct(shape, F32) for shape in outs],
            in_specs=in_specs or [pl.BlockSpec(memory_space=pltpu.VMEM)] * len(args),
            out_specs=out_specs or [pl.BlockSpec(memory_space=pltpu.VMEM)] * len(outs),
            scratch_shapes=list(scratch),
            input_output_aliases=aliases or {},
            compiler_params=PARAMS,
        )(*args)

    return run


def faces_kernel(
    sat_in, press_in, rock_in, sat, press, kinds, face_a, face_b, pack_a, pack_b, rock, sem
):
    place = here()
    lane = lane_iota()
    depth, rows_all, _ = sat.shape
    groups = 8
    each = rows_all // groups
    copies = []
    for g in range(groups):
        part = pl.ds(g * each, each)
        for n, (src, dst) in enumerate(((rock_in, rock), (sat_in, sat), (press_in, press))):
            copies.append(
                pltpu.make_async_copy(src.at[:, part, :], dst.at[:, part, :], sem.at[g * 3 + n])
            )
            copies[-1].start()
    even_row = place[2] % 2 == 0
    even_col = place[0] % 2 == 0

    def rows(step, carry):
        at = pl.ds(pl.multiple_of(step * 8, 8), 8)
        first = jnp.zeros((8, 128), F32)
        last = jnp.zeros((8, 128), F32)
        for d in range(depth):
            kind = rock[d, at, :].astype(F32) + 1.0
            kinds[d, at, :] = kind
            fields = (kind, sat[d, at, :], press[d, at, :])
            for n, field in enumerate(fields):
                spot = n * depth + d
                turned = pltpu.roll(field, spot + 1, 1)
                first = jnp.where(lane == spot + 1, turned, first)
                last = jnp.where(lane == spot, turned, last)
                if d == 0:
                    face_a[n, at, :] = field
                if d + 1 == depth:
                    low = face_a[n, at, :]
                    face_a[n, at, :] = jnp.where(even_row, field, low)
                    face_b[n, at, :] = jnp.where(even_row, low, field)
        first = pltpu.roll(first, 127, 1)
        pack_a[at, :] = jnp.where(even_col, last, first)
        pack_b[at, :] = jnp.where(even_col, first, last)
        return carry

    def two_rows(step, carry):
        return rows(2 * step + 1, rows(2 * step, carry))

    for g in range(groups):
        for copy in copies[g * 3 : g * 3 + 3]:
            copy.wait()
        lax.fori_loop(g * (each // 16), (g + 1) * (each // 16), two_rows, 0)


def rock_of(tables, kind, s):
    index = jnp.maximum(kind.astype(jnp.int32) - 1, 0)
    k, wg, og = [lane_take(table, index) for table in tables]
    water, both = mobility(wg, og, s)
    return jnp.where(kind > 0.5, k, 0.0), water / both


def columns_of(tables, depth, pack):
    lane = lane_iota()
    kind = jnp.where(lane < depth, pack, 0.0)
    k, f = rock_of(tables, kind, pltpu.roll(pack, 128 - depth, 1))
    return [pltpu.roll(pack, 128 - 2 * depth, 1), k, f]


def lookup_kernel(
    bricks, table, kinds, sat, pack_a, pack_b, columns, rates, residual,
    perm, wgain, ogain, frac, own_a, own_b, source, rest,
):
    place = here()
    depth, rows_all, cols = sat.shape
    tables = [lane_table(table, n) for n in range(3)]
    entries = [jnp.broadcast_to(table[2:3, m : m + 1], (8, 128)) for m in range(16)]

    def rows(step, carry):
        at = pl.ds(pl.multiple_of(step * 8, 8), 8)
        for d in range(depth):
            kind = kinds[d, at, :].astype(jnp.int32) - 1
            k = lane_take(tables[0], kind)
            wg = lane_take(tables[1], kind)
            values = entries
            for bit in range(4):
                taken = (kind & (1 << bit)) != 0
                values = [
                    jnp.where(taken, values[m + 1], values[m]) for m in range(0, len(values), 2)
                ]
            og = values[0]
            water, both = mobility(wg, og, sat[d, at, :])
            perm[d, at, :] = k
            wgain[d, at, :] = wg
            ogain[d, at, :] = og
            frac[d, at, :] = water / both
        for pack, own in ((pack_a, own_a), (pack_b, own_b)):
            for n, field in enumerate(columns_of(tables, depth, pack[at, :])):
                own[n, at, :] = field
        return carry

    def some_rows(step, carry):
        for n in range(8):
            carry = rows(8 * step + n, carry)
        return carry

    lax.fori_loop(0, rows_all // 64, some_rows, 0)

    def add(step, sums):
        at = step * 8
        return tuple(s + residual[at + n] for n, s in enumerate(sums))

    sums = lax.fori_loop(0, residual.shape[0] // 8, add, (jnp.zeros((8, 128), F32),) * 8)
    total = sum(sums[1:], sums[0])
    rest[...] = jnp.broadcast_to(jnp.sum(total, keepdims=True), (8, 128))

    wells = columns.shape[1]
    spot = lax.broadcasted_iota(jnp.int32, (rows_all, wells), 0)
    apart = columns[...] - spot * (cols * bricks)
    in_row = jnp.where((apart >= 0) & (apart < cols * bricks), 1.0, 0.0)
    number = columns[...]
    well_col = number & (cols * bricks - 1) if (cols * bricks) & (cols * bricks - 1) == 0 else number % (cols * bricks)
    spot = lax.broadcasted_iota(jnp.int32, (cols, wells), 0)
    in_col = jnp.where(well_col - place[0] * cols == spot, rates[...], 0.0)
    source[...] = lax.dot_general(
        in_row, in_col, (((1,), (1,)), ((), ())), precision=HIGH, preferred_element_type=F32
    )


def flows(low, high, lift, keep=None):
    total = low[1] * high[1] / (low[1] + high[1]) * (low[0] - high[0] + lift)
    if keep is not None:
        total = jnp.where(keep, total, 0.0)
    return total, total * jnp.where(total > 0, low[2], high[2])


def flow_kernel(
    table, press, perm, frac, face_a, face_b, own_a, own_b, got_a, got_b,
    source, rest, net, ahead, message, qp, wp, rq, rw,
):
    place = here()
    lane = lane_iota()
    sub = sub_iota()
    depth, rows_all, _ = perm.shape
    tiles = rows_all // 8
    even_row = place[2] % 2 == 0
    even_col = place[0] % 2 == 0
    half = lane >> 1
    odd = (lane & 1) == 1
    tables = [lane_table(table, n) for n in range(3)]

    def edge(step, carry):
        at = pl.ds(pl.multiple_of(step * 8, 8), 8)

        mine_a, mine_b = [[ref[n, at, :] for n in range(3)] for ref in (own_a, own_b)]
        other_a, other_b = [columns_of(tables, depth, ref[at, :]) for ref in (got_a, got_b)]

        def choose(one, two):
            return [jnp.where(even_col, a, b) for a, b in zip(one, two)]

        left = flows(choose(other_b, other_a), choose(mine_b, mine_a), 0.0)
        right = flows(choose(mine_a, mine_b), choose(other_a, other_b), 0.0)
        for out, low, high in zip((qp, wp), left, right):
            out[at, :] = jnp.where(
                odd,
                jnp.take_along_axis(low, half, axis=1),
                jnp.take_along_axis(high, half, axis=1),
            )
        return carry

    def two_edges(step, carry):
        return edge(2 * step + 1, edge(2 * step, carry))

    lax.fori_loop(0, tiles // 2, two_edges, 0)
    rq[...] = jnp.zeros(rq.shape, F32)
    rw[...] = jnp.zeros(rw.shape, F32)

    def rows(step, top):
        begin = pl.multiple_of(step * 8, 8)
        at = pl.ds(begin, 8)
        beyond = pl.ds(pl.multiple_of(jnp.minimum(begin + 8, rows_all - 8), 8), 8)
        inner = (sub < 7) | (step < tiles - 1)
        edge_q, edge_w = qp[at, :], wp[at, :]
        kind, s, p = [jnp.where(even_row, face_b[n, at, :], face_a[n, at, :]) for n in range(3)]
        below = [p, *rock_of(tables, kind, s)]
        kind, s, p = [jnp.where(even_row, face_a[n, at, :], face_b[n, at, :]) for n in range(3)]
        above = [p, *rock_of(tables, kind, s)]
        cur = [ref[0, at, :] for ref in (press, perm, frac)]
        depth_q, depth_w = flows(below, cur, gravity)
        told = jnp.where(
            (lane >= depth) & (lane < 2 * depth), spread(source[at, :], 127), 0.0
        )
        for d in range(depth):
            nxt = [ref[d + 1, at, :] for ref in (press, perm, frac)] if d + 1 < depth else above
            q, w = flows(cur, nxt, gravity)
            net_sum = w - depth_w
            out = jnp.maximum(q, 0.0) - jnp.minimum(depth_q, 0.0)
            depth_q, depth_w = q, w
            up = [
                pltpu.roll(jnp.where(sub == 0, ref[d, beyond, :], x), 7, 0)
                for ref, x in zip((press, perm, frac), cur)
            ]
            q, w = flows(cur, up, 0.0, inner)
            q_roll, w_roll = pltpu.roll(q, 1, 0), pltpu.roll(w, 1, 0)
            low_q = jnp.where(sub == 0, rq[d], q_roll)
            low_w = jnp.where(sub == 0, rw[d], w_roll)
            rq[d] = q_roll
            rw[d] = w_roll
            net_sum = net_sum + (w - low_w)
            out = out + (jnp.maximum(q, 0.0) - jnp.minimum(low_q, 0.0))
            q, w = flows(cur, [pltpu.roll(x, 127, 1) for x in cur], 0.0)
            side_q = pltpu.roll(edge_q, 127 - 2 * d, 1)
            side_w = pltpu.roll(edge_w, 127 - 2 * d, 1)
            low_q = jnp.where(lane == 0, side_q, pltpu.roll(q, 1, 1))
            low_w = jnp.where(lane == 0, side_w, pltpu.roll(w, 1, 1))
            q = jnp.where(lane == 127, side_q, q)
            w = jnp.where(lane == 127, side_w, w)
            net_sum = 2.0 * (net_sum + (w - low_w))
            net[d, at, :] = net_sum
            told = jnp.where(lane == d, pltpu.roll(net_sum, d + 1, 1), told)
            out = out + (jnp.maximum(q, 0.0) - jnp.minimum(low_q, 0.0))
            top = jnp.maximum(top, out)
            cur = nxt
        ahead[at, :] = told
        return top

    top = lax.fori_loop(0, tiles, rows, jnp.zeros((8, 128), F32))

    message[...] = jnp.where(
        lax.broadcasted_iota(jnp.int32, message.shape, 1) == 0,
        2.0 * jnp.max(top),
        rest[0:1, :],
    )


def update_kernel(
    gathered, table, sat, net, source, perm, wgain, ogain, got_a, got_b, beside,
    new, chunks, cell_sum, row_sum, col_sum,
):
    place = here()
    lane = lane_iota()
    depth, rows_all, _ = sat.shape
    tiles = rows_all // 8
    stride = (depth + 1) * 8
    spot = lax.broadcasted_iota(jnp.int32, gathered.shape, 1)
    top = jnp.max(jnp.where(spot == 0, gathered[...], 0.0), keepdims=True)
    step_size = jnp.broadcast_to(courant / (top + tiny), (8, 128))
    even_col = place[0] % 2 == 0
    tables = [lane_table(table, n) for n in range(3)]

    def coefficient(k, wg, og, s):
        return k * (wg * s * s + og * (1.0 - s) * (1.0 - s))

    def rows(step, carry):
        at = pl.ds(pl.multiple_of(step * 8, 8), 8)
        begin = step * stride
        add = step_size * source[at, :]
        total = jnp.zeros((8, 128), F32)
        first = jnp.zeros((8, 128), F32)
        for d in range(depth):
            s = sat[d, at, :] - step_size * net[d, at, :] + add
            new[d, at, :] = s
            c = coefficient(perm[d, at, :], wgain[d, at, :], ogain[d, at, :], s)
            chunks[pl.ds(pl.multiple_of(begin + d * 8, 8), 8), :] = c
            total = total + c
            first = jnp.where(lane == d, pltpu.roll(c, d, 1) if d else c, first)
        cell_sum[at, :] = total
        tile = jnp.where(even_col, got_b[at, :], got_a[at, :])
        flow = beside[at, :]
        kind = jnp.where(lane < depth, tile, 0.0)
        index = jnp.maximum(kind.astype(jnp.int32) - 1, 0)
        k, wg, og = [lane_take(each, index) for each in tables]
        s = pltpu.roll(tile, 128 - depth, 1) - step_size * flow
        s = s + step_size * pltpu.roll(flow, 128 - depth, 1)
        c = coefficient(jnp.where(kind > 0.5, k, 0.0), wg, og, s)
        col_sum[at, :] = jnp.where(lane < depth, harmonic(c, first), 0.0)
        return carry

    def some_rows(step, carry):
        for n in range(8):
            carry = rows(8 * step + n, carry)
        return carry

    lax.fori_loop(0, tiles // 8, some_rows, 0)
    row_sum[0:8, :] = jnp.zeros((8, 128), F32)
    for p in range(1, tiles):
        total = jnp.zeros((8, 128), F32)
        for half in range(depth // 8):
            low = chunks[pl.ds((p - 1) * stride + half * 64 + 7, 8, stride=8), :]
            high = chunks[pl.ds(p * stride + half * 64, 8, stride=8), :]
            total = total + harmonic(low, high)
        row_sum[p * 8 : p * 8 + 8, :] = total
    brick = lax.broadcasted_iota(jnp.int32, (rows_all, 128), 0) // 8
    spot = lax.broadcasted_iota(jnp.int32, (rows_all, 128), 1)
    total = jnp.zeros((1, 128), F32)
    for n, part in enumerate((cell_sum, row_sum, col_sum)):
        each = jnp.sum(part[...], axis=1, keepdims=True)
        placed = jnp.where(spot == n * 16 + brick, each, 0.0)
        total = total + jnp.sum(placed, axis=0, keepdims=True)
    for p in range(tiles):
        chunks[p * stride + depth * 8 : (p + 1) * stride, :] = jnp.broadcast_to(total, (8, 128))


def relax_kernel(
    depth, got, residual, new, values, row_a, row_b, message, new_out, fd, fr, fc, gain, base, sem
):
    place = here()
    leave = pltpu.make_async_copy(new, new_out, sem.at[0])
    leave.start()
    lane = lane_iota()
    sub = sub_iota()
    layers = residual.shape[0] // 8
    parts = layers // depth
    zero = jnp.zeros((8, 128), F32)
    fd[0:8, :] = zero
    values[layers * 8 :, :] = jnp.zeros((64, 128), F32)
    fc[layers * 8 :, :] = jnp.zeros((64, 128), F32)
    even_row = place[2] % 2 == 0

    def half_face(low, high):
        return low * high / (low + high)

    def part(w, carry):
        below, total = carry
        begin = w * (depth + 1) * 8
        place_w = w * depth * 8
        after = jnp.minimum(w + 1, parts - 1) * (depth + 1) * 8
        c = got[pl.ds(pl.multiple_of(begin, 8), 8), :]
        for d in range(depth):
            here = pl.ds(pl.multiple_of(place_w + d * 8, 8), 8)
            if d + 1 < depth:
                c_next = got[pl.ds(pl.multiple_of(begin + d * 8 + 8, 8), 8), :]
                above = half_face(c, c_next)
            else:
                c_next = got[pl.ds(pl.multiple_of(after, 8), 8), :]
                above = jnp.where(w + 1 < parts, half_face(c, c_next), 0.0)
            row = jnp.where(sub == 0, 0.0, half_face(pltpu.roll(c, 1, 0), c))
            col = jnp.where(lane == 0, 0.0, half_face(pltpu.roll(c, 1, 1), c))
            diag = (
                (0.5 * compress) * c + below + above
                + row + pltpu.roll(row, 7, 0) + col + pltpu.roll(col, 127, 1)
            )
            scale = relax / diag
            fd[pl.ds(pl.multiple_of(place_w + d * 8 + 8, 8), 8), :] = above
            fr[here, :] = row
            fc[here, :] = col
            gain[here, :] = scale
            first = (0.5 * scale) * residual[here, :]
            base[here, :] = first
            values[here, :] = first
            c, below = c_next, above
        total = total + got[pl.ds(pl.multiple_of(begin + depth * 8, 8), 8), :]
        return below, total

    def build(step, carry):
        for n in range(4):
            carry = part(4 * step + n, carry)
        return carry

    _, total = lax.fori_loop(0, parts // 4, build, (zero, zero))

    block = 256

    def sweep(number, carry):
        def some(step, prev):
            begin = step * (block * 8)
            v = values[pl.ds(pl.multiple_of(begin, 8), 8), :]
            for n in range(block):
                here = pl.ds(pl.multiple_of(begin + n * 8, 8), 8)
                above = pl.ds(pl.multiple_of(begin + n * 8 + 8, 8), 8)
                v_next = values[above, :]
                row = fr[here, :]
                col = fc[here, :]
                total = fd[here, :] * prev + fd[above, :] * v_next
                total = total + (row * pltpu.roll(v, 1, 0) + pltpu.roll(row * v, 7, 0))
                total = total + (col * pltpu.roll(v, 1, 1) + pltpu.roll(col * v, 127, 1))
                values[here, :] = ((1.0 - relax) * v + base[here, :]) + gain[here, :] * total
                prev, v = v, v_next
            return prev

        lax.fori_loop(0, layers // block, some, zero)
        return carry

    lax.fori_loop(0, SWEEPS - 1, sweep, 0)

    for w in range(parts):
        for half in range(depth // 8):
            at = w * (depth + 1) * 8 + half * 64
            spot = w * depth + half * 8
            pairs = []
            for row in (0, 7):
                c = got[pl.ds(at + row, 8, stride=8), :]
                v = values[pl.ds(spot * 8 + row, 8, stride=8), :]
                pairs.append((c * v, c))
            for n in range(2):
                low, high = pairs[0][n], pairs[1][n]
                rows = slice(n * layers + spot, n * layers + spot + 8)
                row_a[rows, :] = jnp.where(even_row, high, low)
                row_b[rows, :] = jnp.where(even_row, low, high)

    quarters = layers // 64
    per_tile = 64 // depth
    peers = message.shape[0] // (quarters * 16 + 8)

    def pack(quarter, carry):
        packed = [zero, zero]
        for l in range(64):
            part = quarter * per_tile + l // depth
            c = got[pl.ds(pl.multiple_of(part * (depth + 1) * 8 + l % depth * 8, 8), 8), :]
            v = values[pl.ds(pl.multiple_of(quarter * 512 + l * 8, 8), 8), :]
            spot = (2 * l + 2) % 128
            mark = (lane == 2 * l + 1) | (lane == spot)
            for n, tile in enumerate((c * v, c)):
                turned = pltpu.roll(tile, spot, 1) if spot else tile
                packed[n] = jnp.where(mark, turned, packed[n])
        for peer in range(peers):
            for n in range(2):
                begin = peer * (quarters * 16 + 8) + (n * quarters + quarter) * 8
                message[pl.ds(pl.multiple_of(begin, 8), 8), :] = packed[n]
        return carry

    lax.fori_loop(0, quarters, pack, 0)
    for peer in range(peers):
        begin = peer * (quarters * 16 + 8) + quarters * 16
        message[begin : begin + 8, :] = total
    leave.wait()


def coarse_kernel(count, news, gathered, out):
    place = here()
    lane = lane_iota()
    sub = sub_iota()
    inside = lane < count
    width = gathered.shape[0] // count
    stride = news.shape[0] // width
    sums = jnp.zeros((8, 128), F32)
    for k in range(width):
        sums = jnp.where(sub == k, news[(k + 1) * stride - 8 : (k + 1) * stride, :], sums)
    cells = jnp.where(inside, sums, 0.0)
    low_row = jnp.where(inside, pltpu.roll(sums, 128 - 16, 1), 0.0)
    low_col = jnp.where(inside, pltpu.roll(sums, 128 - 32, 1), 0.0)
    low_row = jnp.where(lane == 0, 0.0, low_row)
    low_col = jnp.where(sub == 0, 0.0, low_col)
    high_row = pltpu.roll(low_row, 127, 1)
    high_col = pltpu.roll(low_col, 7, 0)
    diagonal = jnp.where(inside, compress * cells + low_row + high_row + low_col + high_col, 1.0)
    rhs = jnp.zeros((8, 128), F32)
    for p in range(count):
        rhs = jnp.where(lane == p, spread(gathered[p * width : p * width + width, :], 1), rhs)

    def line(tile, k):
        return jnp.broadcast_to(tile[k : k + 1, :], (8, 128))

    zero = jnp.zeros((8, 128), F32)
    main, lower, upper, right = [], [], [], []
    for k in range(width):
        row = jnp.where(sub == k, line(diagonal, k), zero)
        if k > 0:
            row = jnp.where(sub == k - 1, -line(low_col, k), row)
        if k + 1 < width:
            row = jnp.where(sub == k + 1, -line(low_col, k + 1), row)
        main.append(row)
        lower.append(jnp.where(sub == k, -line(low_row, k), zero))
        upper.append(jnp.where(sub == k, -line(high_row, k), zero))
        right.append(line(rhs, k))

    def eliminate(main, others):
        main = list(main)
        others = [list(rows) for rows in others]
        for k in range(width):
            inverse = 1.0 / line(main[k], k)
            main[k] = main[k] * inverse
            for rows in others:
                rows[k] = rows[k] * inverse
            for j in range(width):
                if j != k:
                    factor = line(main[j], k)
                    main[j] = main[j] - factor * main[k]
                    for rows in others:
                        rows[j] = rows[j] - factor * rows[k]
        return others

    stride = 1
    while stride < count:
        solved = eliminate(main, [lower, upper, right])
        back = [[pltpu.roll(x, stride, 1) for x in rows] for rows in solved]
        ahead = [[pltpu.roll(x, 128 - stride, 1) for x in rows] for rows in solved]
        new_lower, new_upper, new_main, new_right = [], [], [], []
        for k in range(width):
            lo, up, mid, rt = zero, zero, main[k], right[k]
            for j in [k] if stride == 1 else range(width):
                a = line(lower[k], j)
                b = line(upper[k], j)
                if 2 * stride < count:
                    lo = lo - a * back[0][j]
                    up = up - b * ahead[1][j]
                mid = mid - a * back[1][j] - b * ahead[0][j]
                rt = rt - a * back[2][j] - b * ahead[2][j]
            new_lower.append(lo)
            new_upper.append(up)
            new_main.append(mid)
            new_right.append(rt)
        lower, upper, main, right = new_lower, new_upper, new_main, new_right
        stride *= 2
    (right,) = eliminate(main, [right])
    mine = zero
    for k in range(width):
        mine = jnp.where(place[0] == k, right[k], mine)
    out[...] = lane_pick(mine, place[2])


def final_kernel(depth, got, values, row_a, row_b, news, coarse, result, packs, out, sem):
    place = here()
    lane = lane_iota()
    sub = sub_iota()
    layers = out.shape[0] // 8
    quarters = layers // 64
    per_tile = 64 // depth
    add = coarse[...]
    even_row = place[2] % 2 == 0
    stride = quarters * 16 + 8
    left = pl.multiple_of(jnp.maximum(place[0] - 1, 0) * stride, 8)
    right = pl.multiple_of(jnp.minimum(place[0] + 1, place[1] - 1) * stride, 8)
    odd = (lane & 1) == 1
    has_left = odd & (place[0] > 0)
    has_right = jnp.logical_not(odd) & (place[0] + 1 < place[1])
    for n in range(quarters * 2):
        low = news[pl.ds(left + n * 8, 8), :]
        high = pltpu.roll(news[pl.ds(right + n * 8, 8), :], 126, 1)
        packs[n * 8 : n * 8 + 8, :] = jnp.where(has_left, low, jnp.where(has_right, high, 0.0))
    ends = (lane == 0) | (lane == 127)

    def some(quarter, carry):
        sides = [
            packs[pl.ds(pl.multiple_of((n * quarters + quarter) * 8, 8), 8), :] for n in range(2)
        ]
        for l in range(64):
            g = quarter * 64 + l
            part = quarter * per_tile + l // depth
            here = pl.ds(pl.multiple_of(g * 8, 8), 8)
            c = got[pl.ds(pl.multiple_of(part * (depth + 1) * 8 + l % depth * 8, 8), 8), :]
            v = values[here, :]
            pair = []
            for n, tile in enumerate((c * v, c)):
                at = pl.ds(n * layers + g, 1)
                low = jnp.where(even_row, row_b[at, :], row_a[at, :])
                high = jnp.where(even_row, row_a[at, :], row_b[at, :])
                tile = tile + jnp.where(sub == 0, low, jnp.where(sub == 7, high, 0.0))
                tile = tile + jnp.where(ends, pltpu.roll(sides[n], 127 - 2 * l, 1), 0.0)
                pair.append(tile)
            out[here, :] = pair[0] / pair[1] + add
        leave(quarter).start()
        return carry

    def leave(quarter):
        part = pl.ds(pl.multiple_of(quarter * 512, 512), 512)
        return pltpu.make_async_copy(out.at[part, :], result.at[part, :], sem.at[quarter])

    def several(step, carry):
        for n in range(4):
            carry = some(4 * step + n, carry)
        return carry

    lax.fori_loop(0, quarters // 4, several, 0)
    for quarter in range(quarters):
        leave(quarter).wait()


def partners(array, axis, odd):
    count = lax.axis_size(axis)
    pairs = [(i, i + 1) for i in range(odd, count - 1, 2)]
    return lax.ppermute(array, axis, pairs + [(j, i) for i, j in pairs])


def forward(array, axis):
    count = lax.axis_size(axis)
    return lax.ppermute(array, axis, [(i, i + 1) for i in range(count - 1)])


def shards(saturation, pressure, rock_class, rock_table, well_columns, well_rates, residual):
    depth, rows_all, cols = saturation.shape
    layers, brick_rows, _ = residual.shape
    wide, narrow = lax.axis_size("wide"), lax.axis_size("narrow")
    block = (depth, rows_all, cols)
    plane = (rows_all, cols)
    vmem = pl.BlockSpec(memory_space=pltpu.VMEM)
    far = pl.BlockSpec(memory_space=pltpu.HBM)

    sat, press, kinds, face_a, face_b, pack_a, pack_b = call(
        faces_kernel,
        [block] * 3 + [(3,) + plane] * 2 + [plane] * 2,
        scratch=[pltpu.VMEM(block, jnp.int32), pltpu.SemaphoreType.DMA((24,))],
        in_specs=[far] * 3,
    )(
        *(
            pltpu.with_memory_space_constraint(array, pltpu.HBM)
            for array in (saturation, pressure, rock_class)
        ),
    )
    perm, wgain, ogain, frac, own_a, own_b, source, rest = call(
        functools.partial(lookup_kernel, narrow),
        [block] * 4 + [(3,) + plane] * 2 + [plane, (8, 128)],
        in_specs=[vmem] * 8,
    )(
        rock_table, kinds, sat, pack_a, pack_b,
        well_columns.reshape(1, -1), well_rates.reshape(1, -1), residual,
    )
    got_face_a = partners(face_a, "wide", 0)
    got_face_b = partners(face_b, "wide", 1)
    got_pack_b = partners(pack_b, "narrow", 1)
    got_pack_a = partners(pack_a, "narrow", 0)
    net, ahead, message = call(
        flow_kernel,
        [block, plane, (wide * narrow, 128)],
        scratch=[pltpu.VMEM(plane, F32)] * 2 + [pltpu.VMEM((depth, 8, cols), F32)] * 2,
        in_specs=[vmem] * 12,
    )(
        rock_table, press, perm, frac, got_face_a, got_face_b, own_a, own_b,
        got_pack_a, got_pack_b, source, rest,
    )
    beside = forward(ahead, "narrow")
    gathered = lax.all_to_all(message, ("wide", "narrow"), 0, 0, tiled=True)
    chunk_rows = wide * (depth + 1) * 8
    new, chunks = call(
        update_kernel,
        [block, (chunk_rows, 128)],
        scratch=[pltpu.VMEM(plane, F32)] * 3,
        in_specs=[vmem] * 11,
    )(
        gathered, rock_table, sat, net, source, perm, wgain, ogain, got_pack_a, got_pack_b,
        beside,
    )
    got = lax.all_to_all(chunks, "wide", 0, 0, tiled=True)
    message_rows = narrow * (layers // 4 + 8)
    values, row_a, row_b, message, sat_new = call(
        functools.partial(relax_kernel, depth),
        [(layers * 8 + 64, 128)] + [(2 * layers, 128)] * 2 + [(message_rows, 128), block],
        scratch=[pltpu.VMEM((layers * 8 + 64, 128), F32)] * 5 + [pltpu.SemaphoreType.DMA((1,))],
        in_specs=[vmem] * 3,
        out_specs=[vmem] * 4 + [far],
    )(got, residual.reshape(layers * 8, 128), new)
    got_row_a = partners(row_a, "wide", 0)
    got_row_b = partners(row_b, "wide", 1)
    news = lax.all_to_all(message, "narrow", 0, 0, tiled=True)
    (coarse,) = call(
        functools.partial(coarse_kernel, wide), [(8, 128)], in_specs=[vmem, vmem]
    )(news, gathered)
    (precond,) = call(
        functools.partial(final_kernel, depth),
        [(layers * 8, 128)],
        scratch=[
            pltpu.VMEM((layers // 4, 128), F32),
            pltpu.VMEM((layers * 8, 128), F32),
            pltpu.SemaphoreType.DMA((layers // 64,)),
        ],
        in_specs=[vmem] * 6,
        out_specs=[far],
    )(got, values, got_row_a, got_row_b, news, coarse)
    return (sat_new, precond.reshape(layers, brick_rows, cols))


def solution(mesh):
    placed = (
        P("wide", None, "narrow"),
        P("wide", None, "narrow"),
        P("wide", None, "narrow"),
        P(),
        P(),
        P(),
        P(None, "wide", "narrow"),
    )
    return jax.shard_map(
        shards,
        mesh=mesh,
        in_specs=placed,
        out_specs=(P("wide", None, "narrow"), P(None, "wide", "narrow")),
        check_vma=False,
    )
```
